32 devices in a mesh: sector: 8 (over z, y), mp: 4 (over x, core).
Axes of the slice: x: 2, y: 2, z: 4, core: 2. Of those that a mesh axis runs over, the one named last changes fastest.
Arguments:
- input_field: bfloat16 [2, 48, 64, 128], P(None, None, None, 'sector'), may hold values from -6 to 6
- present_mask: int32 [2, 48], replicated, may hold values from 0 to 1, as said below
- lead_index: int32 [2], replicated, may hold values from 0 to 7
- patch_weight: bfloat16 [48, 16, 1024], replicated, may hold values from -1.5 to 1.5
- patch_bias: bfloat16 [48, 1024], replicated, may hold values from -3 to 3
- agg_query: bfloat16 [16, 1024], replicated, may hold values from -0.1875 to 0.1875
- agg_value: bfloat16 [1024, 1024], replicated, may hold values from -0.1875 to 0.1875
- agg_out: bfloat16 [1024, 1024], replicated, may hold values from -0.1875 to 0.1875
- lead_table: bfloat16 [8, 1024], replicated, may hold values from -3 to 3
- norm1_gain: float32 [1024], replicated, may hold values from 0.1 to 1.9
- qkv_weight: bfloat16 [1024, 3, 1024], P(None, None, 'mp'), may hold values from -0.1875 to 0.1875
- attn_out_weight: bfloat16 [1024, 1024], P('mp'), may hold values from -3 to 3
- norm2_gain: float32 [1024], replicated, may hold values from 0.1 to 1.9
- up_weight: bfloat16 [1024, 4096], P(None, 'mp'), may hold values from -0.1875 to 0.1875
- down_weight: bfloat16 [4096, 1024], P('mp'), may hold values from -0.375 to 0.375
- head_weight: bfloat16 [1024, 768], replicated, may hold values from -0.1875 to 0.1875
- pred_cotangent: bfloat16 [2, 48, 64, 128], P(None, None, None, 'sector'), may hold values from -6 to 6
Outputs:
- prediction: float32 [2, 48, 64, 128], P(None, None, None, 'sector')
- field_grad: float32 [2, 48, 64, 128], P(None, 'mp', None, 'sector')
- grad_patch_weight: float32 [48, 16, 1024], P('mp', None, 'sector')
- grad_patch_bias: float32 [48, 1024], P('mp', 'sector')
- grad_agg_query: float32 [16, 1024], P('mp', 'sector')
- grad_agg_value: float32 [1024, 1024], P('mp', 'sector')
- grad_agg_out: float32 [1024, 1024], P('mp', 'sector')
- grad_lead_table: float32 [8, 1024], P(None, 'sector')
- grad_norm1: float32 [1024], P('sector')
- grad_qkv: float32 [1024, 3, 1024], P('sector', None, 'mp')
- grad_attn_out: float32 [1024, 1024], P('mp', 'sector')
- grad_norm2: float32 [1024], P('sector')
- grad_up: float32 [1024, 4096], P('sector', 'mp')
- grad_down: float32 [4096, 1024], P('mp', 'sector')
- grad_head: float32 [1024, 768], P('sector', 'mp')
The draws below stay inside these ranges and needn't reach their ends.
Inputs may be any that keep to these rules, and one draw needn't show every extreme that they name: `present_mask`: each sample has at least 8 present slots; one sample has all 48, another has exactly 8.
All inputs are finite; a program needn't handle non-finite values.
Results may differ from the reference program's by a relative error of at most 0.04.
Values may be sent and summed in bfloat16 or wider, within the bound.
No kernel may reach another device: no remote copies, remote signals or barrier semaphores. Data moves between devices by JAX's collectives and lax.ppermute only.
A program may use at most 576 MiB of HBM per device.

```python
import jax
import jax.numpy as jnp
from jax import lax

D = 1024
HEADS = 16
FF = 4096
VARS = 48
HEAD_DIM = 64
FEWEST = 8
LAT = 32
LEADS = 8
LON = 64
SAMPLES = 2


def draw_present_mask(key, part):
    count_key, full_key, order_key = jax.random.split(jax.random.fold_in(key, 11), 3)
    fewest = FEWEST
    counts = jax.random.randint(count_key, (SAMPLES,), fewest, VARS + 1)
    full_at = jax.random.randint(full_key, (), 0, SAMPLES)
    places = jnp.arange(SAMPLES)
    counts = jnp.where(places == full_at, VARS, counts)
    counts = jnp.where(places == (full_at + 1) % SAMPLES, fewest, counts)
    order_keys = jax.random.split(order_key, SAMPLES)
    orders = jax.vmap(lambda one_key: jax.random.permutation(one_key, VARS))(order_keys)
    return (orders < counts[:, None]).astype(jnp.int32)


def levels(key, shape, cuts, least, largest):
    gain = 1.0
    for axis_at, parts in cuts:
        heights = jax.random.uniform(jax.random.fold_in(jax.random.fold_in(key, 6), axis_at), (parts,), jnp.float32, least / len(cuts), largest / len(cuts))
        gain = gain * jnp.repeat(jnp.exp(heights), shape[axis_at] // parts).reshape((-1,) + (1,) * (len(shape) - 1 - axis_at))
    return gain


def bell_draw(key, extent, width, most, shards=(), kind=jnp.bfloat16):
    drawn = width * jax.random.normal(key, extent, jnp.float32)
    if shards:
        drawn = drawn * levels(key, extent, shards, -0.22, 0.18)
    return jnp.clip(drawn, -most, most).astype(kind)


def setup_inputs(seed: int = 0) -> dict:
    key_list = jax.random.split(jax.random.key(seed), 18)
    input_field = bell_draw(key_list[0], (SAMPLES, VARS, 2 * LAT, 2 * LON), 1.0, 6.0, ((3, 8),))
    present_mask = draw_present_mask(jax.random.fold_in(key_list[17], 71), 0)
    lead_index = jax.random.randint(key_list[2], (SAMPLES,), 0, LEADS).astype(jnp.int32)
    patch_weight = bell_draw(key_list[3], (VARS, 16, D), 16 ** -0.5, 1.5)
    patch_bias = bell_draw(key_list[4], (VARS, D), 0.5, 3.0)
    agg_query = bell_draw(key_list[5], (HEADS, D), D ** -0.5, 0.1875)
    agg_value = bell_draw(key_list[6], (D, D), D ** -0.5, 0.1875)
    agg_out = bell_draw(key_list[7], (D, D), D ** -0.5, 0.1875)
    lead_table = bell_draw(key_list[8], (LEADS, D), 0.5, 3.0)
    norm1_gain = jnp.clip(1.0 + 0.18 * jax.random.normal(key_list[9], (D,), jnp.float32), 0.1, 1.9)
    qkv_weight = bell_draw(key_list[10], (D, 3, D), D ** -0.5, 0.1875, ((2, 4),))
    attn_out_weight = bell_draw(key_list[11], (D, D), (max(4, D // 256)) ** -0.5, 3.0, ((0, 4),))
    norm2_gain = jnp.clip(1.0 + 0.18 * jax.random.normal(key_list[12], (D,), jnp.float32), 0.1, 1.9)
    up_weight = bell_draw(key_list[13], (D, FF), D ** -0.5, 0.1875, ((1, 4),))
    down_weight = bell_draw(key_list[14], (FF, D), (max(4, FF // 16)) ** -0.5, 0.375, ((0, 4),))
    head_weight = bell_draw(key_list[15], (D, VARS * 16), D ** -0.5, 0.1875)
    pred_cotangent = bell_draw(key_list[16], (SAMPLES, VARS, 2 * LAT, 2 * LON), 1.0, 6.0, ((3, 8),))
    return {"input_field": input_field, "present_mask": present_mask, "lead_index": lead_index, "patch_weight": patch_weight, "patch_bias": patch_bias, "agg_query": agg_query, "agg_value": agg_value, "agg_out": agg_out, "lead_table": lead_table, "norm1_gain": norm1_gain, "qkv_weight": qkv_weight, "attn_out_weight": attn_out_weight, "norm2_gain": norm2_gain, "up_weight": up_weight, "down_weight": down_weight, "head_weight": head_weight, "pred_cotangent": pred_cotangent}


@jax.custom_vjp
def low(v):
    return lax.optimization_barrier(v.astype(jnp.bfloat16)).astype(jnp.float32)

@jax.custom_vjp
def low_back(v):
    return v

def low_keep(v):
    return (low(v), None)

def low_pass(kept, grad):
    return (grad,)

def back_keep(v):
    return (v, None)

def back_low(kept, grad):
    return (low(grad),)
low.defvjp(low_keep, low_pass)
low_back.defvjp(back_keep, back_low)
highest = lax.Precision.HIGHEST
norm_eps = 1e-05

def make_windows(padded, row_count, col_count):
    sample_count, channels = (padded.shape[0], padded.shape[1])
    blocks = padded.reshape(sample_count, channels, row_count + 1, 2, col_count + 1, 2)
    stacked = jnp.stack([jnp.stack([blocks[:, :, upper_off:upper_off + row_count, :, left_off:left_off + col_count, :] for left_off in range(2)], 0) for upper_off in range(2)], 0)
    stacked = jnp.transpose(stacked, (2, 4, 6, 3, 0, 5, 1, 7))
    return stacked.reshape(sample_count, row_count * col_count, channels, 16)

def fold_canvas(pieces, row_count, col_count):
    sample_count, channels = (pieces.shape[0], pieces.shape[2])
    shaped = pieces.reshape(sample_count, row_count, col_count, channels, 2, 2, 2, 2)
    summed = jnp.zeros((sample_count, channels, row_count + 1, 2, col_count + 1, 2), pieces.dtype)
    for upper_off in range(2):
        for left_off in range(2):
            placed = jnp.transpose(shaped[:, :, :, :, upper_off, :, left_off, :], (0, 3, 1, 4, 2, 5))
            placed = jnp.pad(placed, ((0, 0), (0, 0), (upper_off, 1 - upper_off), (0, 0), (left_off, 1 - left_off), (0, 0)))
            summed = summed + placed
    return summed.reshape(sample_count, channels, 2 * row_count + 2, 2 * col_count + 2)[:, :, 1:-1, :]

def wrap_fold(canvas):
    inner_cols = canvas[..., 1:-1]
    inner_cols = inner_cols.at[..., 0].add(canvas[..., -1])
    return inner_cols.at[..., -1].add(canvas[..., 0])

def layer_norm(values, gain_vec):
    row_mean = lax.optimization_barrier(jnp.mean(values, axis=-1, keepdims=True))
    centered = values - row_mean
    variance = lax.optimization_barrier(jnp.mean(centered * centered, axis=-1, keepdims=True))
    return centered * lax.rsqrt(variance + norm_eps) * gain_vec

def reference(input_field, present_mask, lead_index, patch_weight, patch_bias, agg_query, agg_value, agg_out, lead_table, norm1_gain, qkv_weight, attn_out_weight, norm2_gain, up_weight, down_weight, head_weight, pred_cotangent):
    floats = [item.astype(jnp.float32) for item in (input_field, patch_weight, patch_bias, agg_query, agg_value, agg_out, lead_table, norm1_gain, qkv_weight, attn_out_weight, norm2_gain, up_weight, down_weight, head_weight)]
    score_scale = HEAD_DIM ** (-0.5)
    seq_len = LAT * LON

    def forward(field_f, patch_w, patch_b, query_w, value_w, aggout_w, lead_w, gain_one, qkv_w, attout_w, gain_two, up_w, down_w, head_w):
        weight_ext = jnp.concatenate([patch_w, patch_b[:, None, :]], axis=1)
        key_map = jnp.einsum('vkd,hd->vkh', weight_ext, query_w, precision=highest)
        value_map = low(jnp.einsum('vkd,de->vke', weight_ext, value_w, precision=highest))
        value_heads = value_map.reshape(VARS * 17, HEADS, HEAD_DIM)

        def per_sample(inputs):
            field_one, mask_one, lead_one = inputs
            padded = jnp.pad(field_one[None], ((0, 0), (0, 0), (1, 1), (0, 0)))
            padded = jnp.concatenate([padded[..., -1:], padded, padded[..., :1]], axis=3)
            window_vals = make_windows(padded, LAT, LON)[0]
            win_ext = jnp.concatenate([window_vals, jnp.ones((seq_len, VARS, 1), jnp.float32)], axis=2)
            agg_scores = jnp.einsum('lvk,vkh->lhv', win_ext, key_map, precision=highest)
            agg_scores = jnp.where((mask_one > 0)[None, None, :], agg_scores, -1e+30)
            agg_probs = jax.nn.softmax(agg_scores, axis=-1)
            weighted = low((agg_probs[..., None] * win_ext[:, None, :, :]).reshape(seq_len, HEADS, VARS * 17))
            pooled = jnp.einsum('lhm,mhj->lhj', weighted, value_heads, precision=highest).reshape(seq_len, D)
            pooled = low_back(low(pooled))
            lead_hot = (lead_one == jnp.arange(LEADS)).astype(jnp.float32)
            lead_row = jnp.dot(lead_hot, lead_w, precision=highest)
            start_x = low_back(jnp.dot(pooled, aggout_w, precision=highest)) + lead_row[None, :]
            normed1 = low(layer_norm(start_x, gain_one))
            qkv = jnp.einsum('ld,dme->lme', normed1, qkv_w, precision=highest)
            query = low_back(low(qkv[:, 0])).reshape(seq_len, HEADS, HEAD_DIM)
            keys = low_back(low(qkv[:, 1])).reshape(seq_len, HEADS, HEAD_DIM)
            values = low_back(low(qkv[:, 2])).reshape(seq_len, HEADS, HEAD_DIM)
            att_scores = low_back(jnp.einsum('qhd,khd->hqk', query, keys, precision=highest) * score_scale)
            att_probs = low(jax.nn.softmax(att_scores, axis=-1))
            att_out = jnp.einsum('hqk,khd->qhd', att_probs, values, precision=highest).reshape(seq_len, D)
            att_out = low_back(low(att_out))
            mid_x = start_x + low_back(jnp.dot(att_out, attout_w, precision=highest))
            normed2 = low(layer_norm(mid_x, gain_two))
            hidden = low_back(jnp.dot(normed2, up_w, precision=highest))
            active = low(jax.nn.gelu(hidden, approximate=False))
            end_x = mid_x + low_back(jnp.dot(active, down_w, precision=highest))
            head_out = jnp.dot(low(end_x), head_w, precision=highest).reshape(1, seq_len, VARS, 16)
            return wrap_fold(fold_canvas(head_out, LAT, LON))[0]
        return lax.map(jax.checkpoint(per_sample), (field_f, present_mask, lead_index))
    prediction, pullback = jax.vjp(forward, *floats)
    gradients = pullback(pred_cotangent.astype(jnp.float32))
    field_grad, grad_pw, grad_pb, grad_aq, grad_av, grad_ao, grad_lt, grad_n1, grad_qkv, grad_att, grad_n2, grad_upw, grad_downw, grad_headw = gradients
    return (prediction, field_grad, grad_pw, grad_pb, grad_aq, grad_av, grad_ao, grad_lt, grad_n1, grad_qkv, grad_att, grad_n2, grad_upw, grad_downw, grad_headw)
```

```python
import functools

import jax
import jax.numpy as jnp
from jax import lax
from jax.experimental import pallas as pl
from jax.experimental.pallas import tpu as pltpu
from jax.sharding import PartitionSpec as P

bf16 = jnp.bfloat16
f32 = jnp.float32
highest = lax.Precision.HIGHEST
norm_eps = 1e-05
sqrt_half = 0.7071067811865476
inv_root_two_pi = 0.3989422804014327
vmem_most = 56 * 1024 * 1024


def mm(left, right, left_dim, right_dim):
    return lax.dot_general(
        left, right, (((left_dim,), (right_dim,)), ((), ())), preferred_element_type=f32
    )


def call(body, out_shape, cost, grid=None, in_specs=None, out_specs=None, scratch=()):
    more = {}
    if grid is not None:
        more = dict(grid=grid, in_specs=in_specs, out_specs=out_specs)
    return pl.pallas_call(
        body,
        out_shape=out_shape,
        scratch_shapes=list(scratch),
        compiler_params=pltpu.CompilerParams(vmem_limit_bytes=vmem_most),
        cost_estimate=pl.CostEstimate(
            flops=int(cost[0]), bytes_accessed=int(cost[1]), transcendentals=int(cost[2])
        ),
        **more,
    )


def row_pick(rows, patch_rows, patch_cols):
    span = patch_rows * patch_cols
    lane = lax.broadcasted_iota(jnp.int32, (rows, 4 * span), 1)
    row = lax.broadcasted_iota(jnp.int32, (rows, 4 * span), 0)
    r = lane // span
    rest = lane - r * span
    j = rest // patch_rows
    i = rest - j * patch_rows
    return (row == 2 * i + r - 1), j


def windows_body(x_ref, o_ref):
    samples, wide, chans, rows = x_ref.shape
    cols, patch_rows = (wide - 2) // 2, rows // 2
    span = cols * patch_rows
    hit, lane_col = row_pick(rows, patch_rows, cols)
    total = None
    for j in range(cols):
        left = jnp.concatenate(
            [x_ref[s, 2 * j + c] for s in range(samples) for c in range(4)], axis=0
        )
        pick = jnp.where(hit & (lane_col == j), 1.0, 0.0).astype(bf16)
        part = jnp.dot(left, pick, preferred_element_type=f32)
        total = part if total is None else total + part
    for s in range(samples):
        for c in range(4):
            at = (s * 4 + c) * chans
            for r in range(4):
                o_ref[r * 4 + c, :, s * span : (s + 1) * span] = total[
                    at : at + chans, r * span : (r + 1) * span
                ].astype(o_ref.dtype)


def windows(x):
    samples, wide, chans, rows = x.shape
    tokens = samples * (wide - 2) * rows // 4
    return call(
        windows_body,
        jax.ShapeDtypeStruct((16, chans, tokens), bf16),
        (2 * 16 * chans * tokens * 512, 4 * 16 * chans * tokens, 0),
    )(x)


def fold_body(g_ref, o_ref, *, samples, cols, rows):
    chans = g_ref.shape[1]
    patch_rows = rows // 2
    span = cols * patch_rows
    hit, lane_col = row_pick(rows, patch_rows, cols)
    left = jnp.concatenate(
        [
            jnp.concatenate(
                [g_ref[r * 4 + c, :, s * span : (s + 1) * span] for r in range(4)], axis=1
            )
            for s in range(samples)
            for c in range(4)
        ],
        axis=0,
    ).astype(bf16)
    held = [[None] * (2 * cols + 2) for _ in range(samples)]
    for j in range(cols):
        pick = jnp.where(hit & (lane_col == j), 1.0, 0.0).astype(bf16)
        part = mm(left, pick, 1, 1)
        for s in range(samples):
            for c in range(4):
                at = (s * 4 + c) * chans
                piece = part[at : at + chans]
                before = held[s][2 * j + c]
                held[s][2 * j + c] = piece if before is None else before + piece
        for s in range(samples):
            for col in (2 * j, 2 * j + 1):
                o_ref[s, col] = held[s][col]
    for s in range(samples):
        for col in (2 * cols, 2 * cols + 1):
            o_ref[s, col] = held[s][col]


def fold(g, samples, cols, rows):
    chans, tokens = g.shape[1:]
    return call(
        functools.partial(fold_body, samples=samples, cols=cols, rows=rows),
        jax.ShapeDtypeStruct((samples, 2 * cols + 2, chans, rows), f32),
        (2 * 16 * chans * tokens * 512, 4 * 16 * chans * tokens, 0),
    )(g)


def agg_forward_body(win_ref, bd_ref, vht_ref, mask_ref, probs_ref, pooled_ref):
    window_size, chans, lanes = win_ref.shape
    heads = probs_ref.shape[0]
    head_dim = pooled_ref.shape[0] // heads
    ones = jnp.ones((1, chans, lanes), bf16)
    win = jnp.concatenate([win_ref[...], ones], axis=0)
    flat = win.reshape((window_size + 1) * chans, lanes)
    scores = (
        jnp.dot(bd_ref[0], flat, preferred_element_type=f32)
        + jnp.dot(bd_ref[1], flat, preferred_element_type=f32)
        + jnp.dot(bd_ref[2], flat, preferred_element_type=f32)
    )
    present = mask_ref[...] > 0
    wide = win.astype(f32)
    for h in range(heads):
        score = jnp.where(present, scores[h * chans : (h + 1) * chans], -1e30)
        raised = jnp.exp(score - jnp.max(score, axis=0, keepdims=True))
        probs = raised / jnp.sum(raised, axis=0, keepdims=True)
        probs_ref[h] = probs
        weighted = (wide * probs[None]).astype(bf16).reshape(flat.shape)
        pooled_ref[h * head_dim : (h + 1) * head_dim, :] = jnp.dot(
            vht_ref[h * head_dim : (h + 1) * head_dim, :], weighted, preferred_element_type=f32
        ).astype(bf16)


def agg_forward(win, block_diag, value_t, mask, heads):
    window_size, chans, tokens = win.shape
    width, depth = value_t.shape
    lanes = 256 if tokens % 256 == 0 else tokens
    whole = lambda i: (0, 0)
    return call(
        agg_forward_body,
        (
            jax.ShapeDtypeStruct((heads, chans, tokens), f32),
            jax.ShapeDtypeStruct((width, tokens), bf16),
        ),
        (2 * tokens * depth * (width + 3 * heads * chans), 12 * 2**20, heads * chans * tokens),
        grid=(tokens // lanes,),
        in_specs=[
            pl.BlockSpec((window_size, chans, lanes), lambda i: (0, 0, i)),
            pl.BlockSpec(block_diag.shape, lambda i: (0, 0, 0)),
            pl.BlockSpec(value_t.shape, whole),
            pl.BlockSpec((chans, lanes), lambda i: (0, i)),
        ],
        out_specs=(
            pl.BlockSpec((heads, chans, lanes), lambda i: (0, 0, i)),
            pl.BlockSpec((width, lanes), lambda i: (0, i)),
        ),
    )(win, block_diag, value_t, mask)


def agg_backward_body(
    win_ref, probs_ref, gp_ref, vh_ref, bdt_ref, gwin_ref, gvmt_ref, gkm_ref, gs_ref, acc_ref
):
    window_size, chans, lanes = win_ref.shape
    heads = probs_ref.shape[0]
    head_dim = gp_ref.shape[0] // heads
    step = pl.program_id(0)
    ones = jnp.ones((1, chans, lanes), bf16)
    win = jnp.concatenate([win_ref[...], ones], axis=0)
    wide = win.astype(f32)
    depth = (window_size + 1) * chans
    acc_ref[...] = jnp.zeros_like(acc_ref)

    @pl.when(step == 0)
    def _():
        gvmt_ref[...] = jnp.zeros_like(gvmt_ref)
        gkm_ref[...] = jnp.zeros_like(gkm_ref)

    for h in range(heads):
        gp = gp_ref[h * head_dim : (h + 1) * head_dim, :]
        probs = probs_ref[h]
        gw = jnp.dot(vh_ref[h], gp, preferred_element_type=f32).reshape(wide.shape)
        grad_probs = jnp.sum(gw * wide, axis=0)
        delta = jnp.sum(probs * grad_probs, axis=0, keepdims=True)
        gs_ref[h * chans : (h + 1) * chans, :] = (probs * (grad_probs - delta)).astype(bf16)
        acc_ref[...] += gw[:window_size] * probs[None]
        weighted = (wide * probs[None]).astype(bf16).reshape(depth, lanes)
        gvmt_ref[h * head_dim : (h + 1) * head_dim, :] += mm(gp, weighted, 1, 1)
    gs = gs_ref[...]
    extra = jnp.dot(bdt_ref[...], gs, preferred_element_type=f32)
    gwin_ref[...] = (acc_ref[...] + extra.reshape(acc_ref.shape)).astype(bf16)
    gkm_ref[...] += mm(win.reshape(depth, lanes), gs, 1, 1)


def agg_backward(win, probs, grad_pooled_t, value_heads, block_diag_t):
    window_size, chans, tokens = win.shape
    heads, depth, head_dim = value_heads.shape
    lanes = 256 if tokens % 256 == 0 else tokens
    width = heads * head_dim
    whole = lambda i: (0, 0)
    return call(
        agg_backward_body,
        (
            jax.ShapeDtypeStruct(win.shape, bf16),
            jax.ShapeDtypeStruct((width, depth), f32),
            jax.ShapeDtypeStruct((depth, heads * chans), f32),
        ),
        (4 * tokens * depth * (width + heads * chans), 20 * 2**20, 0),
        grid=(tokens // lanes,),
        in_specs=[
            pl.BlockSpec((window_size, chans, lanes), lambda i: (0, 0, i)),
            pl.BlockSpec((heads, chans, lanes), lambda i: (0, 0, i)),
            pl.BlockSpec((width, lanes), lambda i: (0, i)),
            pl.BlockSpec(value_heads.shape, lambda i: (0, 0, 0)),
            pl.BlockSpec(block_diag_t.shape, whole),
        ],
        out_specs=(
            pl.BlockSpec((window_size, chans, lanes), lambda i: (0, 0, i)),
            pl.BlockSpec((width, depth), whole),
            pl.BlockSpec((depth, heads * chans), whole),
        ),
        scratch=(
            pltpu.VMEM((heads * chans, lanes), bf16),
            pltpu.VMEM((window_size, chans, lanes), f32),
        ),
    )(win, probs, grad_pooled_t, value_heads, block_diag_t)


def attend_body(x_ref, o_ref, lse_ref, key_ref, value_ref, *, scale):
    blocks, triple, span = x_ref.shape
    head_dim = triple // 3
    step = pl.program_id(0)

    @pl.when(step == 0)
    def _():
        for n in range(blocks):
            key_ref[n * span : (n + 1) * span, :] = x_ref[n, head_dim : 2 * head_dim, :].T
            value_ref[:, n * span : (n + 1) * span] = x_ref[n, 2 * head_dim :, :]

    query = x_ref[step, :head_dim, :] * jnp.asarray(scale, bf16)
    scores = jnp.dot(key_ref[...], query, preferred_element_type=f32)
    most = jnp.max(scores, axis=0, keepdims=True)
    raised = jnp.exp(scores - most)
    total = jnp.sum(raised, axis=0, keepdims=True)
    probs = (raised * (1.0 / total)).astype(bf16)
    o_ref[0] = jnp.dot(value_ref[...], probs, preferred_element_type=f32).astype(bf16)
    lse_ref[0] = most + jnp.log(total)


def attend(x, scale):
    blocks, triple, span = x.shape
    head_dim = triple // 3
    seq = blocks * span
    return call(
        functools.partial(attend_body, scale=scale),
        (
            jax.ShapeDtypeStruct((blocks, head_dim, span), bf16),
            jax.ShapeDtypeStruct((blocks, 1, span), f32),
        ),
        (4 * seq * seq * head_dim, 2 * x.size, seq * seq),
        grid=(blocks,),
        in_specs=[pl.BlockSpec(x.shape, lambda i: (0, 0, 0))],
        out_specs=(
            pl.BlockSpec((1, head_dim, span), lambda i: (i, 0, 0)),
            pl.BlockSpec((1, 1, span), lambda i: (i, 0, 0)),
        ),
        scratch=(pltpu.VMEM((seq, head_dim), bf16), pltpu.VMEM((head_dim, seq), bf16)),
    )(x)


def attend_back_body(
    x_ref, do_ref, lse_ref, o_ref, key_ref, keyt_ref, value_ref, dkey_ref, dvalue_ref, *, scale
):
    blocks, triple, span = x_ref.shape
    head_dim = triple // 3
    step = pl.program_id(0)

    @pl.when(step == 0)
    def _():
        for n in range(blocks):
            here = slice(n * span, (n + 1) * span)
            key_ref[here, :] = x_ref[n, head_dim : 2 * head_dim, :].T
            keyt_ref[:, here] = x_ref[n, head_dim : 2 * head_dim, :]
            value_ref[here, :] = x_ref[n, 2 * head_dim :, :].T
        dkey_ref[...] = jnp.zeros_like(dkey_ref)
        dvalue_ref[...] = jnp.zeros_like(dvalue_ref)

    query = x_ref[step, :head_dim, :] * jnp.asarray(scale, bf16)
    grad = do_ref[step]
    scores = jnp.dot(key_ref[...], query, preferred_element_type=f32)
    probs = jnp.exp(scores - lse_ref[step])
    grad_probs = jnp.dot(value_ref[...], grad, preferred_element_type=f32)
    delta = jnp.sum(probs * grad_probs, axis=0, keepdims=True)
    grad_scores = (probs * (grad_probs - delta)).astype(bf16)
    o_ref[step, :head_dim, :] = (
        jnp.dot(keyt_ref[...], grad_scores, preferred_element_type=f32) * scale
    ).astype(bf16)
    dkey_ref[...] += jnp.dot(grad_scores, query.T, preferred_element_type=f32)
    dvalue_ref[...] += jnp.dot(probs.astype(bf16), grad.T, preferred_element_type=f32)

    @pl.when(step == blocks - 1)
    def _():
        for n in range(blocks):
            here = slice(n * span, (n + 1) * span)
            o_ref[n, head_dim : 2 * head_dim, :] = dkey_ref[here, :].T.astype(bf16)
            o_ref[n, 2 * head_dim :, :] = dvalue_ref[here, :].T.astype(bf16)


def attend_back(x, grad, lse, scale):
    blocks, triple, span = x.shape
    head_dim = triple // 3
    seq = blocks * span
    three = lambda i: (0, 0, 0)
    return call(
        functools.partial(attend_back_body, scale=scale),
        jax.ShapeDtypeStruct(x.shape, bf16),
        (10 * seq * seq * head_dim, 4 * x.size, seq * seq),
        grid=(blocks,),
        in_specs=[
            pl.BlockSpec(x.shape, three),
            pl.BlockSpec(grad.shape, three),
            pl.BlockSpec(lse.shape, three),
        ],
        out_specs=pl.BlockSpec(x.shape, three),
        scratch=(
            pltpu.VMEM((seq, head_dim), bf16),
            pltpu.VMEM((head_dim, seq), bf16),
            pltpu.VMEM((seq, head_dim), bf16),
            pltpu.VMEM((seq, head_dim), f32),
            pltpu.VMEM((seq, head_dim), f32),
        ),
    )(x, grad, lse)


def attend_gathered(packed, scale):
    head_dim = packed.shape[2] // 3
    whole = lax.all_gather(packed[:, :, head_dim:, :], "sector", axis=0)
    keys, values = (whole[:, :, :, :head_dim], whole[:, :, :, head_dim:])
    scores = (
        jnp.einsum("hsdq,nhsdk->hsqnk", packed[:, :, :head_dim], keys, preferred_element_type=f32)
        * scale
    )
    most = jnp.max(scores, axis=(3, 4), keepdims=True)
    raised = jnp.exp(scores - most)
    total = jnp.sum(raised, axis=(3, 4), keepdims=True)
    probs = (raised / total).astype(bf16)
    out = jnp.einsum("hsqnk,nhsdk->hsdq", probs, values, preferred_element_type=f32)
    return out.astype(bf16), most + jnp.log(total)


def attend_back_gathered(packed, grad, lse, scale):
    head_dim = packed.shape[2] // 3
    query = packed[:, :, :head_dim]
    whole = lax.all_gather(packed[:, :, head_dim:, :], "sector", axis=0)
    keys, values = (whole[:, :, :, :head_dim], whole[:, :, :, head_dim:])
    scores = jnp.einsum("hsdq,nhsdk->hsqnk", query, keys, preferred_element_type=f32) * scale
    probs = jnp.exp(scores - lse)
    grad_probs = jnp.einsum("hsdq,nhsdk->hsqnk", grad, values, preferred_element_type=f32)
    delta = jnp.sum(probs * grad_probs, axis=(3, 4), keepdims=True)
    grad_scores = (probs * (grad_probs - delta)).astype(bf16)
    grad_query = jnp.einsum("hsqnk,nhsdk->hsdq", grad_scores, keys, preferred_element_type=f32)
    grad_keys = jnp.einsum("hsqnk,hsdq->nhsdk", grad_scores, query, preferred_element_type=f32)
    grad_values = jnp.einsum(
        "hsqnk,hsdq->nhsdk", probs.astype(bf16), grad, preferred_element_type=f32
    )
    both = lax.psum_scatter(
        jnp.concatenate([grad_keys * scale, grad_values], axis=3), "sector", scatter_dimension=0
    )
    return jnp.concatenate([grad_query * scale, both], axis=2).astype(bf16)


def swap(x, axis, bit):
    size = lax.axis_size(axis)
    return lax.ppermute(x, axis, [(i, i ^ bit) for i in range(size)])


def rounded(x):
    return lax.reduce_precision(x, 8, 7)


def sum_over_mp(x):
    if lax.axis_size("mp") != 4:
        return lax.psum(x.astype(bf16), "mp").astype(f32)
    half = x.shape[0] // 2
    low, high = (rounded(x[:half]), rounded(x[half:]))
    first = lax.axis_index("mp") % 2 == 0
    mine, other = (jnp.where(first, low, high), jnp.where(first, high, low))
    mine = rounded(mine + swap(other.astype(bf16), "mp", 1).astype(f32))
    mine = rounded(mine + swap(mine.astype(bf16), "mp", 2).astype(f32))
    other = swap(mine.astype(bf16), "mp", 1).astype(f32)
    return jnp.concatenate([jnp.where(first, mine, other), jnp.where(first, other, mine)], axis=0)


def ring_pair(leading, last):
    size = lax.axis_size("sector")
    up = [(i, (i + 1) % size) for i in range(size)]
    down = [(j, i) for i, j in up]
    return lax.ppermute(last, "sector", up), lax.ppermute(leading, "sector", down)


def scatter_sum(x):
    got = lax.all_to_all(x.astype(bf16), "sector", 0, 0, tiled=True)
    return jnp.sum(got.astype(f32), axis=0)


def norm_forward(values, gain_vec):
    row_mean = jnp.mean(values, axis=-1, keepdims=True)
    centered = values - row_mean
    inverse = lax.rsqrt(jnp.mean(centered * centered, axis=-1, keepdims=True) + norm_eps)
    normed = centered * inverse
    return (normed * gain_vec, normed, inverse)


def norm_backward(grad_out, gain_vec, normed, inverse):
    grad_normed = grad_out * gain_vec
    grad_gain = jnp.sum(grad_out * normed, axis=0)
    grad_in = inverse * (
        grad_normed
        - jnp.mean(grad_normed, axis=-1, keepdims=True)
        - normed * jnp.mean(grad_normed * normed, axis=-1, keepdims=True)
    )
    return (grad_in, grad_gain)


def gelu_slope(values):
    return (
        0.5 * (1.0 + lax.erf(values * sqrt_half))
        + values * jnp.exp(-0.5 * values * values) * inv_root_two_pi
    )


def mp_slice(values, axis_dim, mp_index, mp_count):
    piece_len = values.shape[axis_dim] // mp_count
    return lax.dynamic_slice_in_dim(values, mp_index * piece_len, piece_len, axis_dim)


def column_blocks(x, sectors):
    return jnp.transpose(x.reshape(x.shape[0], sectors, x.shape[1] // sectors), (1, 0, 2))


def shards(
    input_field,
    present_mask,
    lead_index,
    patch_weight,
    patch_bias,
    agg_query,
    agg_value,
    agg_out,
    lead_table,
    norm1_gain,
    qkv_weight,
    attn_out_weight,
    norm2_gain,
    up_weight,
    down_weight,
    head_weight,
    pred_cotangent,
):
    samples, chans, pix_rows, pix_cols = input_field.shape
    rows, cols = (pix_rows // 2, pix_cols // 2)
    span = rows * cols
    tokens = samples * span
    width = patch_weight.shape[2]
    heads = agg_query.shape[0]
    head_dim = width // heads
    local_width = qkv_weight.shape[2]
    local_heads = local_width // head_dim
    sectors = lax.axis_size("sector")
    mp_count = lax.axis_size("mp")
    mp_index = lax.axis_index("mp")
    score_scale = head_dim ** (-0.5)
    depth = 17 * chans

    fields = jnp.transpose(input_field, (0, 3, 1, 2))
    cots = jnp.transpose(pred_cotangent, (0, 3, 1, 2))
    before, after = ring_pair(
        jnp.stack([fields[:, 0], cots[:, 0]]), jnp.stack([fields[:, -1], cots[:, -1]])
    )
    win = windows(jnp.concatenate([before[0][:, None], fields, after[0][:, None]], axis=1))
    grad_head_t = windows(jnp.concatenate([before[1][:, None], cots, after[1][:, None]], axis=1))

    weight_kv = jnp.concatenate(
        [jnp.transpose(patch_weight, (1, 0, 2)), patch_bias[None]], axis=0
    ).reshape(depth, width)
    key_map_t = mm(agg_query, weight_kv, 1, 1)
    key_high = rounded(key_map_t)
    key_mid = rounded(key_map_t - key_high)
    key_low = key_map_t - key_high - key_mid
    own = (
        lax.broadcasted_iota(jnp.int32, (chans, 17, chans), 0)
        == lax.broadcasted_iota(jnp.int32, (chans, 17, chans), 2)
    ).reshape(1, 1, chans, depth)
    splits = jnp.stack([key_high, key_mid, key_low])[:, :, None, :]
    block_diag = jnp.where(own, splits, 0.0).astype(bf16).reshape(3, heads * chans, depth)
    value_t = mm(agg_value, weight_kv, 0, 1).astype(bf16)
    mask = jnp.broadcast_to(
        jnp.transpose(present_mask)[:, :, None], (chans, samples, span)
    ).reshape(chans, tokens)
    probs, pooled_t = agg_forward(win, block_diag, value_t, mask, heads)

    lead_hot = (lead_index[:, None] == jnp.arange(lead_table.shape[0])[None, :]).astype(f32)
    lead_rows = jnp.dot(lead_hot, lead_table.astype(f32), precision=highest)
    start_x = (
        mm(pooled_t, agg_out, 0, 0).reshape(samples, span, width) + lead_rows[:, None, :]
    ).reshape(tokens, width)
    normed1, hat_one, inv_one = norm_forward(start_x, norm1_gain)
    normed1_low = normed1.astype(bf16)

    qkv_t = lax.dot_general(
        qkv_weight, normed1_low, (((0,), (1,)), ((), ())), preferred_element_type=f32
    ).astype(bf16)
    packed = jnp.transpose(
        qkv_t.reshape(3, local_heads, head_dim, samples, span), (1, 3, 0, 2, 4)
    ).reshape(local_heads, samples, 3 * head_dim, span)
    by_head = sectors == local_heads * samples
    exchange = lambda x: lax.all_to_all(x, "sector", 0, 0, tiled=True)
    if by_head:
        held = exchange(packed.reshape(sectors, 3 * head_dim, span))
        att, lse = attend(held, score_scale)
        att = exchange(att).reshape(local_heads, samples, head_dim, span)
    else:
        att, lse = attend_gathered(packed, score_scale)
    att_t = jnp.transpose(att, (0, 2, 1, 3)).reshape(local_width, tokens)
    mid_x = start_x + sum_over_mp(mm(att_t, attn_out_weight, 0, 0))
    normed2, hat_two, inv_two = norm_forward(mid_x, norm2_gain)
    normed2_low = normed2.astype(bf16)
    hidden = jnp.dot(normed2_low, up_weight, preferred_element_type=f32)
    active_low = jax.nn.gelu(hidden, approximate=False).astype(bf16)

    head_cols = head_weight.shape[1]
    spot = lax.broadcasted_iota(jnp.int32, (head_cols, head_cols), 1)
    source = lax.broadcasted_iota(jnp.int32, (head_cols, head_cols), 0)
    shuffle = (source == (spot % chans) * 16 + spot // chans).astype(bf16)
    head_kv = jnp.dot(head_weight, shuffle, preferred_element_type=f32).astype(bf16)
    grad_head_flat = grad_head_t.reshape(head_cols, tokens)
    grad_end = mm(grad_head_flat, head_kv, 0, 1)
    grad_mlp = grad_end.astype(bf16)
    grad_active = mm(grad_mlp, down_weight, 1, 1)
    grad_hidden = (grad_active * gelu_slope(hidden)).astype(bf16)
    grad_normed2 = sum_over_mp(mm(grad_hidden, up_weight, 1, 1))
    grad_mid_norm, grad_gain_two = norm_backward(grad_normed2, norm2_gain, hat_two, inv_two)
    grad_mid = grad_end + grad_mid_norm
    grad_att = grad_mid.astype(bf16)
    grad_heads_t = mm(attn_out_weight, grad_att, 1, 1).astype(bf16)
    grad_heads = jnp.transpose(
        grad_heads_t.reshape(local_heads, head_dim, samples, span), (0, 2, 1, 3)
    )
    if by_head:
        grad_held = attend_back(
            held, exchange(grad_heads.reshape(sectors, head_dim, span)), lse, score_scale
        )
        grad_packed = exchange(grad_held)
    else:
        grad_packed = attend_back_gathered(packed, grad_heads, lse, score_scale)
    grad_qkv_t = jnp.transpose(
        grad_packed.reshape(local_heads, samples, 3, head_dim, span), (2, 0, 3, 1, 4)
    ).reshape(3, local_width, tokens)

    end_x = mid_x + sum_over_mp(jnp.dot(active_low, down_weight, preferred_element_type=f32))
    end_low = end_x.astype(bf16)
    head_out = mm(head_kv, end_low, 0, 1).astype(bf16).reshape(16, chans, tokens)
    canvas = fold(head_out, samples, cols, pix_rows)
    rim_before, rim_after = ring_pair(canvas[:, 0].astype(bf16), canvas[:, -1].astype(bf16))

    def close(canvas, rim_before, rim_after):
        inner = canvas[:, 1:-1]
        inner = inner.at[:, 0].add(rim_before.astype(f32))
        return inner.at[:, -1].add(rim_after.astype(f32))

    prediction = jnp.transpose(close(canvas, rim_before, rim_after), (0, 2, 3, 1))
    my_chans = chans // mp_count
    grad_head_rows = mp_slice(grad_head_t, 1, mp_index, mp_count).reshape(16 * my_chans, tokens)
    grad_head = jnp.dot(grad_head_rows, end_low, preferred_element_type=f32)

    grad_down = mm(active_low, grad_mlp, 0, 0)
    grad_up = mm(normed2_low, grad_hidden, 0, 0)
    grad_attn_out = jnp.dot(att_t, grad_att, preferred_element_type=f32)

    grad_normed1 = sum_over_mp(
        lax.dot_general(
            grad_qkv_t, qkv_weight, (((0, 1), (1, 2)), ((), ())), preferred_element_type=f32
        )
    )
    grad_qkv = lax.dot_general(
        normed1_low, grad_qkv_t, (((0,), (2,)), ((), ())), preferred_element_type=f32
    )
    grad_start_norm, grad_gain_one = norm_backward(grad_normed1, norm1_gain, hat_one, inv_one)
    grad_start = grad_mid + grad_start_norm
    grad_agg = grad_start.astype(bf16)
    grad_agg_out = jnp.dot(
        mp_slice(pooled_t, 0, mp_index, mp_count), grad_agg, preferred_element_type=f32
    )
    sample_sums = jnp.sum(grad_start.reshape(samples, span, width), axis=1)
    grad_lead = jnp.einsum("sl,sd->ld", lead_hot, sample_sums, precision=highest)
    grad_pooled_t = mm(agg_out, grad_agg, 1, 1).astype(bf16)
    value_heads = jnp.transpose(value_t.reshape(heads, head_dim, depth), (0, 2, 1))
    key_bd_t = jnp.transpose(block_diag[0, :, : 16 * chans])
    grad_win, value_grad_t, key_grad = agg_backward(
        win, probs, grad_pooled_t, value_heads, key_bd_t
    )
    value_grad_t = value_grad_t.astype(bf16)
    to_head = (
        lax.broadcasted_iota(jnp.int32, (heads * chans, heads), 0) // chans
        == lax.broadcasted_iota(jnp.int32, (heads * chans, heads), 1)
    ).astype(bf16)
    at_var = (
        lax.broadcasted_iota(jnp.int32, (depth, heads * chans), 0) % chans
        == lax.broadcasted_iota(jnp.int32, (depth, heads * chans), 1) % chans
    )
    key_map_grad = jnp.dot(
        jnp.where(at_var, key_grad, 0.0).astype(bf16), to_head, preferred_element_type=f32
    ).astype(bf16)
    grad_agg_value = mm(mp_slice(weight_kv, 1, mp_index, mp_count), value_grad_t, 0, 1)
    my_rows = lax.broadcasted_iota(jnp.int32, (17 * my_chans, depth), 0)
    all_rows = lax.broadcasted_iota(jnp.int32, (17 * my_chans, depth), 1)
    select = (
        all_rows
        == (my_rows // my_chans) * chans + mp_index * my_chans + my_rows % my_chans
    ).astype(bf16)
    value_grad_mine = mm(select, value_grad_t, 1, 1).astype(bf16)
    key_grad_mine = jnp.dot(select, key_map_grad, preferred_element_type=f32).astype(bf16)
    grad_ext = mm(value_grad_mine, agg_value, 1, 1) + jnp.dot(
        key_grad_mine, agg_query, preferred_element_type=f32
    )
    grad_agg_query = mm(mp_slice(key_map_grad, 1, mp_index, mp_count), weight_kv, 0, 0)

    grad_canvas = mp_slice(fold(grad_win, samples, cols, pix_rows), 2, mp_index, mp_count)
    grad_before, grad_after = ring_pair(
        grad_canvas[:, 0].astype(bf16), grad_canvas[:, -1].astype(bf16)
    )
    field_grad = jnp.transpose(close(grad_canvas, grad_before, grad_after), (0, 2, 3, 1))

    my_heads = heads // mp_count
    block = width // sectors
    if block % 128 == 0:
        early = jnp.concatenate(
            [
                grad_up.astype(bf16).reshape(sectors, block, grad_up.shape[1]),
                lanes_of(column_blocks(grad_down.astype(bf16), sectors), grad_up.shape[1]),
                lanes_of(column_blocks(grad_attn_out.astype(bf16), sectors), grad_up.shape[1]),
                lanes_of(column_blocks(grad_head.astype(bf16), sectors), grad_up.shape[1]),
            ],
            axis=1,
        )
        early = lax.psum_scatter(early, "sector", scatter_dimension=0).astype(f32)
        up_sum, down_sum, out_sum, head_sum = jnp.split(
            early,
            [
                block,
                block + grad_down.shape[0] * block // grad_up.shape[1],
                block + (grad_down.shape[0] + local_width) * block // grad_up.shape[1],
            ],
            axis=0,
        )
        down_sum, out_sum, head_sum = [rows_of(x, block) for x in (down_sum, out_sum, head_sum)]
        qkv_sum = scatter_sum(grad_qkv.reshape(sectors, block, 3, local_width))
        agg_out_sum = scatter_sum(column_blocks(grad_agg_out, sectors))
        late = jnp.concatenate(
            [grad_agg_value, grad_ext, grad_agg_query, grad_lead]
            + [grad_gain_one[None], grad_gain_two[None]],
            axis=0,
        )
        late = scatter_sum(column_blocks(late, sectors))
        sizes = (local_width, 17 * my_chans, my_heads, grad_lead.shape[0], 1, 1)
        sums = []
        at = 0
        for size in sizes:
            sums.append(late[at : at + size])
            at += size
        value_sum, ext_sum, query_sum, lead_sum, one_sum, two_sum = sums
    else:
        put = lambda x, dim: lax.psum_scatter(x, "sector", scatter_dimension=dim, tiled=True)
        up_sum, down_sum, out_sum, head_sum = (
            put(grad_up, 0),
            put(grad_down, 1),
            put(grad_attn_out, 1),
            put(grad_head, 1),
        )
        qkv_sum = put(grad_qkv, 0)
        agg_out_sum, value_sum, ext_sum, query_sum, lead_sum = (
            put(grad_agg_out, 1),
            put(grad_agg_value, 1),
            put(grad_ext, 1),
            put(grad_agg_query, 1),
            put(grad_lead, 1),
        )
        one_sum, two_sum = (put(grad_gain_one[None], 1), put(grad_gain_two[None], 1))
    ext_sum = jnp.transpose(ext_sum.reshape(17, my_chans, block), (1, 0, 2))
    head_sum = jnp.transpose(head_sum.reshape(16, my_chans, block), (2, 1, 0)).reshape(
        block, 16 * my_chans
    )
    return (
        prediction,
        field_grad,
        ext_sum[:, :16],
        ext_sum[:, 16],
        query_sum,
        value_sum,
        agg_out_sum,
        lead_sum,
        one_sum[0],
        qkv_sum,
        out_sum,
        two_sum[0],
        up_sum,
        down_sum,
        head_sum,
    )


def lanes_of(x, wide):
    sectors, count, block = x.shape
    beside = wide // block
    return jnp.transpose(x.reshape(sectors, beside, count // beside, block), (0, 2, 1, 3)).reshape(
        sectors, count // beside, wide
    )


def rows_of(x, block):
    count, wide = x.shape
    beside = wide // block
    return jnp.transpose(x.reshape(count, beside, block), (1, 0, 2)).reshape(count * beside, block)


def solution(mesh):
    placed = (
        P(None, None, None, "sector"),
        P(),
        P(),
        P(),
        P(),
        P(),
        P(),
        P(),
        P(),
        P(),
        P(None, None, "mp"),
        P("mp", None),
        P(),
        P(None, "mp"),
        P("mp", None),
        P(),
        P(None, None, None, "sector"),
    )
    return jax.shard_map(
        shards,
        mesh=mesh,
        in_specs=placed,
        out_specs=(
            P(None, None, None, "sector"),
            P(None, "mp", None, "sector"),
            P("mp", None, "sector"),
            P("mp", "sector"),
            P("mp", "sector"),
            P("mp", "sector"),
            P("mp", "sector"),
            P(None, "sector"),
            P("sector"),
            P("sector", None, "mp"),
            P("mp", "sector"),
            P("sector"),
            P("sector", "mp"),
            P("mp", "sector"),
            P("sector", "mp"),
        ),
        check_vma=False,
    )
```

```python
import functools

import jax
import jax.numpy as jnp
from jax import lax
from jax.experimental import pallas as pl
from jax.experimental.pallas import tpu as pltpu
from jax.sharding import PartitionSpec as P

bf16 = jnp.bfloat16
f32 = jnp.float32
highest = lax.Precision.HIGHEST
norm_eps = 1e-05
sqrt_half = 0.7071067811865476
inv_root_two_pi = 0.3989422804014327
vmem_most = 56 * 1024 * 1024


def mm(left, right, left_dim, right_dim):
    return lax.dot_general(
        left, right, (((left_dim,), (right_dim,)), ((), ())), preferred_element_type=f32
    )


def call(body, out_shape, cost, scalars=0, tensors=0, scratch=()):
    more = {}
    if scalars:
        more = dict(
            in_specs=[pl.BlockSpec(memory_space=pltpu.SMEM)] * scalars
            + [pl.BlockSpec(memory_space=pltpu.VMEM)] * tensors
        )
    return pl.pallas_call(
        body,
        out_shape=out_shape,
        scratch_shapes=list(scratch),
        compiler_params=pltpu.CompilerParams(vmem_limit_bytes=vmem_most),
        cost_estimate=pl.CostEstimate(
            flops=int(cost[0]), bytes_accessed=int(cost[1]), transcendentals=int(cost[2])
        ),
        **more,
    )


def row_pick(rows, patch_rows, patch_cols):
    span = patch_rows * patch_cols
    lane = lax.broadcasted_iota(jnp.int32, (rows, 4 * span), 1)
    row = lax.broadcasted_iota(jnp.int32, (rows, 4 * span), 0)
    r = lane // span
    rest = lane - r * span
    j = rest // patch_rows
    i = rest - j * patch_rows
    return (row == 2 * i + r - 1), j


def windows_body(x_ref, o_ref, *, group):
    samples, wide, chans, rows = x_ref.shape
    cols, patch_rows = (wide - 2) // 2, rows // 2
    span = cols * patch_rows
    hit, lane_col = row_pick(rows, patch_rows, cols)
    total = None
    for j in range(cols):
        left = jnp.concatenate(
            [x_ref[s, 2 * j + c] for s in range(samples) for c in range(4)], axis=0
        )
        pick = jnp.where(hit & (lane_col == j), 1.0, 0.0).astype(bf16)
        part = jnp.dot(left, pick, preferred_element_type=f32)
        total = part if total is None else total + part
    for s in range(samples):
        for c in range(4):
            for g in range(chans // group):
                at = (s * 4 + c) * chans + g * group
                for r in range(4):
                    to = (g * 16 + r * 4 + c) * group
                    o_ref[to : to + group, s * span : (s + 1) * span] = total[
                        at : at + group, r * span : (r + 1) * span
                    ].astype(o_ref.dtype)


def windows(x, group):
    samples, wide, chans, rows = x.shape
    tokens = samples * (wide - 2) * rows // 4
    return call(
        functools.partial(windows_body, group=group),
        jax.ShapeDtypeStruct((16 * chans, tokens), bf16),
        (2 * 16 * chans * tokens * 512, 4 * 16 * chans * tokens, 0),
    )(x)


def fold_body(g_ref, o_ref, *, cols, group):
    samples, _, chans, rows = o_ref.shape
    span = cols * rows // 2
    hit, lane_col = row_pick(rows, rows // 2, cols)

    def block(s, c, r):
        parts = []
        for g in range(chans // group):
            at = (g * 16 + r * 4 + c) * group
            parts.append(g_ref[at : at + group, s * span : (s + 1) * span])
        return jnp.concatenate(parts, axis=0)

    left = jnp.concatenate(
        [
            jnp.concatenate([block(s, c, r) for r in range(4)], axis=1)
            for s in range(samples)
            for c in range(4)
        ],
        axis=0,
    )
    held = [[None] * (2 * cols + 2) for _ in range(samples)]
    for j in range(cols):
        pick = jnp.where(hit & (lane_col == j), 1.0, 0.0).astype(bf16)
        part = mm(left, pick, 1, 1)
        for s in range(samples):
            for c in range(4):
                at = (s * 4 + c) * chans
                piece = part[at : at + chans]
                before = held[s][2 * j + c]
                held[s][2 * j + c] = piece if before is None else before + piece
    for s in range(samples):
        for col in range(2 * cols + 2):
            o_ref[s, col] = held[s][col]


def fold(g, samples, cols, rows, group):
    chans, tokens = (g.shape[0] // 16, g.shape[1])
    return call(
        functools.partial(fold_body, cols=cols, group=group),
        jax.ShapeDtypeStruct((samples, 2 * cols + 2, chans, rows), f32),
        (2 * 16 * chans * tokens * 512, 4 * 16 * chans * tokens, 0),
    )(g)


def own_lane(rows, lanes, group):
    row = lax.broadcasted_iota(jnp.int32, (rows, lanes), 0)
    lane = lax.broadcasted_iota(jnp.int32, (rows, lanes), 1)
    return row % group == lane % group


def agg_forward_body(win_ref, key_ref, value_ref, mask_ref, probs_ref, pooled_ref):
    groups, heads, group, lanes = probs_ref.shape
    inner = win_ref.shape[0] // groups
    head_dim = pooled_ref.shape[0] // heads
    own = own_lane(heads * group, inner, group)
    own_bias = own_lane(heads * group, group, group)
    spread = lambda x: jnp.broadcast_to(x[:, None, :], (heads, group, x.shape[1])).reshape(
        heads * group, x.shape[1]
    )
    scores = []
    for g in range(groups):
        keys = spread(key_ref[:, g * inner : (g + 1) * inner])
        keys = jnp.where(own, keys, 0.0)
        high = keys.astype(bf16)
        rest = keys - high.astype(f32)
        mid = rest.astype(bf16)
        least = (rest - mid.astype(f32)).astype(bf16)
        here = win_ref[g * inner : (g + 1) * inner, :]
        at = groups * inner + g * group
        bias = jnp.where(own_bias, spread(key_ref[:, at : at + group]), 0.0)
        scores.append(
            jnp.dot(high, here, preferred_element_type=f32)
            + jnp.dot(mid, here, preferred_element_type=f32)
            + jnp.dot(least, here, preferred_element_type=f32)
            + jnp.sum(bias, axis=1, keepdims=True)
        )
    window = inner // group
    win = win_ref[...].astype(f32).reshape(groups, window, group, lanes)
    pair = 128 // head_dim
    present = mask_ref[...].reshape(groups, group, lanes) > 0
    for h in range(heads):
        score = jnp.stack([x[h * group : (h + 1) * group] for x in scores])
        score = jnp.where(present, score, -1e30)
        most = jnp.max(jnp.max(score, axis=0), axis=0, keepdims=True)
        raised = jnp.exp(score - most[None])
        total = jnp.sum(jnp.sum(raised, axis=0), axis=0, keepdims=True)
        probs = raised * (1.0 / total)[None]
        probs_ref[:, h] = probs
        weighted = (win * probs[:, None]).astype(bf16).reshape(groups * inner, lanes)
        weighted = jnp.concatenate(
            [weighted, probs.astype(bf16).reshape(groups * group, lanes)], axis=0
        )
        if h % pair == 0:
            values = value_ref[:, h * head_dim : (h + pair) * head_dim].T
        at = h % pair * head_dim
        pooled_ref[h * head_dim : (h + 1) * head_dim, :] = jnp.dot(
            values[at : at + head_dim], weighted, preferred_element_type=f32
        ).astype(bf16)


def agg_forward(win, key_map_t, value_map, mask, group):
    rows, tokens = win.shape
    heads = key_map_t.shape[0]
    chans = mask.shape[0]
    depth, width = value_map.shape
    return call(
        agg_forward_body,
        (
            jax.ShapeDtypeStruct((chans // group, heads, group, tokens), f32),
            jax.ShapeDtypeStruct((width, tokens), bf16),
        ),
        (2 * tokens * depth * (width + heads * group), 6 * 2**20, heads * chans * tokens),
    )(win, key_map_t, value_map, mask)


def agg_backward_body(
    win_ref, probs_ref, gp_ref, value_ref, key_ref, gwin_ref, gvmt_ref, gkm_ref, gs_ref, acc_ref
):
    groups, heads, group, lanes = probs_ref.shape
    rows = win_ref.shape[0]
    inner = rows // groups
    window = inner // group
    head_dim = gp_ref.shape[0] // heads
    shape = (groups, window, group, lanes)
    win = win_ref[...].astype(f32).reshape(shape)
    for h in range(heads):
        here = slice(h * head_dim, (h + 1) * head_dim)
        gp = gp_ref[here, :]
        probs = probs_ref[:, h]
        gw = jnp.dot(value_ref[:, here], gp, preferred_element_type=f32)
        main = gw[:rows].reshape(shape)
        grad_probs = jnp.sum(main * win, axis=1) + gw[rows:].reshape(groups, group, lanes)
        delta = jnp.sum(jnp.sum(probs * grad_probs, axis=0), axis=0, keepdims=True)
        gs_ref[:, h * group : (h + 1) * group, :] = (probs * (grad_probs - delta[None])).astype(bf16)
        part = (main * probs[:, None]).reshape(rows, lanes)
        if h == 0:
            acc_ref[...] = part
        else:
            acc_ref[...] += part
        weighted = (win * probs[:, None]).astype(bf16).reshape(rows, lanes)
        weighted = jnp.concatenate(
            [weighted, probs.astype(bf16).reshape(groups * group, lanes)], axis=0
        )
        gvmt_ref[here, :] = mm(gp, weighted, 1, 1).astype(bf16)
    own = own_lane(heads * group, inner, group)
    own_bias = own_lane(heads * group, group, group)
    fold_in = lambda x: jnp.sum(x.reshape(heads, group, x.shape[1]), axis=1)
    for g in range(groups):
        here = slice(g * inner, (g + 1) * inner)
        keys = jnp.broadcast_to(key_ref[:, here][:, None, :], (heads, group, inner)).reshape(
            heads * group, inner
        )
        keys = jnp.where(own, keys, 0.0).astype(bf16)
        gs = gs_ref[g]
        gwin_ref[here, :] = (acc_ref[here, :] + mm(keys, gs, 0, 0)).astype(bf16)
        gkm_ref[:, here] = fold_in(jnp.where(own, mm(gs, win_ref[here, :], 1, 1), 0.0))
        total = jnp.sum(gs.astype(f32), axis=1, keepdims=True)
        at = rows + g * group
        gkm_ref[:, at : at + group] = fold_in(jnp.where(own_bias, total, 0.0))


def agg_backward(win, probs, grad_pooled_t, value_map, key_map_t):
    rows, tokens = win.shape
    groups, heads, group, _ = probs.shape
    depth, width = value_map.shape
    return call(
        agg_backward_body,
        (
            jax.ShapeDtypeStruct(win.shape, bf16),
            jax.ShapeDtypeStruct((width, depth), bf16),
            jax.ShapeDtypeStruct((heads, depth), f32),
        ),
        (4 * tokens * depth * (width + heads * group), 8 * 2**20, 0),
        scratch=(
            pltpu.VMEM((groups, heads * group, tokens), bf16),
            pltpu.VMEM((rows, tokens), f32),
        ),
    )(win, probs, grad_pooled_t, value_map, key_map_t)


def attend_body(x_ref, o_ref, lse_ref, key_ref, value_ref, query_ref, *, scale, wide):
    blocks, triple, span = x_ref.shape
    head_dim = triple // 3
    seq = blocks * span
    for n in range(blocks):
        here = slice(n * span, (n + 1) * span)
        query_ref[:, here] = x_ref[n, :head_dim, :] * jnp.asarray(scale, bf16)
        key_ref[here, :] = x_ref[n, head_dim : 2 * head_dim, :].T
        value_ref[:head_dim, here] = x_ref[n, 2 * head_dim :, :]
    value_ref[head_dim:, :] = jnp.ones((8, seq), bf16)
    for w in range(seq // wide):
        scores = jnp.dot(
            key_ref[...], query_ref[:, w * wide : (w + 1) * wide], preferred_element_type=f32
        )
        most = jnp.max(scores, axis=0, keepdims=True)
        raised = jnp.exp(scores - most).astype(bf16)
        both = jnp.dot(value_ref[...], raised, preferred_element_type=f32)
        total = both[head_dim : head_dim + 1]
        out = (both[:head_dim] * (1.0 / total)).astype(bf16)
        lse = most + jnp.log(total)
        for n in range(wide // span):
            here = slice(n * span, (n + 1) * span)
            o_ref[w * (wide // span) + n] = out[:, here]
            lse_ref[w * (wide // span) + n] = lse[:, here]


def attend(x, scale):
    blocks, triple, span = x.shape
    head_dim = triple // 3
    seq = blocks * span
    return call(
        functools.partial(attend_body, scale=scale, wide=max(span, seq // 2)),
        (
            jax.ShapeDtypeStruct((blocks, head_dim, span), bf16),
            jax.ShapeDtypeStruct((blocks, 1, span), f32),
        ),
        (4 * seq * seq * head_dim, 2 * x.size, seq * seq),
        scratch=(
            pltpu.VMEM((seq, head_dim), bf16),
            pltpu.VMEM((head_dim + 8, seq), bf16),
            pltpu.VMEM((head_dim, seq), bf16),
        ),
    )(x)


def attend_back_body(
    x_ref, do_ref, lse_ref, o_ref, key_ref, keyt_ref, value_ref, dkey_ref, dvalue_ref, *, scale
):
    blocks, triple, span = x_ref.shape
    head_dim = triple // 3
    for n in range(blocks):
        here = slice(n * span, (n + 1) * span)
        key_ref[here, :] = x_ref[n, head_dim : 2 * head_dim, :].T
        keyt_ref[:, here] = x_ref[n, head_dim : 2 * head_dim, :]
        value_ref[here, :] = x_ref[n, 2 * head_dim :, :].T
    for n in range(blocks):
        query = x_ref[n, :head_dim, :] * jnp.asarray(scale, bf16)
        grad = do_ref[n]
        scores = jnp.dot(key_ref[...], query, preferred_element_type=f32)
        probs = jnp.exp(scores - lse_ref[n])
        grad_probs = jnp.dot(value_ref[...], grad, preferred_element_type=f32)
        delta = jnp.sum(probs * grad_probs, axis=0, keepdims=True)
        grad_scores = (probs * (grad_probs - delta)).astype(bf16)
        o_ref[n, :head_dim, :] = (
            jnp.dot(keyt_ref[...], grad_scores, preferred_element_type=f32) * scale
        ).astype(bf16)
        dkey = jnp.dot(grad_scores, query.T, preferred_element_type=f32)
        dvalue = jnp.dot(probs.astype(bf16), grad.T, preferred_element_type=f32)
        if n == 0:
            dkey_ref[...] = dkey
            dvalue_ref[...] = dvalue
        else:
            dkey_ref[...] += dkey
            dvalue_ref[...] += dvalue
    for n in range(blocks):
        here = slice(n * span, (n + 1) * span)
        o_ref[n, head_dim : 2 * head_dim, :] = dkey_ref[here, :].T.astype(bf16)
        o_ref[n, 2 * head_dim :, :] = dvalue_ref[here, :].T.astype(bf16)


def attend_back(x, grad, lse, scale):
    blocks, triple, span = x.shape
    head_dim = triple // 3
    seq = blocks * span
    return call(
        functools.partial(attend_back_body, scale=scale),
        jax.ShapeDtypeStruct(x.shape, bf16),
        (10 * seq * seq * head_dim, 4 * x.size, seq * seq),
        scratch=(
            pltpu.VMEM((seq, head_dim), bf16),
            pltpu.VMEM((head_dim, seq), bf16),
            pltpu.VMEM((seq, head_dim), bf16),
            pltpu.VMEM((seq, head_dim), f32),
            pltpu.VMEM((seq, head_dim), f32),
        ),
    )(x, grad, lse)


def stats(x):
    centered = x - jnp.mean(x, axis=-1, keepdims=True)
    inverse = lax.rsqrt(jnp.mean(centered * centered, axis=-1, keepdims=True) + norm_eps)
    return centered * inverse, inverse


def norm_back(grad_out, gain, hat, inverse):
    grad_hat = grad_out * gain
    return inverse * (
        grad_hat
        - jnp.mean(grad_hat, axis=-1, keepdims=True)
        - hat * jnp.mean(grad_hat * hat, axis=-1, keepdims=True)
    )


def halves(core_ref, part_ref, mine_ref, other_ref):
    half = mine_ref.shape[0]
    core = core_ref[0]
    mine_ref[...] = part_ref[pl.ds(pl.multiple_of(core * half, half), half), :].astype(bf16)
    other_ref[...] = part_ref[pl.ds(pl.multiple_of((1 - core) * half, half), half), :].astype(bf16)


def joined(core_ref, mine_ref, other_ref, whole_ref):
    half = mine_ref.shape[0]
    core = core_ref[0]
    whole_ref[pl.ds(pl.multiple_of(core * half, half), half), :] = mine_ref[...].astype(f32)
    whole_ref[pl.ds(pl.multiple_of((1 - core) * half, half), half), :] = other_ref[...].astype(f32)


def enter_body(pooled_ref, out_ref, lead_ref, gain_ref, qkv_ref, start_ref, normed_ref, packed_ref):
    heads, samples, triple, span = packed_ref.shape
    head_dim = triple // 3
    x = jnp.dot(pooled_ref[...].T, out_ref[...], preferred_element_type=f32)
    for s in range(samples):
        here = slice(s * span, (s + 1) * span)
        start = x[here] + lead_ref[s : s + 1, :]
        start_ref[here, :] = start
        normed_ref[here, :] = (stats(start)[0] * gain_ref[...]).astype(bf16)
    for m in range(3):
        got = jnp.dot(normed_ref[...], qkv_ref[m], preferred_element_type=f32).astype(bf16).T
        for h in range(heads):
            for s in range(samples):
                packed_ref[h, s, m * head_dim : (m + 1) * head_dim, :] = got[
                    h * head_dim : (h + 1) * head_dim, s * span : (s + 1) * span
                ]


def enter(pooled_t, agg_out, lead_rows, gain, qkv, heads):
    width, tokens = pooled_t.shape
    samples = lead_rows.shape[0]
    head_dim = qkv.shape[2] // heads
    return call(
        enter_body,
        (
            jax.ShapeDtypeStruct((tokens, width), f32),
            jax.ShapeDtypeStruct((tokens, width), bf16),
            jax.ShapeDtypeStruct((heads, samples, 3 * head_dim, tokens // samples), bf16),
        ),
        (2 * tokens * width * (width + 3 * qkv.shape[2]), 8 * 2**20, 0),
    )(pooled_t, agg_out, lead_rows, gain, qkv)


def leave_body(core_ref, att_ref, weight_ref, att_t_ref, mine_ref, other_ref, part_ref):
    heads, samples, head_dim, span = att_ref.shape
    for s in range(samples):
        here = slice(s * span, (s + 1) * span)
        for h in range(heads):
            att_t_ref[h * head_dim : (h + 1) * head_dim, here] = att_ref[h, s]
    part_ref[...] = jnp.dot(att_t_ref[...].T, weight_ref[...], preferred_element_type=f32)
    halves(core_ref, part_ref, mine_ref, other_ref)


def leave(core, att, weight):
    heads, samples, head_dim, span = att.shape
    tokens, width = (samples * span, weight.shape[1])
    half = jax.ShapeDtypeStruct((tokens // 2, width), bf16)
    return call(
        leave_body,
        (jax.ShapeDtypeStruct((heads * head_dim, tokens), bf16), half, half),
        (2 * tokens * width * heads * head_dim, 3 * 2**20, 0),
        1,
        2,
        scratch=(pltpu.VMEM((tokens, width), f32),),
    )(core, att, weight)


def feed_body(
    core_ref,
    start_ref,
    mine_ref,
    other_ref,
    gain_ref,
    up_ref,
    grad_active_ref,
    mid_ref,
    normed_ref,
    active_ref,
    grad_hidden_ref,
    out_mine_ref,
    out_other_ref,
    part_ref,
):
    joined(core_ref, mine_ref, other_ref, part_ref)
    step = 128
    for at in range(0, start_ref.shape[0], step):
        here = slice(at, at + step)
        mid = start_ref[here, :] + part_ref[here, :]
        mid_ref[here, :] = mid
        normed = (stats(mid)[0] * gain_ref[...]).astype(bf16)
        normed_ref[here, :] = normed
        hidden = jnp.dot(normed, up_ref[...], preferred_element_type=f32)
        both = 0.5 * (1.0 + lax.erf(hidden * sqrt_half))
        active_ref[here, :] = (hidden * both).astype(bf16)
        slope = both + hidden * jnp.exp(-0.5 * hidden * hidden) * inv_root_two_pi
        grad = (grad_active_ref[here, :].astype(f32) * slope).astype(bf16)
        grad_hidden_ref[here, :] = grad
        part_ref[here, :] = mm(grad, up_ref[...], 1, 1)
    halves(core_ref, part_ref, out_mine_ref, out_other_ref)


def feed(core, start, mine, other, gain, up, grad_active):
    tokens, width = start.shape
    low = jax.ShapeDtypeStruct((tokens, width), bf16)
    wide = jax.ShapeDtypeStruct((tokens, up.shape[1]), bf16)
    half = jax.ShapeDtypeStruct(mine.shape, bf16)
    return call(
        feed_body,
        (jax.ShapeDtypeStruct((tokens, width), f32), low, wide, wide, half, half),
        (4 * tokens * width * up.shape[1], 14 * 2**20, 2 * tokens * up.shape[1]),
        1,
        6,
        scratch=(pltpu.VMEM((tokens, width), f32),),
    )(core, start, mine, other, gain, up, grad_active)


def feed_back_body(
    core_ref,
    mid_ref,
    mine_ref,
    other_ref,
    gain_ref,
    grad_end_ref,
    weight_ref,
    grad_mid_ref,
    grad_att_ref,
    grad_gain_ref,
    packed_ref,
    part_ref,
):
    heads, samples, head_dim, span = packed_ref.shape
    joined(core_ref, mine_ref, other_ref, part_ref)
    grad_gain = jnp.zeros(grad_gain_ref.shape, f32)
    step = 128
    for at in range(0, mid_ref.shape[0], step):
        here = slice(at, at + step)
        hat, inverse = stats(mid_ref[here, :])
        grad_out = part_ref[here, :]
        grad_gain += jnp.sum(grad_out * hat, axis=0, keepdims=True)
        grad = grad_end_ref[here, :] + norm_back(grad_out, gain_ref[...], hat, inverse)
        grad_mid_ref[here, :] = grad
        grad_att_ref[here, :] = grad.astype(bf16)
    grad_gain_ref[...] = grad_gain
    got = mm(weight_ref[...], grad_att_ref[...], 1, 1).astype(bf16)
    for h in range(heads):
        for s in range(samples):
            packed_ref[h, s] = got[h * head_dim : (h + 1) * head_dim, s * span : (s + 1) * span]


def feed_back(core, mid, mine, other, gain, grad_end, weight, heads, samples):
    tokens, width = mid.shape
    return call(
        feed_back_body,
        (
            jax.ShapeDtypeStruct((tokens, width), f32),
            jax.ShapeDtypeStruct((tokens, width), bf16),
            jax.ShapeDtypeStruct((1, width), f32),
            jax.ShapeDtypeStruct(
                (heads, samples, weight.shape[0] // heads, tokens // samples), bf16
            ),
        ),
        (2 * tokens * width * weight.shape[0], 9 * 2**20, 0),
        1,
        6,
        scratch=(pltpu.VMEM((tokens, width), f32),),
    )(core, mid, mine, other, gain, grad_end, weight)


def enter_back_body(core_ref, packed_ref, qkv_ref, flat_ref, mine_ref, other_ref, part_ref):
    heads, samples, triple, span = packed_ref.shape
    head_dim = triple // 3
    width = heads * head_dim
    for m in range(3):
        for h in range(heads):
            for s in range(samples):
                to = m * width + h * head_dim
                flat_ref[to : to + head_dim, s * span : (s + 1) * span] = packed_ref[
                    h, s, m * head_dim : (m + 1) * head_dim, :
                ]
    for m in range(3):
        part = mm(flat_ref[m * width : (m + 1) * width, :].T, qkv_ref[m], 1, 1)
        if m == 0:
            part_ref[...] = part
        else:
            part_ref[...] += part
    halves(core_ref, part_ref, mine_ref, other_ref)


def enter_back(core, packed, qkv):
    heads, samples, triple, span = packed.shape
    tokens, width = (samples * span, qkv.shape[1])
    half = jax.ShapeDtypeStruct((tokens // 2, width), bf16)
    return call(
        enter_back_body,
        (jax.ShapeDtypeStruct((heads * triple, tokens), bf16), half, half),
        (2 * tokens * width * heads * triple, 5 * 2**20, 0),
        1,
        2,
        scratch=(pltpu.VMEM((tokens, width), f32),),
    )(core, packed, qkv)


def pool_back_body(
    core_ref,
    start_ref,
    mine_ref,
    other_ref,
    gain_ref,
    grad_mid_ref,
    out_ref,
    grad_agg_ref,
    grad_gain_ref,
    sums_ref,
    pooled_ref,
    part_ref,
):
    samples = sums_ref.shape[0]
    tokens = start_ref.shape[0]
    joined(core_ref, mine_ref, other_ref, part_ref)
    grad_gain = jnp.zeros(grad_gain_ref.shape, f32)
    step = min(128, tokens // samples)
    sums = [jnp.zeros(grad_gain_ref.shape, f32) for _ in range(samples)]
    for at in range(0, tokens, step):
        here = slice(at, at + step)
        hat, inverse = stats(start_ref[here, :])
        grad_out = part_ref[here, :]
        grad_gain += jnp.sum(grad_out * hat, axis=0, keepdims=True)
        grad = grad_mid_ref[here, :] + norm_back(grad_out, gain_ref[...], hat, inverse)
        sums[at * samples // tokens] += jnp.sum(grad, axis=0, keepdims=True)
        grad_agg_ref[here, :] = grad.astype(bf16)
    grad_gain_ref[...] = grad_gain
    sums_ref[...] = jnp.concatenate(sums, axis=0)
    pooled_ref[...] = mm(out_ref[...], grad_agg_ref[...], 1, 1).astype(bf16)


def pool_back(core, start, mine, other, gain, grad_mid, agg_out, samples):
    tokens, width = start.shape
    return call(
        pool_back_body,
        (
            jax.ShapeDtypeStruct((tokens, width), bf16),
            jax.ShapeDtypeStruct((1, width), f32),
            jax.ShapeDtypeStruct((samples, width), f32),
            jax.ShapeDtypeStruct((width, tokens), bf16),
        ),
        (2 * tokens * width * width, 9 * 2**20, 0),
        1,
        6,
        scratch=(pltpu.VMEM((tokens, width), f32),),
    )(core, start, mine, other, gain, grad_mid, agg_out)


def feed_grads_body(normed_ref, grad_hidden_ref, grad_mlp_ref, active_ref, o_ref):
    block = o_ref.shape[1] // 2
    o_ref[0, :block] = mm(normed_ref[...], grad_hidden_ref[...], 0, 0).astype(bf16)
    o_ref[0, block:] = mm(grad_mlp_ref[...], active_ref[...], 0, 0).astype(bf16)


def feed_grads(normed, grad_hidden, grad_mlp, active, sectors):
    tokens, width = normed.shape
    hidden = active.shape[1]
    block = width // sectors
    strip = pl.BlockSpec((tokens, block), lambda i: (0, i))
    whole = pl.BlockSpec((tokens, hidden), lambda i: (0, 0))
    return pl.pallas_call(
        feed_grads_body,
        out_shape=jax.ShapeDtypeStruct((sectors, 2 * block, hidden), bf16),
        grid=(sectors,),
        in_specs=[strip, whole, strip, whole],
        out_specs=pl.BlockSpec((1, 2 * block, hidden), lambda i: (i, 0, 0)),
        compiler_params=pltpu.CompilerParams(vmem_limit_bytes=vmem_most),
        cost_estimate=pl.CostEstimate(
            flops=4 * tokens * width * hidden, bytes_accessed=8 * 2**20, transcendentals=0
        ),
    )(normed, grad_hidden, grad_mlp, active)


def attend_gathered(packed, scale):
    head_dim = packed.shape[2] // 3
    whole = lax.all_gather(packed[:, :, head_dim:, :], "sector", axis=0)
    keys, values = (whole[:, :, :, :head_dim], whole[:, :, :, head_dim:])
    scores = (
        jnp.einsum("hsdq,nhsdk->hsqnk", packed[:, :, :head_dim], keys, preferred_element_type=f32)
        * scale
    )
    most = jnp.max(scores, axis=(3, 4), keepdims=True)
    raised = jnp.exp(scores - most)
    total = jnp.sum(raised, axis=(3, 4), keepdims=True)
    probs = (raised / total).astype(bf16)
    out = jnp.einsum("hsqnk,nhsdk->hsdq", probs, values, preferred_element_type=f32)
    return out.astype(bf16), most + jnp.log(total)


def attend_back_gathered(packed, grad, lse, scale):
    head_dim = packed.shape[2] // 3
    query = packed[:, :, :head_dim]
    whole = lax.all_gather(packed[:, :, head_dim:, :], "sector", axis=0)
    keys, values = (whole[:, :, :, :head_dim], whole[:, :, :, head_dim:])
    scores = jnp.einsum("hsdq,nhsdk->hsqnk", query, keys, preferred_element_type=f32) * scale
    probs = jnp.exp(scores - lse)
    grad_probs = jnp.einsum("hsdq,nhsdk->hsqnk", grad, values, preferred_element_type=f32)
    delta = jnp.sum(probs * grad_probs, axis=(3, 4), keepdims=True)
    grad_scores = (probs * (grad_probs - delta)).astype(bf16)
    grad_query = jnp.einsum("hsqnk,nhsdk->hsdq", grad_scores, keys, preferred_element_type=f32)
    grad_keys = jnp.einsum("hsqnk,hsdq->nhsdk", grad_scores, query, preferred_element_type=f32)
    grad_values = jnp.einsum(
        "hsqnk,hsdq->nhsdk", probs.astype(bf16), grad, preferred_element_type=f32
    )
    both = lax.psum_scatter(
        jnp.concatenate([grad_keys * scale, grad_values], axis=3), "sector", scatter_dimension=0
    )
    return jnp.concatenate([grad_query * scale, both], axis=2).astype(bf16)


def swap(x, axis, bit):
    size = lax.axis_size(axis)
    return lax.ppermute(x, axis, [(i, i ^ bit) for i in range(size)])


def rounded(x):
    return lax.reduce_precision(x, 8, 7)


def sum_over_mp(x):
    if lax.axis_size("mp") != 4:
        return lax.psum(x.astype(bf16), "mp").astype(f32)
    half = x.shape[0] // 2
    low, high = (rounded(x[:half]), rounded(x[half:]))
    first = lax.axis_index("mp") % 2 == 0
    mine, other = (jnp.where(first, low, high), jnp.where(first, high, low))
    mine = rounded(mine + swap(other.astype(bf16), "mp", 1).astype(f32))
    mine = rounded(mine + swap(mine.astype(bf16), "mp", 2).astype(f32))
    other = swap(mine.astype(bf16), "mp", 1).astype(f32)
    return jnp.concatenate([jnp.where(first, mine, other), jnp.where(first, other, mine)], axis=0)


def exchange_halves(mine, other):
    mine = rounded(mine.astype(f32) + swap(other, "mp", 1).astype(f32)).astype(bf16)
    mine = rounded(mine.astype(f32) + swap(mine, "mp", 2).astype(f32)).astype(bf16)
    return mine, swap(mine, "mp", 1)


def ring_pair(leading, last):
    size = lax.axis_size("sector")
    up = [(i, (i + 1) % size) for i in range(size)]
    down = [(j, i) for i, j in up]
    return lax.ppermute(last, "sector", up), lax.ppermute(leading, "sector", down)


def split_cols(x, block):
    even = lax.axis_index("sector") % 2 == 0
    pairs = x.shape[1] // (2 * block)
    low = [x[:, 2 * p * block : (2 * p + 1) * block] for p in range(pairs)]
    high = [x[:, (2 * p + 1) * block : (2 * p + 2) * block] for p in range(pairs)]
    mine = [jnp.where(even, a, b) for a, b in zip(low, high)]
    other = [jnp.where(even, b, a) for a, b in zip(low, high)]
    return jnp.concatenate(mine, axis=1), jnp.concatenate(other, axis=1)


def pair_sum(mine, other):
    return mine.astype(f32) + swap(other.astype(bf16), "sector", 1).astype(f32)


def line_sum(x):
    size = lax.axis_size("sector")
    lines = [list(range(parity, size, 2)) for parity in range(2)]
    got = lax.all_to_all(
        x.astype(bf16), "sector", 0, 0, axis_index_groups=lines, tiled=True
    )
    return jnp.sum(got.astype(f32), axis=0)


def norm_forward(values, gain_vec):
    row_mean = jnp.mean(values, axis=-1, keepdims=True)
    centered = values - row_mean
    inverse = lax.rsqrt(jnp.mean(centered * centered, axis=-1, keepdims=True) + norm_eps)
    normed = centered * inverse
    return (normed * gain_vec, normed, inverse)


def norm_backward(grad_out, gain_vec, normed, inverse):
    grad_normed = grad_out * gain_vec
    grad_gain = jnp.sum(grad_out * normed, axis=0)
    grad_in = inverse * (
        grad_normed
        - jnp.mean(grad_normed, axis=-1, keepdims=True)
        - normed * jnp.mean(grad_normed * normed, axis=-1, keepdims=True)
    )
    return (grad_in, grad_gain)


def gelu_slope(values):
    return (
        0.5 * (1.0 + lax.erf(values * sqrt_half))
        + values * jnp.exp(-0.5 * values * values) * inv_root_two_pi
    )


def mp_slice(values, axis_dim, mp_index, mp_count):
    piece_len = values.shape[axis_dim] // mp_count
    return lax.dynamic_slice_in_dim(values, mp_index * piece_len, piece_len, axis_dim)


def side_by_side(x, block):
    return jnp.stack([x[:, at : at + block] for at in range(0, x.shape[1], block)])


def shards(
    input_field,
    present_mask,
    lead_index,
    patch_weight,
    patch_bias,
    agg_query,
    agg_value,
    agg_out,
    lead_table,
    norm1_gain,
    qkv_weight,
    attn_out_weight,
    norm2_gain,
    up_weight,
    down_weight,
    head_weight,
    pred_cotangent,
):
    samples, chans, pix_rows, pix_cols = input_field.shape
    rows, cols = (pix_rows // 2, pix_cols // 2)
    span = rows * cols
    tokens = samples * span
    width = patch_weight.shape[2]
    heads = agg_query.shape[0]
    head_dim = width // heads
    local_width = qkv_weight.shape[2]
    local_heads = local_width // head_dim
    sectors = lax.axis_size("sector")
    mp_count = lax.axis_size("mp")
    mp_index = lax.axis_index("mp")
    score_scale = head_dim ** (-0.5)
    depth = 17 * chans
    group = 16 if chans % 16 == 0 else chans
    groups = chans // group

    by_head = sectors == local_heads * samples
    block = width // sectors
    fast = by_head and block % 128 == 0 and mp_count == 4 and samples % 2 == 0 and span % 128 == 0
    exchange = lambda x: lax.all_to_all(
        x.reshape(sectors, x.shape[-2], x.shape[-1]), "sector", 0, 0, tiled=True
    )
    by_pair = lambda x: x.reshape(local_heads, samples, x.shape[1], x.shape[2])
    core = (mp_index % 2).reshape(1)
    barrier = lax.optimization_barrier

    fields = jnp.transpose(input_field, (0, 3, 1, 2))
    cots = jnp.transpose(pred_cotangent, (0, 3, 1, 2))
    before, after = ring_pair(
        jnp.stack([fields[:, 0], cots[:, 0]]), jnp.stack([fields[:, -1], cots[:, -1]])
    )
    haloed = lambda x, n: jnp.concatenate([before[n][:, None], x, after[n][:, None]], axis=1)
    win = windows(haloed(fields, 0), group)

    weight_kv = jnp.concatenate(
        [
            jnp.transpose(patch_weight.reshape(groups, group, 16, width), (0, 2, 1, 3)).reshape(
                16 * chans, width
            ),
            patch_bias,
        ],
        axis=0,
    )
    key_map_t = mm(agg_query, weight_kv, 1, 1)
    value_map = jnp.dot(weight_kv, agg_value, preferred_element_type=f32).astype(bf16)
    mask = jnp.broadcast_to(
        jnp.transpose(present_mask)[:, :, None], (chans, samples, span)
    ).reshape(chans, tokens)
    probs, pooled_t = agg_forward(win, key_map_t, value_map, mask, group)
    lead_hot = (lead_index[:, None] == jnp.arange(lead_table.shape[0])[None, :]).astype(f32)
    lead_rows = jnp.dot(lead_hot, lead_table.astype(f32), precision=highest)

    head_cols = head_weight.shape[1]
    spot = lax.broadcasted_iota(jnp.int32, (head_cols, head_cols), 1)
    source = lax.broadcasted_iota(jnp.int32, (head_cols, head_cols), 0)
    place = (spot % (16 * group)) // group
    shuffle = ((spot // (16 * group) * group + spot % group) * 16 + place == source).astype(bf16)
    head_kv = jnp.dot(head_weight, shuffle, preferred_element_type=f32).astype(bf16)
    grad_head_t = windows(haloed(cots, 1), group)
    grad_end = mm(grad_head_t, head_kv, 0, 1)
    grad_mlp = grad_end.astype(bf16)
    grad_active = mm(grad_mlp, down_weight, 1, 1)

    if fast:
        qkv = jnp.transpose(qkv_weight, (1, 0, 2))
        start_x, normed1_low, packed = enter(
            pooled_t, agg_out, lead_rows, norm1_gain[None], qkv, local_heads
        )
        held = exchange(packed)
        held, grad_active, grad_end = barrier((held, grad_active, grad_end))
        att_held, lse = attend(held, score_scale)
        att_t, mine, other = leave(core, by_pair(exchange(att_held)), attn_out_weight)
        mid_x, normed2_low, active_low, grad_hidden, mine, other = feed(
            core,
            start_x,
            *exchange_halves(mine, other),
            norm2_gain[None],
            up_weight,
            grad_active,
        )
        early = feed_grads(normed2_low, grad_hidden, grad_mlp, active_low, sectors)
        mine, other, early = barrier((*exchange_halves(mine, other), early))
        early_sum = lax.psum_scatter(early, "sector", scatter_dimension=0)
        grad_mid, grad_att, grad_gain_two, grad_heads = feed_back(
            core,
            mid_x,
            mine,
            other,
            norm2_gain[None],
            grad_end,
            attn_out_weight,
            local_heads,
            samples,
        )
        active_late, grad_heads = barrier((active_low, grad_heads))
        grad_held = attend_back(held, exchange(grad_heads), lse, score_scale)
        grad_packed = by_pair(exchange(grad_held))
    else:
        start_x = (
            mm(pooled_t, agg_out, 0, 0).reshape(samples, span, width) + lead_rows[:, None, :]
        ).reshape(tokens, width)
        normed1, hat_one, inv_one = norm_forward(start_x, norm1_gain)
        normed1_low = normed1.astype(bf16)
        qkv_t = lax.dot_general(
            qkv_weight, normed1_low, (((0,), (1,)), ((), ())), preferred_element_type=f32
        ).astype(bf16)
        packed = jnp.transpose(
            qkv_t.reshape(3, local_heads, head_dim, samples, span), (1, 3, 0, 2, 4)
        ).reshape(local_heads, samples, 3 * head_dim, span)
        att, lse = attend_gathered(packed, score_scale)
        att_t = jnp.transpose(att, (0, 2, 1, 3)).reshape(local_width, tokens)
        mid_x = start_x + sum_over_mp(mm(att_t, attn_out_weight, 0, 0))
        normed2, hat_two, inv_two = norm_forward(mid_x, norm2_gain)
        normed2_low = normed2.astype(bf16)
        hidden = jnp.dot(normed2_low, up_weight, preferred_element_type=f32)
        active_low = jax.nn.gelu(hidden, approximate=False).astype(bf16)
        active_late = active_low
        grad_hidden = (grad_active * gelu_slope(hidden)).astype(bf16)
        grad_normed2 = sum_over_mp(mm(grad_hidden, up_weight, 1, 1))
        grad_mid_norm, grad_gain_two = norm_backward(grad_normed2, norm2_gain, hat_two, inv_two)
        grad_mid = grad_end + grad_mid_norm
        grad_att = grad_mid.astype(bf16)
        grad_heads_t = mm(attn_out_weight, grad_att, 1, 1).astype(bf16)
        grad_heads = jnp.transpose(
            grad_heads_t.reshape(local_heads, head_dim, samples, span), (0, 2, 1, 3)
        )
        grad_packed = attend_back_gathered(packed, grad_heads, lse, score_scale)

    end_x = mid_x + sum_over_mp(jnp.dot(active_late, down_weight, preferred_element_type=f32))
    end_low = end_x.astype(bf16)
    head_out = mm(head_kv, end_low, 0, 1).astype(bf16)
    canvas = fold(head_out, samples, cols, pix_rows, group)
    rim_before, rim_after = ring_pair(canvas[:, 0].astype(bf16), canvas[:, -1].astype(bf16))

    def close(canvas, rim_before, rim_after):
        inner = canvas[:, 1:-1]
        inner = inner.at[:, 0].add(rim_before.astype(f32))
        return inner.at[:, -1].add(rim_after.astype(f32))

    prediction = jnp.transpose(close(canvas, rim_before, rim_after), (0, 2, 3, 1))

    my_chans = chans // mp_count
    row = lax.broadcasted_iota(jnp.int32, (17 * my_chans, depth), 0)
    col = lax.broadcasted_iota(jnp.int32, (17 * my_chans, depth), 1)
    var = mp_index * my_chans + jnp.where(row < 16 * my_chans, row // 16, row - 16 * my_chans)
    from_window = (var // group * 16 + row % 16) * group + var % group
    select = (
        col == jnp.where(row < 16 * my_chans, from_window, 16 * chans + var)
    ).astype(bf16)
    my_head = jnp.dot(
        select[: 16 * my_chans, : 16 * chans], grad_head_t, preferred_element_type=f32
    ).astype(bf16)

    if fast:
        flat, mine, other = enter_back(core, grad_packed, qkv)
        mine, other = exchange_halves(mine, other)
        grad_agg, grad_gain_one, sample_sums, grad_pooled_t = pool_back(
            core, start_x, mine, other, norm1_gain[None], grad_mid, agg_out, samples
        )
    else:
        flat = jnp.transpose(
            grad_packed.reshape(local_heads, samples, 3, head_dim, span), (2, 0, 3, 1, 4)
        ).reshape(3 * local_width, tokens)
        grad_normed1 = sum_over_mp(
            lax.dot_general(
                flat.reshape(3, local_width, tokens),
                qkv_weight,
                (((0, 1), (1, 2)), ((), ())),
                preferred_element_type=f32,
            )
        )
        grad_start_norm, grad_gain_one = norm_backward(grad_normed1, norm1_gain, hat_one, inv_one)
        grad_start = grad_mid + grad_start_norm
        grad_agg = grad_start.astype(bf16)
        sample_sums = jnp.sum(grad_start.reshape(samples, span, width), axis=1)
        grad_pooled_t = mm(agg_out, grad_agg, 1, 1).astype(bf16)
    my_pooled = mp_slice(pooled_t, 0, mp_index, mp_count)
    grad_lead = jnp.einsum("sl,sd->ld", lead_hot, sample_sums, precision=highest)
    gains = [x.reshape(1, width) for x in (grad_gain_one, grad_gain_two)]
    grad_win, value_grad_t, key_grad = agg_backward(
        win, probs, grad_pooled_t, value_map, key_map_t
    )
    key_low = key_grad.astype(bf16)
    grad_agg_value = mm(mp_slice(weight_kv, 1, mp_index, mp_count), value_grad_t, 0, 1)
    my_value = mm(select, value_grad_t, 1, 1).astype(bf16)
    my_key = mm(select, key_low, 1, 1).astype(bf16)
    grad_ext = mm(my_value, agg_value, 1, 1) + jnp.dot(
        my_key, agg_query, preferred_element_type=f32
    )
    grad_agg_query = jnp.dot(
        mp_slice(key_low, 0, mp_index, mp_count), weight_kv, preferred_element_type=f32
    )

    row = lax.broadcasted_iota(jnp.int32, (16 * group, 16 * chans), 0)
    col = lax.broadcasted_iota(jnp.int32, (16 * group, 16 * chans), 1)
    var = mp_index * my_chans + row % group
    pick = (
        (col == (var // group * 16 + row // group) * group + var % group)
        & (row % group < my_chans)
    ).astype(bf16)
    my_win = jnp.dot(pick, grad_win, preferred_element_type=f32).astype(bf16)
    grad_canvas = fold(my_win, samples, cols, pix_rows, group)[:, :, :my_chans]
    grad_before, grad_after = ring_pair(
        grad_canvas[:, 0].astype(bf16), grad_canvas[:, -1].astype(bf16)
    )
    field_grad = jnp.transpose(close(grad_canvas, grad_before, grad_after), (0, 2, 3, 1))

    my_heads = heads // mp_count
    late = [grad_agg_value, grad_ext, grad_agg_query, grad_lead] + gains
    if fast:
        dots = lambda left, pair: [jnp.dot(left, x, preferred_element_type=f32) for x in pair]
        out_pair = pair_sum(*dots(att_t, split_cols(grad_att, block)))
        joint = lambda a, b: [jnp.concatenate([x, y], axis=0) for x, y in zip(a, b)]
        mid_pair = pair_sum(
            *joint(
                dots(my_head, split_cols(end_low, block)),
                dots(flat, split_cols(normed1_low, block)),
            )
        )
        mid_pair = jnp.concatenate([out_pair.astype(bf16), mid_pair.astype(bf16)], axis=0)
        mid_sum = line_sum(side_by_side(mid_pair, block))
        agg_pair = pair_sum(*dots(my_pooled, split_cols(grad_agg, block)))
        late = jnp.concatenate([x.astype(bf16) for x in late], axis=0)
        late_pair = pair_sum(*split_cols(late, block))
        late_sum = line_sum(
            side_by_side(jnp.concatenate([agg_pair.astype(bf16), late_pair.astype(bf16)]), block)
        )
        out_sum, head_sum, qkv_sum = jnp.split(mid_sum, [local_width, local_width + 16 * my_chans])
        qkv_sum = jnp.transpose(qkv_sum.reshape(3, local_width, block), (2, 0, 1))
        sums = []
        at = 0
        sizes = (local_width, local_width, 17 * my_chans, my_heads, grad_lead.shape[0], 1, 1)
        for size in sizes:
            sums.append(late_sum[at : at + size])
            at += size
        agg_out_sum, value_sum, ext_sum, query_sum, lead_sum, one_sum, two_sum = sums
        early_sum = early_sum.astype(f32)
        up_sum, down_sum = (early_sum[:block], jnp.transpose(early_sum[block:]))
    else:
        put = lambda x, dim: lax.psum_scatter(x, "sector", scatter_dimension=dim, tiled=True)
        up_sum = put(mm(normed2_low, grad_hidden, 0, 0), 0)
        down_sum = put(mm(active_low, grad_mlp, 0, 0), 1)
        out_sum = put(jnp.dot(att_t, grad_att, preferred_element_type=f32), 1)
        head_sum = put(jnp.dot(my_head, end_low, preferred_element_type=f32), 1)
        qkv_sum = put(mm(normed1_low, flat, 0, 1), 0).reshape(block, 3, local_width)
        agg_out_sum = put(jnp.dot(my_pooled, grad_agg, preferred_element_type=f32), 1)
        value_sum, ext_sum, query_sum, lead_sum, one_sum, two_sum = [put(x, 1) for x in late]
    return (
        prediction,
        field_grad,
        ext_sum[: 16 * my_chans].reshape(my_chans, 16, block),
        ext_sum[16 * my_chans :],
        query_sum,
        value_sum,
        agg_out_sum,
        lead_sum,
        one_sum[0],
        qkv_sum,
        out_sum,
        two_sum[0],
        up_sum,
        down_sum,
        jnp.transpose(head_sum),
    )


def solution(mesh):
    placed = (
        P(None, None, None, "sector"),
        P(),
        P(),
        P(),
        P(),
        P(),
        P(),
        P(),
        P(),
        P(),
        P(None, None, "mp"),
        P("mp", None),
        P(),
        P(None, "mp"),
        P("mp", None),
        P(),
        P(None, None, None, "sector"),
    )
    return jax.shard_map(
        shards,
        mesh=mesh,
        in_specs=placed,
        out_specs=(
            P(None, None, None, "sector"),
            P(None, "mp", None, "sector"),
            P("mp", None, "sector"),
            P("mp", "sector"),
            P("mp", "sector"),
            P("mp", "sector"),
            P("mp", "sector"),
            P(None, "sector"),
            P("sector"),
            P("sector", None, "mp"),
            P("mp", "sector"),
            P("sector"),
            P("sector", "mp"),
            P("mp", "sector"),
            P("sector", "mp"),
        ),
        check_vma=False,
    )
```

```python
import functools

import jax
import jax.numpy as jnp
from jax import lax
from jax.experimental import pallas as pl
from jax.experimental.pallas import tpu as pltpu
from jax.sharding import PartitionSpec as P

bf16 = jnp.bfloat16
f32 = jnp.float32
highest = lax.Precision.HIGHEST
norm_eps = 1e-05
sqrt_half = 0.7071067811865476
inv_root_two_pi = 0.3989422804014327
vmem_most = 32 * 1024 * 1024


def mm(left, right, left_dim, right_dim):
    return lax.dot_general(
        left, right, (((left_dim,), (right_dim,)), ((), ())), preferred_element_type=f32
    )


def call(body, out_shape, cost, scalars=0, tensors=0, scratch=()):
    more = {}
    if scalars:
        more = dict(
            in_specs=[pl.BlockSpec(memory_space=pltpu.SMEM)] * scalars
            + [pl.BlockSpec(memory_space=pltpu.VMEM)] * tensors
        )
    return pl.pallas_call(
        body,
        out_shape=out_shape,
        scratch_shapes=list(scratch),
        compiler_params=pltpu.CompilerParams(vmem_limit_bytes=vmem_most),
        cost_estimate=pl.CostEstimate(
            flops=int(cost[0]) // 8, bytes_accessed=int(cost[1]) // 8, transcendentals=int(cost[2]) // 8
        ),
        **more,
    )


def row_pick(rows, patch_rows, patch_cols):
    span = patch_rows * patch_cols
    lane = lax.broadcasted_iota(jnp.int32, (rows, 4 * span), 1)
    row = lax.broadcasted_iota(jnp.int32, (rows, 4 * span), 0)
    r = lane // span
    rest = lane - r * span
    j = rest // patch_rows
    i = rest - j * patch_rows
    return (row == 2 * i + r - 1), j


def windows_body(x_ref, o_ref, *, group):
    samples, wide, chans, rows = x_ref.shape
    cols, patch_rows = (wide - 2) // 2, rows // 2
    span = cols * patch_rows
    hit, lane_col = row_pick(rows, patch_rows, cols)
    total = None
    for j in range(cols):
        left = jnp.concatenate(
            [x_ref[s, 2 * j + c] for s in range(samples) for c in range(4)], axis=0
        )
        pick = jnp.where(hit & (lane_col == j), 1.0, 0.0).astype(bf16)
        part = jnp.dot(left, pick, preferred_element_type=f32)
        total = part if total is None else total + part
    for s in range(samples):
        for c in range(4):
            for g in range(chans // group):
                at = (s * 4 + c) * chans + g * group
                for r in range(4):
                    to = (g * 16 + r * 4 + c) * group
                    o_ref[to : to + group, s * span : (s + 1) * span] = total[
                        at : at + group, r * span : (r + 1) * span
                    ].astype(o_ref.dtype)


def windows(x, group):
    samples, wide, chans, rows = x.shape
    tokens = samples * (wide - 2) * rows // 4
    return call(
        functools.partial(windows_body, group=group),
        jax.ShapeDtypeStruct((16 * chans, tokens), bf16),
        (2 * 16 * chans * tokens * 512, 4 * 16 * chans * tokens, 0),
    )(x)


def fold_rows(g_ref, o_ref, cols, group):
    samples, _, chans, rows = o_ref.shape
    span = cols * rows // 2
    hit, lane_col = row_pick(rows, rows // 2, cols)

    def block(s, c, r):
        parts = []
        for g in range(chans // group):
            at = (g * 16 + r * 4 + c) * group
            parts.append(g_ref[at : at + group, s * span : (s + 1) * span])
        return jnp.concatenate(parts, axis=0)

    left = jnp.concatenate(
        [
            jnp.concatenate([block(s, c, r) for r in range(4)], axis=1)
            for s in range(samples)
            for c in range(4)
        ],
        axis=0,
    )
    held = [[None] * (2 * cols + 2) for _ in range(samples)]
    for j in range(cols):
        pick = jnp.where(hit & (lane_col == j), 1.0, 0.0).astype(bf16)
        part = mm(left, pick, 1, 1)
        for s in range(samples):
            for c in range(4):
                at = (s * 4 + c) * chans
                piece = part[at : at + chans]
                before = held[s][2 * j + c]
                held[s][2 * j + c] = piece if before is None else before + piece
    for s in range(samples):
        for col in range(2 * cols + 2):
            o_ref[s, col] = held[s][col]


def fold_body(g_ref, o_ref, edge_ref, *, cols, group):
    fold_rows(g_ref, o_ref, cols, group)
    edge_ref[0] = o_ref[:, 0].astype(bf16)
    edge_ref[1] = o_ref[:, 2 * cols + 1].astype(bf16)


def fold(g, samples, cols, rows, group):
    chans, tokens = (g.shape[0] // 16, g.shape[1])
    return call(
        functools.partial(fold_body, cols=cols, group=group),
        (
            jax.ShapeDtypeStruct((samples, 2 * cols + 2, chans, rows), f32),
            jax.ShapeDtypeStruct((2, samples, chans, rows), bf16),
        ),
        (2 * 16 * chans * tokens * 512, 4 * 16 * chans * tokens, 0),
    )(g)


def own_lane(rows, lanes, group):
    row = lax.broadcasted_iota(jnp.int32, (rows, lanes), 0)
    lane = lax.broadcasted_iota(jnp.int32, (rows, lanes), 1)
    return row % group == lane % group


def agg_forward_body(win_ref, key_ref, value_ref, mask_ref, probs_ref, pooled_ref):
    groups, heads, group, lanes = probs_ref.shape
    inner = win_ref.shape[0] // groups
    head_dim = pooled_ref.shape[0] // heads
    own = own_lane(heads * group, inner, group)
    own_bias = own_lane(heads * group, group, group)
    spread = lambda x: jnp.broadcast_to(x[:, None, :], (heads, group, x.shape[1])).reshape(
        heads * group, x.shape[1]
    )
    scores = []
    for g in range(groups):
        keys = spread(key_ref[:, g * inner : (g + 1) * inner])
        keys = jnp.where(own, keys, 0.0)
        high = keys.astype(bf16)
        rest = keys - high.astype(f32)
        mid = rest.astype(bf16)
        least = (rest - mid.astype(f32)).astype(bf16)
        here = win_ref[g * inner : (g + 1) * inner, :]
        at = groups * inner + g * group
        bias = jnp.where(own_bias, spread(key_ref[:, at : at + group]), 0.0)
        scores.append(
            jnp.dot(high, here, preferred_element_type=f32)
            + jnp.dot(mid, here, preferred_element_type=f32)
            + jnp.dot(least, here, preferred_element_type=f32)
            + jnp.sum(bias, axis=1, keepdims=True)
        )
    window = inner // group
    win = win_ref[...].astype(f32).reshape(groups, window, group, lanes)
    pair = 128 // head_dim
    present = mask_ref[...].reshape(groups, group, lanes) > 0
    for h in range(heads):
        score = jnp.stack([x[h * group : (h + 1) * group] for x in scores])
        score = jnp.where(present, score, -1e30)
        most = jnp.max(jnp.max(score, axis=0), axis=0, keepdims=True)
        raised = jnp.exp(score - most[None])
        total = jnp.sum(jnp.sum(raised, axis=0), axis=0, keepdims=True)
        probs = raised * (1.0 / total)[None]
        probs_ref[:, h] = probs
        weighted = (win * probs[:, None]).astype(bf16).reshape(groups * inner, lanes)
        weighted = jnp.concatenate(
            [weighted, probs.astype(bf16).reshape(groups * group, lanes)], axis=0
        )
        if h % pair == 0:
            values = value_ref[:, h * head_dim : (h + pair) * head_dim].T
        at = h % pair * head_dim
        pooled_ref[h * head_dim : (h + 1) * head_dim, :] = jnp.dot(
            values[at : at + head_dim], weighted, preferred_element_type=f32
        ).astype(bf16)


def agg_forward(win, key_map_t, value_map, mask, group):
    rows, tokens = win.shape
    heads = key_map_t.shape[0]
    chans = mask.shape[0]
    depth, width = value_map.shape
    return call(
        agg_forward_body,
        (
            jax.ShapeDtypeStruct((chans // group, heads, group, tokens), f32),
            jax.ShapeDtypeStruct((width, tokens), bf16),
        ),
        (2 * tokens * depth * (width + heads * group), 6 * 2**20, heads * chans * tokens),
    )(win, key_map_t, value_map, mask)


def agg_backward_core(
    win_ref, probs_ref, gp_ref, value_ref, key_ref, gwin_ref, gvmt_ref, gkm_ref, gs_ref, acc_ref
):
    groups, heads, group, lanes = probs_ref.shape
    rows = win_ref.shape[0]
    inner = rows // groups
    window = inner // group
    head_dim = gp_ref.shape[0] // heads
    shape = (groups, window, group, lanes)
    win = win_ref[...].astype(f32).reshape(shape)
    for h in range(heads):
        here = slice(h * head_dim, (h + 1) * head_dim)
        gp = gp_ref[here, :]
        probs = probs_ref[:, h]
        gw = jnp.dot(value_ref[:, here], gp, preferred_element_type=f32)
        main = gw[:rows].reshape(shape)
        grad_probs = jnp.sum(main * win, axis=1) + gw[rows:].reshape(groups, group, lanes)
        delta = jnp.sum(jnp.sum(probs * grad_probs, axis=0), axis=0, keepdims=True)
        gs_ref[:, h * group : (h + 1) * group, :] = (probs * (grad_probs - delta[None])).astype(bf16)
        part = (main * probs[:, None]).reshape(rows, lanes)
        if h == 0:
            acc_ref[...] = part
        else:
            acc_ref[...] += part
        weighted = (win * probs[:, None]).astype(bf16).reshape(rows, lanes)
        weighted = jnp.concatenate(
            [weighted, probs.astype(bf16).reshape(groups * group, lanes)], axis=0
        )
        gvmt_ref[here, :] = mm(gp, weighted, 1, 1).astype(bf16)
    own = own_lane(heads * group, inner, group)
    own_bias = own_lane(heads * group, group, group)
    fold_in = lambda x: jnp.sum(x.reshape(heads, group, x.shape[1]), axis=1)
    for g in range(groups):
        here = slice(g * inner, (g + 1) * inner)
        keys = jnp.broadcast_to(key_ref[:, here][:, None, :], (heads, group, inner)).reshape(
            heads * group, inner
        )
        keys = jnp.where(own, keys, 0.0).astype(bf16)
        gs = gs_ref[g]
        gwin_ref[here, :] = (acc_ref[here, :] + mm(keys, gs, 0, 0)).astype(bf16)
        gkm_ref[:, here] = fold_in(jnp.where(own, mm(gs, win_ref[here, :], 1, 1), 0.0))
        total = jnp.sum(gs.astype(f32), axis=1, keepdims=True)
        at = rows + g * group
        gkm_ref[:, at : at + group] = fold_in(jnp.where(own_bias, total, 0.0))


def agg_backward(win, probs, grad_pooled_t, value_map, key_map_t):
    rows, tokens = win.shape
    groups, heads, group, _ = probs.shape
    depth, width = value_map.shape
    return call(
        agg_backward_core,
        (
            jax.ShapeDtypeStruct(win.shape, bf16),
            jax.ShapeDtypeStruct((width, depth), bf16),
            jax.ShapeDtypeStruct((heads, depth), f32),
        ),
        (4 * tokens * depth * (width + heads * group), 8 * 2**20, 0),
        scratch=(
            pltpu.VMEM((groups, heads * group, tokens), bf16),
            pltpu.VMEM((rows, tokens), f32),
        ),
    )(win, probs, grad_pooled_t, value_map, key_map_t)


def one_hot(rows, cols, place, keep=None):
    row = lax.broadcasted_iota(jnp.int32, (rows, cols), 0)
    hit = lax.broadcasted_iota(jnp.int32, (rows, cols), 1) == place(row)
    if keep is not None:
        hit = hit & keep(row)
    return jnp.where(hit, 1.0, 0.0).astype(bf16)


def agg_last_body(
    at_ref,
    win_ref,
    probs_ref,
    gp_ref,
    value_ref,
    key_ref,
    weight_ref,
    agg_value_ref,
    agg_query_ref,
    extra_ref,
    canvas_ref,
    edge_ref,
    mine_ref,
    other_ref,
    gwin_ref,
    gvmt_ref,
    gkm_ref,
    gs_ref,
    acc_ref,
    my_win_ref,
    late_ref,
    *,
    cols,
    parts,
):
    groups, heads, group, lanes = probs_ref.shape
    chans = groups * group
    my_chans = chans // parts
    depth, width = weight_ref.shape
    mine = width // parts
    part, parity = (at_ref[0], at_ref[1])
    agg_backward_core(
        win_ref, probs_ref, gp_ref, value_ref, key_ref, gwin_ref, gvmt_ref, gkm_ref, gs_ref, acc_ref
    )
    spot = lambda var, k: (var // group * 16 + k) * group + var % group
    pick = one_hot(
        16 * group,
        16 * chans,
        lambda row: spot(part * my_chans + row % group, row // group),
        lambda row: row % group < my_chans,
    )
    my_win_ref[...] = jnp.dot(pick, gwin_ref[...], preferred_element_type=f32).astype(bf16)
    fold_rows(my_win_ref, canvas_ref, cols, group)
    edge_ref[0] = canvas_ref[:, 0].astype(bf16)
    edge_ref[1] = canvas_ref[:, 2 * cols + 1].astype(bf16)
    key_low = gkm_ref[...].astype(bf16)
    late_ref[:mine, :] = mm(
        weight_ref[:, pl.ds(pl.multiple_of(part * mine, 128), mine)], gvmt_ref[...], 0, 1
    ).astype(bf16)
    ext_rows = -(-17 * my_chans // 16) * 16

    def ext_place(row):
        main = row < 16 * my_chans
        var = part * my_chans + jnp.where(main, row // 16, row - 16 * my_chans)
        return jnp.where(main, spot(var, row % 16), 16 * chans + var)

    select = one_hot(ext_rows, depth, ext_place, lambda row: row < 17 * my_chans)
    my_value = mm(select, gvmt_ref[...], 1, 1).astype(bf16)
    my_key = mm(select, key_low, 1, 1).astype(bf16)
    late_ref[mine : mine + ext_rows, :] = (
        mm(my_value, agg_value_ref[...], 1, 1)
        + jnp.dot(my_key, agg_query_ref[...], preferred_element_type=f32)
    ).astype(bf16)
    my_heads = heads // parts
    pick = one_hot(
        16, heads, lambda row: part * my_heads + row, lambda row: row < my_heads
    )
    query = jnp.dot(pick, key_low, preferred_element_type=f32).astype(bf16)
    at = mine + ext_rows
    late_ref[at : at + 16, :] = jnp.dot(
        query, weight_ref[...], preferred_element_type=f32
    ).astype(bf16)
    late_ref[at + 16 :, :] = extra_ref[...].astype(bf16)
    split_into(late_ref, parity, at_ref[2], mine_ref, other_ref)


def split_into(whole_ref, parity, line, mine_ref, other_ref):
    block = 128
    for pair in range(mine_ref.shape[1] // block):
        to = slice(pair * block, (pair + 1) * block)
        for target, side in ((mine_ref, parity), (other_ref, 1 - parity)):
            start = pl.multiple_of((2 * jnp.bitwise_xor(pair, line) + side) * block, block)
            target[:, to] = whole_ref[:, pl.ds(start, block)]


def agg_last(
    at, win, probs, grad_pooled_t, value_map, key_map_t, weight, agg_value, agg_query, extra, samples, cols, parts
):
    rows, tokens = win.shape
    groups, heads, group, _ = probs.shape
    depth, width = value_map.shape
    pix_rows = 2 * tokens // (samples * cols)
    count = width // parts + -(-17 * groups * group // parts // 16) * 16 + 32
    half = jax.ShapeDtypeStruct((count, width // 2), bf16)
    return call(
        functools.partial(agg_last_body, cols=cols, parts=parts),
        (
            jax.ShapeDtypeStruct((samples, 2 * cols + 2, group, pix_rows), f32),
            jax.ShapeDtypeStruct((2, samples, group, pix_rows), bf16),
            half,
            half,
        ),
        (6 * tokens * depth * (width + heads * group), 12 * 2**20, 0),
        1,
        9,
        scratch=(
            pltpu.VMEM(win.shape, bf16),
            pltpu.VMEM((width, depth), bf16),
            pltpu.VMEM((heads, depth), f32),
            pltpu.VMEM((groups, heads * group, tokens), bf16),
            pltpu.VMEM((rows, tokens), f32),
            pltpu.VMEM((16 * group, tokens), bf16),
            pltpu.VMEM((count, width), bf16),
        ),
    )(at, win, probs, grad_pooled_t, value_map, key_map_t, weight, agg_value, agg_query, extra)


def attend_body(x_ref, o_ref, lse_ref, key_ref, value_ref, query_ref, *, scale, wide):
    blocks, triple, span = x_ref.shape
    head_dim = triple // 3
    seq = blocks * span
    for n in range(blocks):
        here = slice(n * span, (n + 1) * span)
        query_ref[:, here] = x_ref[n, :head_dim, :] * jnp.asarray(scale, bf16)
        key_ref[here, :] = x_ref[n, head_dim : 2 * head_dim, :].T
        value_ref[:head_dim, here] = x_ref[n, 2 * head_dim :, :]
    value_ref[head_dim:, :] = jnp.ones((8, seq), bf16)
    for w in range(seq // wide):
        scores = jnp.dot(
            key_ref[...], query_ref[:, w * wide : (w + 1) * wide], preferred_element_type=f32
        )
        most = jnp.max(scores, axis=0, keepdims=True)
        raised = jnp.exp(scores - most).astype(bf16)
        both = jnp.dot(value_ref[...], raised, preferred_element_type=f32)
        total = both[head_dim : head_dim + 1]
        out = (both[:head_dim] * (1.0 / total)).astype(bf16)
        lse = most + jnp.log(total)
        for n in range(wide // span):
            here = slice(n * span, (n + 1) * span)
            o_ref[w * (wide // span) + n] = out[:, here]
            lse_ref[w * (wide // span) + n] = lse[:, here]


def attend(x, scale):
    blocks, triple, span = x.shape
    head_dim = triple // 3
    seq = blocks * span
    return call(
        functools.partial(attend_body, scale=scale, wide=max(span, seq // 2)),
        (
            jax.ShapeDtypeStruct((blocks, head_dim, span), bf16),
            jax.ShapeDtypeStruct((blocks, 1, span), f32),
        ),
        (4 * seq * seq * head_dim, 2 * x.size, seq * seq),
        scratch=(
            pltpu.VMEM((seq, head_dim), bf16),
            pltpu.VMEM((head_dim + 8, seq), bf16),
            pltpu.VMEM((head_dim, seq), bf16),
        ),
    )(x)


def attend_back_body(
    x_ref, do_ref, lse_ref, o_ref, key_ref, keyt_ref, value_ref, dkey_ref, dvalue_ref, *, scale
):
    blocks, triple, span = x_ref.shape
    head_dim = triple // 3
    for n in range(blocks):
        here = slice(n * span, (n + 1) * span)
        key_ref[here, :] = x_ref[n, head_dim : 2 * head_dim, :].T
        keyt_ref[:, here] = x_ref[n, head_dim : 2 * head_dim, :]
        value_ref[here, :] = x_ref[n, 2 * head_dim :, :].T
    for n in range(blocks):
        query = x_ref[n, :head_dim, :] * jnp.asarray(scale, bf16)
        grad = do_ref[n]
        scores = jnp.dot(key_ref[...], query, preferred_element_type=f32)
        probs = jnp.exp(scores - lse_ref[n])
        grad_probs = jnp.dot(value_ref[...], grad, preferred_element_type=f32)
        delta = jnp.sum(probs * grad_probs, axis=0, keepdims=True)
        grad_scores = (probs * (grad_probs - delta)).astype(bf16)
        o_ref[n, :head_dim, :] = (
            jnp.dot(keyt_ref[...], grad_scores, preferred_element_type=f32) * scale
        ).astype(bf16)
        dkey = jnp.dot(grad_scores, query.T, preferred_element_type=f32)
        dvalue = jnp.dot(probs.astype(bf16), grad.T, preferred_element_type=f32)
        if n == 0:
            dkey_ref[...] = dkey
            dvalue_ref[...] = dvalue
        else:
            dkey_ref[...] += dkey
            dvalue_ref[...] += dvalue
    for n in range(blocks):
        here = slice(n * span, (n + 1) * span)
        o_ref[n, head_dim : 2 * head_dim, :] = dkey_ref[here, :].T.astype(bf16)
        o_ref[n, 2 * head_dim :, :] = dvalue_ref[here, :].T.astype(bf16)


def attend_back(x, grad, lse, scale):
    blocks, triple, span = x.shape
    head_dim = triple // 3
    seq = blocks * span
    return call(
        functools.partial(attend_back_body, scale=scale),
        jax.ShapeDtypeStruct(x.shape, bf16),
        (10 * seq * seq * head_dim, 4 * x.size, seq * seq),
        scratch=(
            pltpu.VMEM((seq, head_dim), bf16),
            pltpu.VMEM((head_dim, seq), bf16),
            pltpu.VMEM((seq, head_dim), bf16),
            pltpu.VMEM((seq, head_dim), f32),
            pltpu.VMEM((seq, head_dim), f32),
        ),
    )(x, grad, lse)


def stats(x):
    centered = x - jnp.mean(x, axis=-1, keepdims=True)
    inverse = lax.rsqrt(jnp.mean(centered * centered, axis=-1, keepdims=True) + norm_eps)
    return centered * inverse, inverse


def norm_back(grad_out, gain, hat, inverse):
    grad_hat = grad_out * gain
    return inverse * (
        grad_hat
        - jnp.mean(grad_hat, axis=-1, keepdims=True)
        - hat * jnp.mean(grad_hat * hat, axis=-1, keepdims=True)
    )


def halves(core_ref, part_ref, mine_ref, other_ref):
    half = mine_ref.shape[0]
    core = core_ref[0]
    mine_ref[...] = part_ref[pl.ds(pl.multiple_of(core * half, half), half), :].astype(bf16)
    other_ref[...] = part_ref[pl.ds(pl.multiple_of((1 - core) * half, half), half), :].astype(bf16)


def joined(core_ref, mine_ref, other_ref, whole_ref):
    half = mine_ref.shape[0]
    core = core_ref[0]
    whole_ref[pl.ds(pl.multiple_of(core * half, half), half), :] = mine_ref[...].astype(f32)
    whole_ref[pl.ds(pl.multiple_of((1 - core) * half, half), half), :] = other_ref[...].astype(f32)


def enter_body(pooled_ref, out_ref, lead_ref, gain_ref, qkv_ref, start_ref, normed_ref, packed_ref):
    heads, samples, triple, span = packed_ref.shape
    head_dim = triple // 3
    x = jnp.dot(pooled_ref[...].T, out_ref[...], preferred_element_type=f32)
    for s in range(samples):
        here = slice(s * span, (s + 1) * span)
        start = x[here] + lead_ref[s : s + 1, :]
        start_ref[here, :] = start
        normed_ref[here, :] = (stats(start)[0] * gain_ref[...]).astype(bf16)
    for m in range(3):
        got = jnp.dot(normed_ref[...], qkv_ref[m], preferred_element_type=f32).astype(bf16).T
        for h in range(heads):
            for s in range(samples):
                packed_ref[h, s, m * head_dim : (m + 1) * head_dim, :] = got[
                    h * head_dim : (h + 1) * head_dim, s * span : (s + 1) * span
                ]


def enter(pooled_t, agg_out, lead_rows, gain, qkv, heads):
    width, tokens = pooled_t.shape
    samples = lead_rows.shape[0]
    head_dim = qkv.shape[2] // heads
    return call(
        enter_body,
        (
            jax.ShapeDtypeStruct((tokens, width), f32),
            jax.ShapeDtypeStruct((tokens, width), bf16),
            jax.ShapeDtypeStruct((heads, samples, 3 * head_dim, tokens // samples), bf16),
        ),
        (2 * tokens * width * (width + 3 * qkv.shape[2]), 8 * 2**20, 0),
    )(pooled_t, agg_out, lead_rows, gain, qkv)


def leave_body(core_ref, att_ref, weight_ref, att_t_ref, mine_ref, other_ref, part_ref):
    heads, samples, head_dim, span = att_ref.shape
    for s in range(samples):
        here = slice(s * span, (s + 1) * span)
        for h in range(heads):
            att_t_ref[h * head_dim : (h + 1) * head_dim, here] = att_ref[h, s]
    part_ref[...] = jnp.dot(att_t_ref[...].T, weight_ref[...], preferred_element_type=f32)
    halves(core_ref, part_ref, mine_ref, other_ref)


def leave(core, att, weight):
    heads, samples, head_dim, span = att.shape
    tokens, width = (samples * span, weight.shape[1])
    half = jax.ShapeDtypeStruct((tokens // 2, width), bf16)
    return call(
        leave_body,
        (jax.ShapeDtypeStruct((heads * head_dim, tokens), bf16), half, half),
        (2 * tokens * width * heads * head_dim, 3 * 2**20, 0),
        1,
        2,
        scratch=(pltpu.VMEM((tokens, width), f32),),
    )(core, att, weight)


def feed_body(
    core_ref,
    start_ref,
    mine_ref,
    other_ref,
    gain_ref,
    up_ref,
    grad_active_ref,
    mid_ref,
    normed_ref,
    active_ref,
    grad_hidden_ref,
    out_mine_ref,
    out_other_ref,
    part_ref,
):
    joined(core_ref, mine_ref, other_ref, part_ref)
    step = 128
    for at in range(0, start_ref.shape[0], step):
        here = slice(at, at + step)
        mid = start_ref[here, :] + part_ref[here, :]
        mid_ref[here, :] = mid
        normed = (stats(mid)[0] * gain_ref[...]).astype(bf16)
        normed_ref[here, :] = normed
        hidden = jnp.dot(normed, up_ref[...], preferred_element_type=f32)
        both = 0.5 * (1.0 + lax.erf(hidden * sqrt_half))
        active_ref[here, :] = (hidden * both).astype(bf16)
        slope = both + hidden * jnp.exp(-0.5 * hidden * hidden) * inv_root_two_pi
        grad = (grad_active_ref[here, :].astype(f32) * slope).astype(bf16)
        grad_hidden_ref[here, :] = grad
        part_ref[here, :] = mm(grad, up_ref[...], 1, 1)
    halves(core_ref, part_ref, out_mine_ref, out_other_ref)


def feed(core, start, mine, other, gain, up, grad_active):
    tokens, width = start.shape
    low = jax.ShapeDtypeStruct((tokens, width), bf16)
    wide = jax.ShapeDtypeStruct((tokens, up.shape[1]), bf16)
    half = jax.ShapeDtypeStruct(mine.shape, bf16)
    return call(
        feed_body,
        (jax.ShapeDtypeStruct((tokens, width), f32), low, wide, wide, half, half),
        (4 * tokens * width * up.shape[1], 14 * 2**20, 2 * tokens * up.shape[1]),
        1,
        6,
        scratch=(pltpu.VMEM((tokens, width), f32),),
    )(core, start, mine, other, gain, up, grad_active)


def feed_back_body(
    core_ref,
    mid_ref,
    mine_ref,
    other_ref,
    gain_ref,
    grad_end_ref,
    weight_ref,
    grad_mid_ref,
    grad_att_ref,
    grad_gain_ref,
    packed_ref,
    part_ref,
):
    heads, samples, head_dim, span = packed_ref.shape
    joined(core_ref, mine_ref, other_ref, part_ref)
    grad_gain = jnp.zeros(grad_gain_ref.shape, f32)
    step = 128
    for at in range(0, mid_ref.shape[0], step):
        here = slice(at, at + step)
        hat, inverse = stats(mid_ref[here, :])
        grad_out = part_ref[here, :]
        grad_gain += jnp.sum(grad_out * hat, axis=0, keepdims=True)
        grad = grad_end_ref[here, :].astype(f32) + norm_back(grad_out, gain_ref[...], hat, inverse)
        grad_mid_ref[here, :] = grad
        grad_att_ref[here, :] = grad.astype(bf16)
    grad_gain_ref[...] = grad_gain
    got = mm(weight_ref[...], grad_att_ref[...], 1, 1).astype(bf16)
    for h in range(heads):
        for s in range(samples):
            packed_ref[h, s] = got[h * head_dim : (h + 1) * head_dim, s * span : (s + 1) * span]


def feed_back(core, mid, mine, other, gain, grad_end, weight, heads, samples):
    tokens, width = mid.shape
    return call(
        feed_back_body,
        (
            jax.ShapeDtypeStruct((tokens, width), f32),
            jax.ShapeDtypeStruct((tokens, width), bf16),
            jax.ShapeDtypeStruct((1, width), f32),
            jax.ShapeDtypeStruct(
                (heads, samples, weight.shape[0] // heads, tokens // samples), bf16
            ),
        ),
        (2 * tokens * width * weight.shape[0], 9 * 2**20, 0),
        1,
        6,
        scratch=(pltpu.VMEM((tokens, width), f32),),
    )(core, mid, mine, other, gain, grad_end, weight)


def enter_back_body(core_ref, packed_ref, qkv_ref, flat_ref, mine_ref, other_ref, part_ref):
    heads, samples, triple, span = packed_ref.shape
    head_dim = triple // 3
    width = heads * head_dim
    for m in range(3):
        for h in range(heads):
            for s in range(samples):
                to = m * width + h * head_dim
                flat_ref[to : to + head_dim, s * span : (s + 1) * span] = packed_ref[
                    h, s, m * head_dim : (m + 1) * head_dim, :
                ]
    for m in range(3):
        part = mm(flat_ref[m * width : (m + 1) * width, :].T, qkv_ref[m], 1, 1)
        if m == 0:
            part_ref[...] = part
        else:
            part_ref[...] += part
    halves(core_ref, part_ref, mine_ref, other_ref)


def enter_back(core, packed, qkv):
    heads, samples, triple, span = packed.shape
    tokens, width = (samples * span, qkv.shape[1])
    half = jax.ShapeDtypeStruct((tokens // 2, width), bf16)
    return call(
        enter_back_body,
        (jax.ShapeDtypeStruct((heads * triple, tokens), bf16), half, half),
        (2 * tokens * width * heads * triple, 5 * 2**20, 0),
        1,
        2,
        scratch=(pltpu.VMEM((tokens, width), f32),),
    )(core, packed, qkv)


def pool_back_body(
    at_ref,
    start_ref,
    mine_ref,
    other_ref,
    gain_ref,
    grad_mid_ref,
    out_ref,
    my_pooled_ref,
    hot_ref,
    gain_two_ref,
    grad_agg_ref,
    extra_ref,
    pooled_ref,
    out_mine_ref,
    out_other_ref,
    part_ref,
    grad_out_ref,
):
    samples = hot_ref.shape[1]
    tokens, width = start_ref.shape
    joined(at_ref, mine_ref, other_ref, part_ref)
    grad_gain = jnp.zeros((1, width), f32)
    step = min(128, tokens // samples)
    sums = [jnp.zeros((1, width), f32) for _ in range(samples)]
    for at in range(0, tokens, step):
        here = slice(at, at + step)
        hat, inverse = stats(start_ref[here, :])
        grad_out = part_ref[here, :]
        grad_gain += jnp.sum(grad_out * hat, axis=0, keepdims=True)
        grad = grad_mid_ref[here, :] + norm_back(grad_out, gain_ref[...], hat, inverse)
        sums[at * samples // tokens] += jnp.sum(grad, axis=0, keepdims=True)
        grad_agg_ref[here, :] = grad.astype(bf16)
    leads = hot_ref.shape[0]
    row = lax.broadcasted_iota(jnp.int32, (leads, width), 0)
    extra = jnp.where(row == leads - 2, grad_gain, 0.0)
    extra = extra + jnp.where(row == leads - 1, gain_two_ref[...], 0.0)
    for s in range(samples):
        extra = extra + hot_ref[:, s : s + 1] * sums[s]
    extra_ref[...] = extra
    pooled_ref[...] = mm(out_ref[...], grad_agg_ref[...], 1, 1).astype(bf16)
    grad_out_ref[...] = jnp.dot(
        my_pooled_ref[...], grad_agg_ref[...], preferred_element_type=f32
    ).astype(bf16)
    split_into(grad_out_ref, at_ref[1], at_ref[2], out_mine_ref, out_other_ref)


def pool_back(at, start, mine, other, gain, grad_mid, agg_out, my_pooled, hot, gain_two):
    tokens, width = start.shape
    half = jax.ShapeDtypeStruct((my_pooled.shape[0], width // 2), bf16)
    return call(
        pool_back_body,
        (
            jax.ShapeDtypeStruct((tokens, width), bf16),
            jax.ShapeDtypeStruct((hot.shape[0], width), f32),
            jax.ShapeDtypeStruct((width, tokens), bf16),
            half,
            half,
        ),
        (3 * tokens * width * width, 9 * 2**20, 0),
        1,
        9,
        scratch=(
            pltpu.VMEM((tokens, width), f32),
            pltpu.VMEM((my_pooled.shape[0], width), bf16),
        ),
    )(at, start, mine, other, gain, grad_mid, agg_out, my_pooled, hot, gain_two)


def strips_body(place_ref, *refs):
    mine_ref, other_ref = refs[-2:]
    step = pl.program_id(0)
    count = pl.num_programs(0) // 2

    def fill(o_ref):
        at = 0
        for left_ref, right_ref in zip(refs[:-2:2], refs[1:-2:2]):
            dim = 0 if right_ref.shape[0] == left_ref.shape[0] else 1
            wide = right_ref.shape[1 - dim]
            o_ref[:, at : at + wide] = mm(left_ref[...], right_ref[...], 0, dim).astype(bf16)
            at += wide

    @pl.when(step < count)
    def _():
        fill(other_ref)

    @pl.when(step >= count)
    def _():
        fill(mine_ref)


def strips(place, *pairs):
    tokens, width = pairs[0][0].shape
    block = 128
    count = width // block // 2
    wide = sum(right.shape[1 if right.shape[0] == tokens else 0] for _, right in pairs)

    def left_map(i, place_ref):
        own = i // count
        side = place_ref[0] * own + (1 - place_ref[0]) * (1 - own)
        return (0, 2 * jnp.bitwise_xor(i % count, place_ref[1]) + side)

    specs = []
    for left, right in pairs:
        specs.append(pl.BlockSpec((tokens, block), left_map))
        specs.append(pl.BlockSpec(right.shape, lambda i, place_ref: (0, 0)))
    half = jax.ShapeDtypeStruct((width // 2, wide), bf16)
    return pl.pallas_call(
        strips_body,
        out_shape=(half, half),
        grid_spec=pltpu.PrefetchScalarGridSpec(
            num_scalar_prefetch=1,
            grid=(2 * count,),
            in_specs=specs,
            out_specs=(
                pl.BlockSpec((block, wide), lambda i, p: (jnp.maximum(i - count, 0), 0)),
                pl.BlockSpec((block, wide), lambda i, p: (jnp.minimum(i, count - 1), 0)),
            ),
        ),
        compiler_params=pltpu.CompilerParams(vmem_limit_bytes=vmem_most),
        cost_estimate=pl.CostEstimate(
            flops=tokens * width * wide // 4, bytes_accessed=width * wide // 2, transcendentals=0
        ),
    )(place, *[x for pair in pairs for x in pair])


def rows_total(refs, columns=slice(None)):
    total = refs[0][:, columns].astype(f32)
    for ref in refs[1:]:
        total = total + ref[:, columns].astype(f32)
    return total


def finish_body(*refs, parts):
    up, down, mid = [refs[n * parts : (n + 1) * parts] for n in range(3)]
    up_ref, down_ref, out_ref, qkv_ref, head_ref = refs[3 * parts :]
    hidden, local = (up_ref.shape[1], out_ref.shape[0])
    up_ref[...] = rows_total(up, slice(0, hidden))
    out_ref[...] = rows_total(up, slice(hidden, hidden + local)).T
    down_ref[...] = rows_total(down).T
    for m in range(3):
        qkv_ref[m] = rows_total(mid, slice(m * local, (m + 1) * local))
    head_ref[...] = rows_total(mid, slice(3 * local, mid[0].shape[1])).T[: head_ref.shape[0]]


def finish(up, down, mid, local, head_rows):
    block = up[0].shape[0]
    hidden = down[0].shape[1]
    f32s = lambda *shape: jax.ShapeDtypeStruct(shape, f32)
    return call(
        functools.partial(finish_body, parts=len(up)),
        (
            f32s(block, hidden),
            f32s(hidden, block),
            f32s(local, block),
            f32s(3, block, local),
            f32s(head_rows, block),
        ),
        (0, 8 * 2**20, 0),
    )(*up, *down, *mid)


def finish_late_body(*refs, parts, outs):
    agg, late = (refs[:parts], refs[parts : 2 * parts])
    outs = refs[2 * parts :]
    outs[0][...] = rows_total(agg)
    total = rows_total(late)
    value_ref, patch_ref, bias_ref, query_ref, lead_ref, gain_ref = outs[1:]
    at = value_ref.shape[0]
    value_ref[...] = total[:at]
    my_chans = bias_ref.shape[0]
    patch_ref[...] = total[at : at + 16 * my_chans].reshape(patch_ref.shape)
    bias_ref[...] = total[at + 16 * my_chans : at + 17 * my_chans]
    at += -(-17 * my_chans // 16) * 16
    query_ref[...] = total[at : at + query_ref.shape[0]]
    lead_ref[...] = total[at + 16 : at + 16 + lead_ref.shape[0]]
    gain_ref[...] = total[at + 16 + lead_ref.shape[0] :]


def finish_late(agg, late, local, my_chans, my_heads, leads):
    block = agg[0].shape[1]
    f32s = lambda *shape: jax.ShapeDtypeStruct(shape, f32)
    return call(
        functools.partial(finish_late_body, parts=len(agg), outs=7),
        (
            f32s(agg[0].shape[0], block),
            f32s(local, block),
            f32s(my_chans, 16, block),
            f32s(my_chans, block),
            f32s(my_heads, block),
            f32s(leads, block),
            f32s(8, block),
        ),
        (0, 2**20, 0),
    )(*agg, *late)


def close_body(canvas_ref, before_ref, after_ref, o_ref):
    samples, chans, cols, _ = o_ref.shape
    for s in range(samples):
        for col in range(cols):
            piece = canvas_ref[s, col + 1, :chans]
            if col == 0:
                piece = piece + before_ref[s, :chans].astype(f32)
            if col == cols - 1:
                piece = piece + after_ref[s, :chans].astype(f32)
            o_ref[s, :, col, :] = piece


def close_kernel(canvas, rims, chans):
    samples, wide, _, rows = canvas.shape
    return call(
        close_body,
        jax.ShapeDtypeStruct((samples, chans, wide - 2, rows), f32),
        (0, 2**20, 0),
    )(canvas, *rims)


def attend_gathered(packed, scale):
    head_dim = packed.shape[2] // 3
    whole = lax.all_gather(packed[:, :, head_dim:, :], "sector", axis=0)
    keys, values = (whole[:, :, :, :head_dim], whole[:, :, :, head_dim:])
    scores = (
        jnp.einsum("hsdq,nhsdk->hsqnk", packed[:, :, :head_dim], keys, preferred_element_type=f32)
        * scale
    )
    most = jnp.max(scores, axis=(3, 4), keepdims=True)
    raised = jnp.exp(scores - most)
    total = jnp.sum(raised, axis=(3, 4), keepdims=True)
    probs = (raised / total).astype(bf16)
    out = jnp.einsum("hsqnk,nhsdk->hsdq", probs, values, preferred_element_type=f32)
    return out.astype(bf16), most + jnp.log(total)


def attend_back_gathered(packed, grad, lse, scale):
    head_dim = packed.shape[2] // 3
    query = packed[:, :, :head_dim]
    whole = lax.all_gather(packed[:, :, head_dim:, :], "sector", axis=0)
    keys, values = (whole[:, :, :, :head_dim], whole[:, :, :, head_dim:])
    scores = jnp.einsum("hsdq,nhsdk->hsqnk", query, keys, preferred_element_type=f32) * scale
    probs = jnp.exp(scores - lse)
    grad_probs = jnp.einsum("hsdq,nhsdk->hsqnk", grad, values, preferred_element_type=f32)
    delta = jnp.sum(probs * grad_probs, axis=(3, 4), keepdims=True)
    grad_scores = (probs * (grad_probs - delta)).astype(bf16)
    grad_query = jnp.einsum("hsqnk,nhsdk->hsdq", grad_scores, keys, preferred_element_type=f32)
    grad_keys = jnp.einsum("hsqnk,hsdq->nhsdk", grad_scores, query, preferred_element_type=f32)
    grad_values = jnp.einsum(
        "hsqnk,hsdq->nhsdk", probs.astype(bf16), grad, preferred_element_type=f32
    )
    both = lax.psum_scatter(
        jnp.concatenate([grad_keys * scale, grad_values], axis=3), "sector", scatter_dimension=0
    )
    return jnp.concatenate([grad_query * scale, both], axis=2).astype(bf16)


def swap(x, axis, bit):
    size = lax.axis_size(axis)
    return lax.ppermute(x, axis, [(i, i ^ bit) for i in range(size)])


def rounded(x):
    return lax.reduce_precision(x, 8, 7)


def sum_over_mp(x):
    if lax.axis_size("mp") != 4:
        return lax.psum(x.astype(bf16), "mp").astype(f32)
    half = x.shape[0] // 2
    low, high = (rounded(x[:half]), rounded(x[half:]))
    first = lax.axis_index("mp") % 2 == 0
    mine, other = (jnp.where(first, low, high), jnp.where(first, high, low))
    mine = rounded(mine + swap(other.astype(bf16), "mp", 1).astype(f32))
    mine = rounded(mine + swap(mine.astype(bf16), "mp", 2).astype(f32))
    other = swap(mine.astype(bf16), "mp", 1).astype(f32)
    return jnp.concatenate([jnp.where(first, mine, other), jnp.where(first, other, mine)], axis=0)


def near_sum(mine, other):
    return rounded(mine.astype(f32) + swap(other, "mp", 1).astype(f32)).astype(bf16)


def far_sum(mine, got):
    mine = rounded(mine.astype(f32) + got.astype(f32)).astype(bf16)
    return mine, swap(mine, "mp", 1)


def ring_pair(leading, last):
    size = lax.axis_size("sector")
    up = [(i, (i + 1) % size) for i in range(size)]
    down = [(j, i) for i, j in up]
    return lax.ppermute(last, "sector", up), lax.ppermute(leading, "sector", down)


def split_cols(x, block):
    even = lax.axis_index("sector") % 2 == 0
    pairs = x.shape[1] // (2 * block)
    low = [x[:, 2 * p * block : (2 * p + 1) * block] for p in range(pairs)]
    high = [x[:, (2 * p + 1) * block : (2 * p + 2) * block] for p in range(pairs)]
    mine = [jnp.where(even, a, b) for a, b in zip(low, high)]
    other = [jnp.where(even, b, a) for a, b in zip(low, high)]
    return jnp.concatenate(mine, axis=1), jnp.concatenate(other, axis=1)


def pair_sum(mine, got):
    return (mine.astype(f32) + got.astype(f32)).astype(bf16)


def line_parts(pieces):
    return [pieces[0]] + [swap(pieces[n], "sector", 2 * n) for n in range(1, len(pieces))]


def norm_forward(values, gain_vec):
    row_mean = jnp.mean(values, axis=-1, keepdims=True)
    centered = values - row_mean
    inverse = lax.rsqrt(jnp.mean(centered * centered, axis=-1, keepdims=True) + norm_eps)
    normed = centered * inverse
    return (normed * gain_vec, normed, inverse)


def norm_backward(grad_out, gain_vec, normed, inverse):
    grad_normed = grad_out * gain_vec
    grad_gain = jnp.sum(grad_out * normed, axis=0)
    grad_in = inverse * (
        grad_normed
        - jnp.mean(grad_normed, axis=-1, keepdims=True)
        - normed * jnp.mean(grad_normed * normed, axis=-1, keepdims=True)
    )
    return (grad_in, grad_gain)


def gelu_slope(values):
    return (
        0.5 * (1.0 + lax.erf(values * sqrt_half))
        + values * jnp.exp(-0.5 * values * values) * inv_root_two_pi
    )


def mp_slice(values, axis_dim, mp_index, mp_count):
    piece_len = values.shape[axis_dim] // mp_count
    return lax.dynamic_slice_in_dim(values, mp_index * piece_len, piece_len, axis_dim)


def shards(
    input_field,
    present_mask,
    lead_index,
    patch_weight,
    patch_bias,
    agg_query,
    agg_value,
    agg_out,
    lead_table,
    norm1_gain,
    qkv_weight,
    attn_out_weight,
    norm2_gain,
    up_weight,
    down_weight,
    head_weight,
    pred_cotangent,
):
    samples, chans, pix_rows, pix_cols = input_field.shape
    rows, cols = (pix_rows // 2, pix_cols // 2)
    span = rows * cols
    tokens = samples * span
    width = patch_weight.shape[2]
    heads = agg_query.shape[0]
    head_dim = width // heads
    local_width = qkv_weight.shape[2]
    local_heads = local_width // head_dim
    sectors = lax.axis_size("sector")
    mp_count = lax.axis_size("mp")
    mp_index = lax.axis_index("mp")
    score_scale = head_dim ** (-0.5)
    depth = 17 * chans
    group = 16 if chans % 16 == 0 else chans
    groups = chans // group

    by_head = sectors == local_heads * samples
    block = width // sectors
    fast = by_head and block == 128 and sectors == 8 and mp_count == 4 and samples % 2 == 0 and span % 128 == 0
    exchange = lambda x: lax.all_to_all(
        x.reshape(sectors, x.shape[-2], x.shape[-1]), "sector", 0, 0, tiled=True
    )
    by_pair = lambda x: x.reshape(local_heads, samples, x.shape[1], x.shape[2])
    sector = lax.axis_index("sector")
    core = jnp.stack([mp_index % 2, sector % 2, sector // 2])
    whereabouts = core[1:]
    row_parts = lambda x: line_parts([x[n * block : (n + 1) * block] for n in range(sectors // 2)])
    lane_parts = lambda x: line_parts([x[:, n * block : (n + 1) * block] for n in range(sectors // 2)])
    across = lambda x: swap(x, "mp", 2)
    beside = lambda x: swap(x, "sector", 1)
    barrier = lax.optimization_barrier

    fields = jnp.transpose(input_field, (0, 3, 1, 2))
    cots = jnp.transpose(pred_cotangent, (0, 3, 1, 2))
    before, after = ring_pair(
        jnp.stack([fields[:, 0], cots[:, 0]]), jnp.stack([fields[:, -1], cots[:, -1]])
    )
    haloed = lambda x, n: jnp.concatenate([before[n][:, None], x, after[n][:, None]], axis=1)
    win = windows(haloed(fields, 0), group)

    weight_kv = jnp.concatenate(
        [
            jnp.transpose(patch_weight.reshape(groups, group, 16, width), (0, 2, 1, 3)).reshape(
                16 * chans, width
            ),
            patch_bias,
        ],
        axis=0,
    )
    key_map_t = mm(agg_query, weight_kv, 1, 1)
    value_map = jnp.dot(weight_kv, agg_value, preferred_element_type=f32).astype(bf16)
    mask = jnp.broadcast_to(
        jnp.transpose(present_mask)[:, :, None], (chans, samples, span)
    ).reshape(chans, tokens)
    probs, pooled_t = agg_forward(win, key_map_t, value_map, mask, group)
    lead_hot = (lead_index[:, None] == jnp.arange(lead_table.shape[0])[None, :]).astype(f32)
    lead_rows = jnp.dot(lead_hot, lead_table.astype(f32), precision=highest)

    head_cols = head_weight.shape[1]
    spot = lax.broadcasted_iota(jnp.int32, (head_cols, head_cols), 1)
    source = lax.broadcasted_iota(jnp.int32, (head_cols, head_cols), 0)
    place = (spot % (16 * group)) // group
    shuffle = ((spot // (16 * group) * group + spot % group) * 16 + place == source).astype(bf16)
    head_kv = jnp.dot(head_weight, shuffle, preferred_element_type=f32).astype(bf16)
    grad_head_t = windows(haloed(cots, 1), group)
    grad_end = mm(grad_head_t, head_kv, 0, 1)
    grad_mlp = grad_end.astype(bf16)
    grad_active = mm(grad_mlp, down_weight, 1, 1)

    if fast:
        qkv = jnp.transpose(qkv_weight, (1, 0, 2))
        start_x, normed1_low, packed = enter(
            pooled_t, agg_out, lead_rows, norm1_gain[None], qkv, local_heads
        )
        held = exchange(packed)
        held, grad_active, grad_mlp = barrier((held, grad_active.astype(bf16), grad_mlp))
        att_held, lse = attend(held, score_scale)
        att_t, mine, other = leave(core, by_pair(exchange(att_held)), attn_out_weight)
        mine = near_sum(mine, other)
        mid_x, normed2_low, active_low, grad_hidden, mine, other = feed(
            core,
            start_x,
            *far_sum(mine, across(mine)),
            norm2_gain[None],
            up_weight,
            grad_active,
        )
        mine = near_sum(mine, other)
        down_mine, down_other = strips(whereabouts, (grad_mlp, active_low))
        low = jnp.dot(active_low, down_weight, preferred_element_type=f32).astype(bf16)
        first = mp_index % 2 == 0
        low, high = (low[: tokens // 2], low[tokens // 2 :])
        end_mine = near_sum(jnp.where(first, low, high), jnp.where(first, high, low))
        up_mine, up_other = strips(whereabouts, (normed2_low, grad_hidden))
        down_got = beside(down_other)
        got, down_mine, up_mine, end_mine = barrier((across(mine), down_mine, up_mine, end_mine))
        grad_mid, grad_att, grad_gain_two, grad_heads = feed_back(
            core,
            mid_x,
            *far_sum(mine, got),
            norm2_gain[None],
            grad_mlp,
            attn_out_weight,
            local_heads,
            samples,
        )
        out_mine, out_other = strips(whereabouts, (grad_att, att_t))
        down_pair = pair_sum(down_mine, down_got)
        grad_att_held, down_pair, out_mine, out_other, up_other = barrier(
            (exchange(grad_heads), down_pair, out_mine, out_other, up_other)
        )
        down_parts = row_parts(down_pair)
        out_got, up_got = (beside(out_other), beside(up_other))
        grad_held = attend_back(held, grad_att_held, lse, score_scale)
        end_got, out_got, grad_held = barrier((across(end_mine), out_got, grad_held))
        near, far = far_sum(end_mine, end_got)
        end_x = mid_x + jnp.concatenate(
            [jnp.where(first, near, far), jnp.where(first, far, near)], axis=0
        ).astype(f32)
        grad_packed = exchange(grad_held)
    else:
        start_x = (
            mm(pooled_t, agg_out, 0, 0).reshape(samples, span, width) + lead_rows[:, None, :]
        ).reshape(tokens, width)
        normed1, hat_one, inv_one = norm_forward(start_x, norm1_gain)
        normed1_low = normed1.astype(bf16)
        qkv_t = lax.dot_general(
            qkv_weight, normed1_low, (((0,), (1,)), ((), ())), preferred_element_type=f32
        ).astype(bf16)
        packed = jnp.transpose(
            qkv_t.reshape(3, local_heads, head_dim, samples, span), (1, 3, 0, 2, 4)
        ).reshape(local_heads, samples, 3 * head_dim, span)
        att, lse = attend_gathered(packed, score_scale)
        att_t = jnp.transpose(att, (0, 2, 1, 3)).reshape(local_width, tokens)
        mid_x = start_x + sum_over_mp(mm(att_t, attn_out_weight, 0, 0))
        normed2, hat_two, inv_two = norm_forward(mid_x, norm2_gain)
        normed2_low = normed2.astype(bf16)
        hidden = jnp.dot(normed2_low, up_weight, preferred_element_type=f32)
        active_low = jax.nn.gelu(hidden, approximate=False).astype(bf16)
        grad_hidden = (grad_active * gelu_slope(hidden)).astype(bf16)
        grad_normed2 = sum_over_mp(mm(grad_hidden, up_weight, 1, 1))
        grad_mid_norm, grad_gain_two = norm_backward(grad_normed2, norm2_gain, hat_two, inv_two)
        grad_mid = grad_end + grad_mid_norm
        grad_att = grad_mid.astype(bf16)
        grad_heads_t = mm(attn_out_weight, grad_att, 1, 1).astype(bf16)
        grad_heads = jnp.transpose(
            grad_heads_t.reshape(local_heads, head_dim, samples, span), (0, 2, 1, 3)
        )
        grad_packed = attend_back_gathered(packed, grad_heads, lse, score_scale)
        end_x = mid_x + sum_over_mp(jnp.dot(active_low, down_weight, preferred_element_type=f32))

    end_low = end_x.astype(bf16)
    head_out = mm(head_kv, end_low, 0, 1).astype(bf16)
    canvas, edges = fold(head_out, samples, cols, pix_rows, group)

    def close(canvas, rims):
        inner = canvas[:, 1:-1]
        inner = inner.at[:, 0].add(rims[0].astype(f32))
        return jnp.transpose(inner.at[:, -1].add(rims[1].astype(f32)), (0, 2, 3, 1))

    my_chans = chans // mp_count
    my_heads = heads // mp_count
    spots = lambda var, k: (var // group * 16 + k) * group + var % group

    def ext_place(row):
        main = row < 16 * my_chans
        var = mp_index * my_chans + jnp.where(main, row // 16, row - 16 * my_chans)
        return jnp.where(main, spots(var, row % 16), 16 * chans + var)

    head_rows = -(-16 * my_chans // 128) * 128
    my_head = jnp.dot(
        one_hot(head_rows, 16 * chans, ext_place, lambda row: row < 16 * my_chans),
        grad_head_t,
        preferred_element_type=f32,
    ).astype(bf16)
    my_pooled = mp_slice(pooled_t, 0, mp_index, mp_count)
    leads = lead_table.shape[0]

    if fast:
        joint = lambda *x: jnp.concatenate(x, axis=0)
        up_pair = jnp.concatenate([pair_sum(up_mine, up_got), pair_sum(out_mine, out_got)], axis=1)
        grad_packed, edges, up_pair, down_parts = barrier(
            (grad_packed, edges, up_pair, down_parts)
        )
        up_parts = row_parts(up_pair)
        rims = ring_pair(edges[0], edges[1])
        flat, mine, other = enter_back(core, by_pair(grad_packed), qkv)
        mine = near_sum(mine, other)
        mid_mine, mid_other = strips(whereabouts, (normed1_low, flat), (end_low, my_head))
        mid_got = beside(mid_other)
        got, mid_mine = barrier((across(mine), mid_mine))
        hot = jnp.zeros((leads + 8, samples), f32).at[:leads].set(jnp.transpose(lead_hot))
        grad_agg, extra, grad_pooled_t, agg_mine, agg_other = pool_back(
            core,
            start_x,
            *far_sum(mine, got),
            norm1_gain[None],
            grad_mid,
            agg_out,
            my_pooled,
            hot,
            grad_gain_two,
        )
        mid_got, rims, up_parts, grad_pooled_t = barrier((mid_got, rims, up_parts, grad_pooled_t))
        mid_parts = row_parts(pair_sum(mid_mine, mid_got))
        grad_canvas, grad_edges, late_mine, late_other = agg_last(
            jnp.stack([mp_index, sector % 2, sector // 2]),
            win,
            probs,
            grad_pooled_t,
            value_map,
            key_map_t,
            weight_kv,
            agg_value,
            agg_query,
            extra,
            samples,
            cols,
            mp_count,
        )
        grad_rims = ring_pair(grad_edges[0], grad_edges[1])
        late_got, grad_rims, mid_parts = barrier((beside(late_other), grad_rims, mid_parts))
        late_parts = lane_parts(pair_sum(late_mine, late_got))
        agg_parts = lane_parts(pair_sum(agg_mine, beside(agg_other)))
        outs = finish(up_parts, down_parts, mid_parts, local_width, 16 * my_chans)
        prediction = close_kernel(canvas, rims, chans)
        field_grad = close_kernel(grad_canvas, grad_rims, my_chans)
        late_parts, outs, prediction, field_grad, agg_parts = barrier(
            (late_parts, outs, prediction, field_grad, agg_parts)
        )
        up_sum, down_sum, out_sum, qkv_sum, head_sum = outs
        qkv_sum = jnp.transpose(qkv_sum, (1, 0, 2))
        head_sum = jnp.transpose(head_sum)
        prediction, field_grad = [jnp.transpose(x, (0, 1, 3, 2)) for x in (prediction, field_grad)]
        agg_out_sum, value_sum, patch_sum, bias_sum, query_sum, lead_sum, gain_sums = finish_late(
            agg_parts, late_parts, local_width, my_chans, my_heads, leads
        )
        one_sum, two_sum = (gain_sums[6:7], gain_sums[7:8])
    else:
        prediction = close(canvas, ring_pair(edges[0], edges[1]))
        flat = jnp.transpose(
            grad_packed.reshape(local_heads, samples, 3, head_dim, span), (2, 0, 3, 1, 4)
        ).reshape(3 * local_width, tokens)
        grad_normed1 = sum_over_mp(
            lax.dot_general(
                flat.reshape(3, local_width, tokens),
                qkv_weight,
                (((0, 1), (1, 2)), ((), ())),
                preferred_element_type=f32,
            )
        )
        grad_start_norm, grad_gain_one = norm_backward(grad_normed1, norm1_gain, hat_one, inv_one)
        grad_start = grad_mid + grad_start_norm
        grad_agg = grad_start.astype(bf16)
        sample_sums = jnp.sum(grad_start.reshape(samples, span, width), axis=1)
        grad_pooled_t = mm(agg_out, grad_agg, 1, 1).astype(bf16)
        grad_lead = jnp.einsum("sl,sd->ld", lead_hot, sample_sums, precision=highest)
        gains = [x.reshape(1, width) for x in (grad_gain_one, grad_gain_two)]
        grad_win, value_grad_t, key_grad = agg_backward(
            win, probs, grad_pooled_t, value_map, key_map_t
        )
        key_low = key_grad.astype(bf16)
        grad_agg_value = mm(mp_slice(weight_kv, 1, mp_index, mp_count), value_grad_t, 0, 1)
        select = one_hot(17 * my_chans, depth, ext_place)
        my_value = mm(select, value_grad_t, 1, 1).astype(bf16)
        my_key = mm(select, key_low, 1, 1).astype(bf16)
        grad_ext = mm(my_value, agg_value, 1, 1) + jnp.dot(
            my_key, agg_query, preferred_element_type=f32
        )
        grad_agg_query = jnp.dot(
            mp_slice(key_low, 0, mp_index, mp_count), weight_kv, preferred_element_type=f32
        )
        grad_canvas, grad_edges = fold(grad_win, samples, cols, pix_rows, group)
        grad_edges = mp_slice(grad_edges, 2, mp_index, mp_count)
        field_grad = close(
            mp_slice(grad_canvas, 2, mp_index, mp_count), ring_pair(grad_edges[0], grad_edges[1])
        )
        put = lambda x, dim: lax.psum_scatter(x, "sector", scatter_dimension=dim, tiled=True)
        up_sum = put(mm(normed2_low, grad_hidden, 0, 0), 0)
        down_sum = put(mm(active_low, grad_mlp, 0, 0), 1)
        out_sum = put(jnp.dot(att_t, grad_att, preferred_element_type=f32), 1)
        head_sum = put(mm(end_low, my_head[: 16 * my_chans], 0, 1), 0)
        qkv_sum = put(mm(normed1_low, flat, 0, 1), 0).reshape(block, 3, local_width)
        agg_out_sum = put(jnp.dot(my_pooled, grad_agg, preferred_element_type=f32), 1)
        late = [grad_agg_value, grad_ext, grad_agg_query, grad_lead] + gains
        value_sum, ext_sum, query_sum, lead_sum, one_sum, two_sum = [put(x, 1) for x in late]
        patch_sum = ext_sum[: 16 * my_chans].reshape(my_chans, 16, block)
        bias_sum = ext_sum[16 * my_chans :]
    return (
        prediction,
        field_grad,
        patch_sum,
        bias_sum,
        query_sum,
        value_sum,
        agg_out_sum,
        lead_sum,
        one_sum[0],
        qkv_sum,
        out_sum,
        two_sum[0],
        up_sum,
        down_sum,
        head_sum,
    )


def solution(mesh):
    placed = (
        P(None, None, None, "sector"),
        P(),
        P(),
        P(),
        P(),
        P(),
        P(),
        P(),
        P(),
        P(),
        P(None, None, "mp"),
        P("mp", None),
        P(),
        P(None, "mp"),
        P("mp", None),
        P(),
        P(None, None, None, "sector"),
    )
    return jax.shard_map(
        shards,
        mesh=mesh,
        in_specs=placed,
        out_specs=(
            P(None, None, None, "sector"),
            P(None, "mp", None, "sector"),
            P("mp", None, "sector"),
            P("mp", "sector"),
            P("mp", "sector"),
            P("mp", "sector"),
            P("mp", "sector"),
            P(None, "sector"),
            P("sector"),
            P("sector", None, "mp"),
            P("mp", "sector"),
            P("sector"),
            P("sector", "mp"),
            P("mp", "sector"),
            P("sector", "mp"),
        ),
        check_vma=False,
    )
```

```python
import functools

import jax
import jax.numpy as jnp
from jax import lax
from jax.experimental import pallas as pl
from jax.experimental.pallas import tpu as pltpu
from jax.sharding import PartitionSpec as P

bf16 = jnp.bfloat16
f32 = jnp.float32
highest = lax.Precision.HIGHEST
norm_eps = 1e-05
sqrt_half = 0.7071067811865476
inv_root_two_pi = 0.3989422804014327
vmem_most = 32 * 1024 * 1024


def mm(left, right, left_dim, right_dim):
    return lax.dot_general(
        left, right, (((left_dim,), (right_dim,)), ((), ())), preferred_element_type=f32
    )


def call(body, out_shape, cost, scalars=0, tensors=0, scratch=()):
    more = {}
    if scalars:
        more = dict(
            in_specs=[pl.BlockSpec(memory_space=pltpu.SMEM)] * scalars
            + [pl.BlockSpec(memory_space=pltpu.VMEM)] * tensors
        )
    return pl.pallas_call(
        body,
        out_shape=out_shape,
        scratch_shapes=list(scratch),
        compiler_params=pltpu.CompilerParams(vmem_limit_bytes=vmem_most),
        cost_estimate=pl.CostEstimate(
            flops=int(cost[0]) // 64, bytes_accessed=int(cost[1]) // 64, transcendentals=int(cost[2]) // 64
        ),
        **more,
    )


def row_pick(rows, patch_rows, patch_cols):
    span = patch_rows * patch_cols
    lane = lax.broadcasted_iota(jnp.int32, (rows, 4 * span), 1)
    row = lax.broadcasted_iota(jnp.int32, (rows, 4 * span), 0)
    r = lane // span
    rest = lane - r * span
    j = rest // patch_rows
    i = rest - j * patch_rows
    return (row == 2 * i + r - 1), j


def windows_body(x_ref, o_ref, *, group):
    samples, wide, chans, rows = x_ref.shape
    cols, patch_rows = (wide - 2) // 2, rows // 2
    span = cols * patch_rows
    hit, lane_col = row_pick(rows, patch_rows, cols)
    total = None
    for j in range(cols):
        left = jnp.concatenate(
            [x_ref[s, 2 * j + c] for s in range(samples) for c in range(4)], axis=0
        )
        pick = jnp.where(hit & (lane_col == j), 1.0, 0.0).astype(bf16)
        part = jnp.dot(left, pick, preferred_element_type=f32)
        total = part if total is None else total + part
    for s in range(samples):
        for c in range(4):
            for g in range(chans // group):
                at = (s * 4 + c) * chans + g * group
                for r in range(4):
                    to = (g * 16 + r * 4 + c) * group
                    o_ref[to : to + group, s * span : (s + 1) * span] = total[
                        at : at + group, r * span : (r + 1) * span
                    ].astype(o_ref.dtype)


def windows(x, group):
    samples, wide, chans, rows = x.shape
    tokens = samples * (wide - 2) * rows // 4
    return call(
        functools.partial(windows_body, group=group),
        jax.ShapeDtypeStruct((16 * chans, tokens), bf16),
        (2 * 16 * chans * tokens * 512, 4 * 16 * chans * tokens, 0),
    )(x)


def fold_rows(g_ref, o_ref, cols, group):
    samples, _, chans, rows = o_ref.shape
    span = cols * rows // 2
    hit, lane_col = row_pick(rows, rows // 2, cols)

    def block(s, c, r):
        parts = []
        for g in range(chans // group):
            at = (g * 16 + r * 4 + c) * group
            parts.append(g_ref[at : at + group, s * span : (s + 1) * span])
        return jnp.concatenate(parts, axis=0)

    left = jnp.concatenate(
        [
            jnp.concatenate([block(s, c, r) for r in range(4)], axis=1)
            for s in range(samples)
            for c in range(4)
        ],
        axis=0,
    )
    held = [[None] * (2 * cols + 2) for _ in range(samples)]
    for j in range(cols):
        pick = jnp.where(hit & (lane_col == j), 1.0, 0.0).astype(bf16)
        part = mm(left, pick, 1, 1)
        for s in range(samples):
            for c in range(4):
                at = (s * 4 + c) * chans
                piece = part[at : at + chans]
                before = held[s][2 * j + c]
                held[s][2 * j + c] = piece if before is None else before + piece
    for s in range(samples):
        for col in range(2 * cols + 2):
            o_ref[s, col] = held[s][col]


def fold_body(g_ref, o_ref, edge_ref, *, cols, group):
    fold_rows(g_ref, o_ref, cols, group)
    edge_ref[0] = o_ref[:, 0].astype(bf16)
    edge_ref[1] = o_ref[:, 2 * cols + 1].astype(bf16)


def fold(g, samples, cols, rows, group):
    chans, tokens = (g.shape[0] // 16, g.shape[1])
    return call(
        functools.partial(fold_body, cols=cols, group=group),
        (
            jax.ShapeDtypeStruct((samples, 2 * cols + 2, chans, rows), f32),
            jax.ShapeDtypeStruct((2, samples, chans, rows), bf16),
        ),
        (2 * 16 * chans * tokens * 512, 4 * 16 * chans * tokens, 0),
    )(g)


def own_lane(rows, lanes, group):
    row = lax.broadcasted_iota(jnp.int32, (rows, lanes), 0)
    lane = lax.broadcasted_iota(jnp.int32, (rows, lanes), 1)
    return row % group == lane % group


def agg_forward_body(win_ref, key_ref, value_ref, mask_ref, probs_ref, pooled_ref):
    groups, heads, group, lanes = probs_ref.shape
    inner = win_ref.shape[0] // groups
    head_dim = pooled_ref.shape[0] // heads
    own = own_lane(heads * group, inner, group)
    own_bias = own_lane(heads * group, group, group)
    spread = lambda x: jnp.broadcast_to(x[:, None, :], (heads, group, x.shape[1])).reshape(
        heads * group, x.shape[1]
    )
    scores = []
    for g in range(groups):
        keys = spread(key_ref[:, g * inner : (g + 1) * inner])
        keys = jnp.where(own, keys, 0.0)
        high = keys.astype(bf16)
        rest = keys - high.astype(f32)
        mid = rest.astype(bf16)
        least = (rest - mid.astype(f32)).astype(bf16)
        here = win_ref[g * inner : (g + 1) * inner, :]
        at = groups * inner + g * group
        bias = jnp.where(own_bias, spread(key_ref[:, at : at + group]), 0.0)
        scores.append(
            jnp.dot(high, here, preferred_element_type=f32)
            + jnp.dot(mid, here, preferred_element_type=f32)
            + jnp.dot(least, here, preferred_element_type=f32)
            + jnp.sum(bias, axis=1, keepdims=True)
        )
    window = inner // group
    win = win_ref[...].astype(f32).reshape(groups, window, group, lanes)
    pair = 128 // head_dim
    present = mask_ref[...].reshape(groups, group, lanes) > 0
    for h in range(heads):
        score = jnp.stack([x[h * group : (h + 1) * group] for x in scores])
        score = jnp.where(present, score, -1e30)
        most = jnp.max(jnp.max(score, axis=0), axis=0, keepdims=True)
        raised = jnp.exp(score - most[None])
        total = jnp.sum(jnp.sum(raised, axis=0), axis=0, keepdims=True)
        probs = raised * (1.0 / total)[None]
        probs_ref[:, h] = probs
        weighted = (win * probs[:, None]).astype(bf16).reshape(groups * inner, lanes)
        weighted = jnp.concatenate(
            [weighted, probs.astype(bf16).reshape(groups * group, lanes)], axis=0
        )
        if h % pair == 0:
            values = value_ref[:, h * head_dim : (h + pair) * head_dim].T
        at = h % pair * head_dim
        pooled_ref[h * head_dim : (h + 1) * head_dim, :] = jnp.dot(
            values[at : at + head_dim], weighted, preferred_element_type=f32
        ).astype(bf16)


def agg_forward(win, key_map_t, value_map, mask, group):
    rows, tokens = win.shape
    heads = key_map_t.shape[0]
    chans = mask.shape[0]
    depth, width = value_map.shape
    return call(
        agg_forward_body,
        (
            jax.ShapeDtypeStruct((chans // group, heads, group, tokens), f32),
            jax.ShapeDtypeStruct((width, tokens), bf16),
        ),
        (2 * tokens * depth * (width + heads * group), 6 * 2**20, heads * chans * tokens),
    )(win, key_map_t, value_map, mask)


def agg_backward_core(
    win_ref, probs_ref, gp_ref, value_ref, key_ref, gwin_ref, gvmt_ref, gkm_ref, gs_ref, acc_ref
):
    groups, heads, group, lanes = probs_ref.shape
    rows = win_ref.shape[0]
    inner = rows // groups
    window = inner // group
    head_dim = gp_ref.shape[0] // heads
    shape = (groups, window, group, lanes)
    win = win_ref[...].astype(f32).reshape(shape)
    for h in range(heads):
        here = slice(h * head_dim, (h + 1) * head_dim)
        gp = gp_ref[here, :]
        probs = probs_ref[:, h]
        gw = jnp.dot(value_ref[:, here], gp, preferred_element_type=f32)
        main = gw[:rows].reshape(shape)
        grad_probs = jnp.sum(main * win, axis=1) + gw[rows:].reshape(groups, group, lanes)
        delta = jnp.sum(jnp.sum(probs * grad_probs, axis=0), axis=0, keepdims=True)
        gs_ref[:, h * group : (h + 1) * group, :] = (probs * (grad_probs - delta[None])).astype(bf16)
        part = (main * probs[:, None]).reshape(rows, lanes)
        if h == 0:
            acc_ref[...] = part
        else:
            acc_ref[...] += part
        weighted = (win * probs[:, None]).astype(bf16).reshape(rows, lanes)
        weighted = jnp.concatenate(
            [weighted, probs.astype(bf16).reshape(groups * group, lanes)], axis=0
        )
        gvmt_ref[here, :] = mm(gp, weighted, 1, 1).astype(bf16)
    own = own_lane(heads * group, inner, group)
    own_bias = own_lane(heads * group, group, group)
    fold_in = lambda x: jnp.sum(x.reshape(heads, group, x.shape[1]), axis=1)
    for g in range(groups):
        here = slice(g * inner, (g + 1) * inner)
        keys = jnp.broadcast_to(key_ref[:, here][:, None, :], (heads, group, inner)).reshape(
            heads * group, inner
        )
        keys = jnp.where(own, keys, 0.0).astype(bf16)
        gs = gs_ref[g]
        gwin_ref[here, :] = (acc_ref[here, :] + mm(keys, gs, 0, 0)).astype(bf16)
        gkm_ref[:, here] = fold_in(jnp.where(own, mm(gs, win_ref[here, :], 1, 1), 0.0))
        total = jnp.sum(gs.astype(f32), axis=1, keepdims=True)
        at = rows + g * group
        gkm_ref[:, at : at + group] = fold_in(jnp.where(own_bias, total, 0.0))


def agg_backward(win, probs, grad_pooled_t, value_map, key_map_t):
    rows, tokens = win.shape
    groups, heads, group, _ = probs.shape
    depth, width = value_map.shape
    return call(
        agg_backward_core,
        (
            jax.ShapeDtypeStruct(win.shape, bf16),
            jax.ShapeDtypeStruct((width, depth), bf16),
            jax.ShapeDtypeStruct((heads, depth), f32),
        ),
        (4 * tokens * depth * (width + heads * group), 8 * 2**20, 0),
        scratch=(
            pltpu.VMEM((groups, heads * group, tokens), bf16),
            pltpu.VMEM((rows, tokens), f32),
        ),
    )(win, probs, grad_pooled_t, value_map, key_map_t)


def one_hot(rows, cols, place, keep=None):
    row = lax.broadcasted_iota(jnp.int32, (rows, cols), 0)
    hit = lax.broadcasted_iota(jnp.int32, (rows, cols), 1) == place(row)
    if keep is not None:
        hit = hit & keep(row)
    return jnp.where(hit, 1.0, 0.0).astype(bf16)


def agg_last_body(
    at_ref,
    win_ref,
    probs_ref,
    gp_ref,
    value_ref,
    key_ref,
    weight_ref,
    agg_value_ref,
    agg_query_ref,
    extra_ref,
    canvas_ref,
    edge_ref,
    mine_ref,
    other_ref,
    gwin_ref,
    gvmt_ref,
    gkm_ref,
    gs_ref,
    acc_ref,
    my_win_ref,
    late_ref,
    *,
    cols,
    parts,
):
    groups, heads, group, lanes = probs_ref.shape
    chans = groups * group
    my_chans = chans // parts
    depth, width = weight_ref.shape
    mine = width // parts
    part, parity = (at_ref[0], at_ref[1])
    agg_backward_core(
        win_ref, probs_ref, gp_ref, value_ref, key_ref, gwin_ref, gvmt_ref, gkm_ref, gs_ref, acc_ref
    )
    spot = lambda var, k: (var // group * 16 + k) * group + var % group
    pick = one_hot(
        16 * group,
        16 * chans,
        lambda row: spot(part * my_chans + row % group, row // group),
        lambda row: row % group < my_chans,
    )
    my_win_ref[...] = jnp.dot(pick, gwin_ref[...], preferred_element_type=f32).astype(bf16)
    fold_rows(my_win_ref, canvas_ref, cols, group)
    edge_ref[0] = canvas_ref[:, 0].astype(bf16)
    edge_ref[1] = canvas_ref[:, 2 * cols + 1].astype(bf16)
    key_low = gkm_ref[...].astype(bf16)
    late_ref[:mine, :] = mm(
        weight_ref[:, pl.ds(pl.multiple_of(part * mine, 128), mine)], gvmt_ref[...], 0, 1
    ).astype(bf16)
    ext_rows = -(-17 * my_chans // 16) * 16

    def ext_place(row):
        main = row < 16 * my_chans
        var = part * my_chans + jnp.where(main, row // 16, row - 16 * my_chans)
        return jnp.where(main, spot(var, row % 16), 16 * chans + var)

    select = one_hot(ext_rows, depth, ext_place, lambda row: row < 17 * my_chans)
    my_value = mm(select, gvmt_ref[...], 1, 1).astype(bf16)
    my_key = mm(select, key_low, 1, 1).astype(bf16)
    late_ref[mine : mine + ext_rows, :] = (
        mm(my_value, agg_value_ref[...], 1, 1)
        + jnp.dot(my_key, agg_query_ref[...], preferred_element_type=f32)
    ).astype(bf16)
    my_heads = heads // parts
    pick = one_hot(
        16, heads, lambda row: part * my_heads + row, lambda row: row < my_heads
    )
    query = jnp.dot(pick, key_low, preferred_element_type=f32).astype(bf16)
    at = mine + ext_rows
    late_ref[at : at + 16, :] = jnp.dot(
        query, weight_ref[...], preferred_element_type=f32
    ).astype(bf16)
    late_ref[at + 16 :, :] = extra_ref[...].astype(bf16)
    split_into(late_ref, parity, at_ref[2], mine_ref, other_ref)


def split_into(whole_ref, parity, line, mine_ref, other_ref):
    block = 128
    for pair in range(mine_ref.shape[1] // block):
        to = slice(pair * block, (pair + 1) * block)
        for target, side in ((mine_ref, parity), (other_ref, 1 - parity)):
            start = pl.multiple_of((2 * jnp.bitwise_xor(pair, line) + side) * block, block)
            target[:, to] = whole_ref[:, pl.ds(start, block)]


def agg_last(
    at, win, probs, grad_pooled_t, value_map, key_map_t, weight, agg_value, agg_query, extra, samples, cols, parts
):
    rows, tokens = win.shape
    groups, heads, group, _ = probs.shape
    depth, width = value_map.shape
    pix_rows = 2 * tokens // (samples * cols)
    count = width // parts + -(-17 * groups * group // parts // 16) * 16 + 32
    half = jax.ShapeDtypeStruct((count, width // 2), bf16)
    return call(
        functools.partial(agg_last_body, cols=cols, parts=parts),
        (
            jax.ShapeDtypeStruct((samples, 2 * cols + 2, group, pix_rows), f32),
            jax.ShapeDtypeStruct((2, samples, group, pix_rows), bf16),
            half,
            half,
        ),
        (6 * tokens * depth * (width + heads * group), 12 * 2**20, 0),
        1,
        9,
        scratch=(
            pltpu.VMEM(win.shape, bf16),
            pltpu.VMEM((width, depth), bf16),
            pltpu.VMEM((heads, depth), f32),
            pltpu.VMEM((groups, heads * group, tokens), bf16),
            pltpu.VMEM((rows, tokens), f32),
            pltpu.VMEM((16 * group, tokens), bf16),
            pltpu.VMEM((count, width), bf16),
        ),
    )(at, win, probs, grad_pooled_t, value_map, key_map_t, weight, agg_value, agg_query, extra)


def attend_body(x_ref, o_ref, lse_ref, key_ref, value_ref, query_ref, *, scale, wide):
    blocks, triple, span = x_ref.shape
    head_dim = triple // 3
    seq = blocks * span
    for n in range(blocks):
        here = slice(n * span, (n + 1) * span)
        query_ref[:, here] = x_ref[n, :head_dim, :] * jnp.asarray(scale, bf16)
        key_ref[here, :] = x_ref[n, head_dim : 2 * head_dim, :].T
        value_ref[:head_dim, here] = x_ref[n, 2 * head_dim :, :]
    value_ref[head_dim:, :] = jnp.ones((8, seq), bf16)
    for w in range(seq // wide):
        scores = jnp.dot(
            key_ref[...], query_ref[:, w * wide : (w + 1) * wide], preferred_element_type=f32
        )
        most = jnp.max(scores, axis=0, keepdims=True)
        raised = jnp.exp(scores - most).astype(bf16)
        both = jnp.dot(value_ref[...], raised, preferred_element_type=f32)
        total = both[head_dim : head_dim + 1]
        out = (both[:head_dim] * (1.0 / total)).astype(bf16)
        lse = most + jnp.log(total)
        for n in range(wide // span):
            here = slice(n * span, (n + 1) * span)
            o_ref[w * (wide // span) + n] = out[:, here]
            lse_ref[w * (wide // span) + n] = lse[:, here]


def attend(x, scale):
    blocks, triple, span = x.shape
    head_dim = triple // 3
    seq = blocks * span
    return call(
        functools.partial(attend_body, scale=scale, wide=max(span, seq // 2)),
        (
            jax.ShapeDtypeStruct((blocks, head_dim, span), bf16),
            jax.ShapeDtypeStruct((blocks, 1, span), f32),
        ),
        (4 * seq * seq * head_dim, 2 * x.size, seq * seq),
        scratch=(
            pltpu.VMEM((seq, head_dim), bf16),
            pltpu.VMEM((head_dim + 8, seq), bf16),
            pltpu.VMEM((head_dim, seq), bf16),
        ),
    )(x)


def attend_back_body(
    x_ref, do_ref, lse_ref, o_ref, key_ref, keyt_ref, value_ref, dkey_ref, dvalue_ref, *, scale
):
    blocks, triple, span = x_ref.shape
    head_dim = triple // 3
    for n in range(blocks):
        here = slice(n * span, (n + 1) * span)
        key_ref[here, :] = x_ref[n, head_dim : 2 * head_dim, :].T
        keyt_ref[:, here] = x_ref[n, head_dim : 2 * head_dim, :]
        value_ref[here, :] = x_ref[n, 2 * head_dim :, :].T
    for n in range(blocks):
        query = x_ref[n, :head_dim, :] * jnp.asarray(scale, bf16)
        grad = do_ref[n]
        scores = jnp.dot(key_ref[...], query, preferred_element_type=f32)
        probs = jnp.exp(scores - lse_ref[n])
        grad_probs = jnp.dot(value_ref[...], grad, preferred_element_type=f32)
        delta = jnp.sum(probs * grad_probs, axis=0, keepdims=True)
        grad_scores = (probs * (grad_probs - delta)).astype(bf16)
        o_ref[n, :head_dim, :] = (
            jnp.dot(keyt_ref[...], grad_scores, preferred_element_type=f32) * scale
        ).astype(bf16)
        dkey = jnp.dot(grad_scores, query.T, preferred_element_type=f32)
        dvalue = jnp.dot(probs.astype(bf16), grad.T, preferred_element_type=f32)
        if n == 0:
            dkey_ref[...] = dkey
            dvalue_ref[...] = dvalue
        else:
            dkey_ref[...] += dkey
            dvalue_ref[...] += dvalue
    for n in range(blocks):
        here = slice(n * span, (n + 1) * span)
        o_ref[n, head_dim : 2 * head_dim, :] = dkey_ref[here, :].T.astype(bf16)
        o_ref[n, 2 * head_dim :, :] = dvalue_ref[here, :].T.astype(bf16)


def attend_back(x, grad, lse, scale):
    blocks, triple, span = x.shape
    head_dim = triple // 3
    seq = blocks * span
    return call(
        functools.partial(attend_back_body, scale=scale),
        jax.ShapeDtypeStruct(x.shape, bf16),
        (10 * seq * seq * head_dim, 4 * x.size, seq * seq),
        scratch=(
            pltpu.VMEM((seq, head_dim), bf16),
            pltpu.VMEM((head_dim, seq), bf16),
            pltpu.VMEM((seq, head_dim), bf16),
            pltpu.VMEM((seq, head_dim), f32),
            pltpu.VMEM((seq, head_dim), f32),
        ),
    )(x, grad, lse)


def stats(x):
    centered = x - jnp.mean(x, axis=-1, keepdims=True)
    inverse = lax.rsqrt(jnp.mean(centered * centered, axis=-1, keepdims=True) + norm_eps)
    return centered * inverse, inverse


def norm_back(grad_out, gain, hat, inverse):
    grad_hat = grad_out * gain
    return inverse * (
        grad_hat
        - jnp.mean(grad_hat, axis=-1, keepdims=True)
        - hat * jnp.mean(grad_hat * hat, axis=-1, keepdims=True)
    )


def halves(core_ref, part_ref, mine_ref, other_ref):
    half = mine_ref.shape[0]
    core = core_ref[0]
    mine_ref[...] = part_ref[pl.ds(pl.multiple_of(core * half, half), half), :].astype(bf16)
    other_ref[...] = part_ref[pl.ds(pl.multiple_of((1 - core) * half, half), half), :].astype(bf16)


def joined(core_ref, mine_ref, other_ref, whole_ref):
    half = mine_ref.shape[0]
    core = core_ref[0]
    whole_ref[pl.ds(pl.multiple_of(core * half, half), half), :] = mine_ref[...].astype(f32)
    whole_ref[pl.ds(pl.multiple_of((1 - core) * half, half), half), :] = other_ref[...].astype(f32)


def enter_body(pooled_ref, out_ref, lead_ref, gain_ref, qkv_ref, start_ref, normed_ref, packed_ref):
    heads, samples, triple, span = packed_ref.shape
    head_dim = triple // 3
    x = jnp.dot(pooled_ref[...].T, out_ref[...], preferred_element_type=f32)
    for s in range(samples):
        here = slice(s * span, (s + 1) * span)
        start = x[here] + lead_ref[s : s + 1, :]
        start_ref[here, :] = start
        normed_ref[here, :] = (stats(start)[0] * gain_ref[...]).astype(bf16)
    for m in range(3):
        got = jnp.dot(normed_ref[...], qkv_ref[m], preferred_element_type=f32).astype(bf16).T
        for h in range(heads):
            for s in range(samples):
                packed_ref[h, s, m * head_dim : (m + 1) * head_dim, :] = got[
                    h * head_dim : (h + 1) * head_dim, s * span : (s + 1) * span
                ]


def enter(pooled_t, agg_out, lead_rows, gain, qkv, heads):
    width, tokens = pooled_t.shape
    samples = lead_rows.shape[0]
    head_dim = qkv.shape[2] // heads
    return call(
        enter_body,
        (
            jax.ShapeDtypeStruct((tokens, width), f32),
            jax.ShapeDtypeStruct((tokens, width), bf16),
            jax.ShapeDtypeStruct((heads, samples, 3 * head_dim, tokens // samples), bf16),
        ),
        (2 * tokens * width * (width + 3 * qkv.shape[2]), 8 * 2**20, 0),
    )(pooled_t, agg_out, lead_rows, gain, qkv)


def leave_body(core_ref, att_ref, weight_ref, att_t_ref, mine_ref, other_ref, part_ref):
    heads, samples, head_dim, span = att_ref.shape
    for s in range(samples):
        here = slice(s * span, (s + 1) * span)
        for h in range(heads):
            att_t_ref[h * head_dim : (h + 1) * head_dim, here] = att_ref[h, s]
    part_ref[...] = jnp.dot(att_t_ref[...].T, weight_ref[...], preferred_element_type=f32)
    halves(core_ref, part_ref, mine_ref, other_ref)


def leave(core, att, weight):
    heads, samples, head_dim, span = att.shape
    tokens, width = (samples * span, weight.shape[1])
    half = jax.ShapeDtypeStruct((tokens // 2, width), bf16)
    return call(
        leave_body,
        (jax.ShapeDtypeStruct((heads * head_dim, tokens), bf16), half, half),
        (2 * tokens * width * heads * head_dim, 3 * 2**20, 0),
        1,
        2,
        scratch=(pltpu.VMEM((tokens, width), f32),),
    )(core, att, weight)


def feed_body(
    core_ref,
    start_ref,
    mine_ref,
    other_ref,
    gain_ref,
    up_ref,
    grad_active_ref,
    mid_ref,
    normed_ref,
    active_ref,
    grad_hidden_ref,
    out_mine_ref,
    out_other_ref,
    part_ref,
):
    joined(core_ref, mine_ref, other_ref, part_ref)
    step = 128
    for at in range(0, start_ref.shape[0], step):
        here = slice(at, at + step)
        mid = start_ref[here, :] + part_ref[here, :]
        mid_ref[here, :] = mid
        normed = (stats(mid)[0] * gain_ref[...]).astype(bf16)
        normed_ref[here, :] = normed
        hidden = jnp.dot(normed, up_ref[...], preferred_element_type=f32)
        both = 0.5 * (1.0 + lax.erf(hidden * sqrt_half))
        active_ref[here, :] = (hidden * both).astype(bf16)
        slope = both + hidden * jnp.exp(-0.5 * hidden * hidden) * inv_root_two_pi
        grad = (grad_active_ref[here, :].astype(f32) * slope).astype(bf16)
        grad_hidden_ref[here, :] = grad
        part_ref[here, :] = mm(grad, up_ref[...], 1, 1)
    halves(core_ref, part_ref, out_mine_ref, out_other_ref)


def feed(core, start, mine, other, gain, up, grad_active):
    tokens, width = start.shape
    low = jax.ShapeDtypeStruct((tokens, width), bf16)
    wide = jax.ShapeDtypeStruct((tokens, up.shape[1]), bf16)
    half = jax.ShapeDtypeStruct(mine.shape, bf16)
    return call(
        feed_body,
        (jax.ShapeDtypeStruct((tokens, width), f32), low, wide, wide, half, half),
        (4 * tokens * width * up.shape[1], 14 * 2**20, 2 * tokens * up.shape[1]),
        1,
        6,
        scratch=(pltpu.VMEM((tokens, width), f32),),
    )(core, start, mine, other, gain, up, grad_active)


def feed_back_body(
    core_ref,
    mid_ref,
    mine_ref,
    other_ref,
    gain_ref,
    grad_end_ref,
    weight_ref,
    grad_mid_ref,
    grad_att_ref,
    grad_gain_ref,
    packed_ref,
    part_ref,
):
    heads, samples, head_dim, span = packed_ref.shape
    joined(core_ref, mine_ref, other_ref, part_ref)
    grad_gain = jnp.zeros(grad_gain_ref.shape, f32)
    step = 128
    for at in range(0, mid_ref.shape[0], step):
        here = slice(at, at + step)
        hat, inverse = stats(mid_ref[here, :])
        grad_out = part_ref[here, :]
        grad_gain += jnp.sum(grad_out * hat, axis=0, keepdims=True)
        grad = grad_end_ref[here, :].astype(f32) + norm_back(grad_out, gain_ref[...], hat, inverse)
        grad_mid_ref[here, :] = grad
        grad_att_ref[here, :] = grad.astype(bf16)
    grad_gain_ref[...] = grad_gain
    got = mm(weight_ref[...], grad_att_ref[...], 1, 1).astype(bf16)
    for h in range(heads):
        for s in range(samples):
            packed_ref[h, s] = got[h * head_dim : (h + 1) * head_dim, s * span : (s + 1) * span]


def feed_back(core, mid, mine, other, gain, grad_end, weight, heads, samples):
    tokens, width = mid.shape
    return call(
        feed_back_body,
        (
            jax.ShapeDtypeStruct((tokens, width), f32),
            jax.ShapeDtypeStruct((tokens, width), bf16),
            jax.ShapeDtypeStruct((1, width), f32),
            jax.ShapeDtypeStruct(
                (heads, samples, weight.shape[0] // heads, tokens // samples), bf16
            ),
        ),
        (2 * tokens * width * weight.shape[0], 9 * 2**20, 0),
        1,
        6,
        scratch=(pltpu.VMEM((tokens, width), f32),),
    )(core, mid, mine, other, gain, grad_end, weight)


def enter_back_body(core_ref, packed_ref, qkv_ref, flat_ref, mine_ref, other_ref, part_ref):
    heads, samples, triple, span = packed_ref.shape
    head_dim = triple // 3
    width = heads * head_dim
    for m in range(3):
        for h in range(heads):
            for s in range(samples):
                to = m * width + h * head_dim
                flat_ref[to : to + head_dim, s * span : (s + 1) * span] = packed_ref[
                    h, s, m * head_dim : (m + 1) * head_dim, :
                ]
    for m in range(3):
        part = mm(flat_ref[m * width : (m + 1) * width, :].T, qkv_ref[m], 1, 1)
        if m == 0:
            part_ref[...] = part
        else:
            part_ref[...] += part
    halves(core_ref, part_ref, mine_ref, other_ref)


def enter_back(core, packed, qkv):
    heads, samples, triple, span = packed.shape
    tokens, width = (samples * span, qkv.shape[1])
    half = jax.ShapeDtypeStruct((tokens // 2, width), bf16)
    return call(
        enter_back_body,
        (jax.ShapeDtypeStruct((heads * triple, tokens), bf16), half, half),
        (2 * tokens * width * heads * triple, 5 * 2**20, 0),
        1,
        2,
        scratch=(pltpu.VMEM((tokens, width), f32),),
    )(core, packed, qkv)


def pool_back_body(
    at_ref,
    start_ref,
    mine_ref,
    other_ref,
    gain_ref,
    grad_mid_ref,
    out_ref,
    my_pooled_ref,
    hot_ref,
    gain_two_ref,
    grad_agg_ref,
    extra_ref,
    pooled_ref,
    out_mine_ref,
    out_other_ref,
    part_ref,
    grad_out_ref,
):
    samples = hot_ref.shape[1]
    tokens, width = start_ref.shape
    joined(at_ref, mine_ref, other_ref, part_ref)
    grad_gain = jnp.zeros((1, width), f32)
    step = min(128, tokens // samples)
    sums = [jnp.zeros((1, width), f32) for _ in range(samples)]
    for at in range(0, tokens, step):
        here = slice(at, at + step)
        hat, inverse = stats(start_ref[here, :])
        grad_out = part_ref[here, :]
        grad_gain += jnp.sum(grad_out * hat, axis=0, keepdims=True)
        grad = grad_mid_ref[here, :] + norm_back(grad_out, gain_ref[...], hat, inverse)
        sums[at * samples // tokens] += jnp.sum(grad, axis=0, keepdims=True)
        grad_agg_ref[here, :] = grad.astype(bf16)
    leads = hot_ref.shape[0]
    row = lax.broadcasted_iota(jnp.int32, (leads, width), 0)
    extra = jnp.where(row == leads - 2, grad_gain, 0.0)
    extra = extra + jnp.where(row == leads - 1, gain_two_ref[...], 0.0)
    for s in range(samples):
        extra = extra + hot_ref[:, s : s + 1] * sums[s]
    extra_ref[...] = extra
    pooled_ref[...] = mm(out_ref[...], grad_agg_ref[...], 1, 1).astype(bf16)
    grad_out_ref[...] = jnp.dot(
        my_pooled_ref[...], grad_agg_ref[...], preferred_element_type=f32
    ).astype(bf16)
    split_into(grad_out_ref, at_ref[1], at_ref[2], out_mine_ref, out_other_ref)


def pool_back(at, start, mine, other, gain, grad_mid, agg_out, my_pooled, hot, gain_two):
    tokens, width = start.shape
    half = jax.ShapeDtypeStruct((my_pooled.shape[0], width // 2), bf16)
    return call(
        pool_back_body,
        (
            jax.ShapeDtypeStruct((tokens, width), bf16),
            jax.ShapeDtypeStruct((hot.shape[0], width), f32),
            jax.ShapeDtypeStruct((width, tokens), bf16),
            half,
            half,
        ),
        (3 * tokens * width * width, 9 * 2**20, 0),
        1,
        9,
        scratch=(
            pltpu.VMEM((tokens, width), f32),
            pltpu.VMEM((my_pooled.shape[0], width), bf16),
        ),
    )(at, start, mine, other, gain, grad_mid, agg_out, my_pooled, hot, gain_two)


def strips_body(place_ref, *refs, dims):
    mine_ref, other_ref = refs[-2:]
    step = pl.program_id(0)
    count = pl.num_programs(0) // 2

    def fill(o_ref):
        at = 0
        for left_ref, right_ref, dim in zip(refs[:-2:2], refs[1:-2:2], dims):
            wide = right_ref.shape[1 - dim]
            o_ref[:, at : at + wide] = mm(left_ref[...], right_ref[...], 0, dim).astype(bf16)
            at += wide

    @pl.when(step < count)
    def _():
        fill(other_ref)

    @pl.when(step >= count)
    def _():
        fill(mine_ref)


def strips(place, *pairs):
    tokens, width = pairs[0][0].shape
    block = 128
    count = width // block // 2
    wide = sum(right.shape[1 - dim] for _, right, dim in pairs)

    def left_map(i, place_ref):
        own = i // count
        side = place_ref[0] * own + (1 - place_ref[0]) * (1 - own)
        return (0, 2 * jnp.bitwise_xor(i % count, place_ref[1]) + side)

    specs = []
    for left, right, _ in pairs:
        specs.append(pl.BlockSpec((tokens, block), left_map))
        specs.append(pl.BlockSpec(right.shape, lambda i, place_ref: (0, 0)))
    half = jax.ShapeDtypeStruct((width // 2, wide), bf16)
    return pl.pallas_call(
        functools.partial(strips_body, dims=[dim for _, _, dim in pairs]),
        out_shape=(half, half),
        grid_spec=pltpu.PrefetchScalarGridSpec(
            num_scalar_prefetch=1,
            grid=(2 * count,),
            in_specs=specs,
            out_specs=(
                pl.BlockSpec((block, wide), lambda i, p: (jnp.maximum(i - count, 0), 0)),
                pl.BlockSpec((block, wide), lambda i, p: (jnp.minimum(i, count - 1), 0)),
            ),
        ),
        compiler_params=pltpu.CompilerParams(vmem_limit_bytes=vmem_most),
        cost_estimate=pl.CostEstimate(
            flops=tokens * width * wide // 32, bytes_accessed=width * wide // 16, transcendentals=0
        ),
    )(place, *[x for pair in pairs for x in pair[:2]])


def rows_total(refs, columns=slice(None)):
    total = refs[0][:, columns].astype(f32)
    for ref in refs[1:]:
        total = total + ref[:, columns].astype(f32)
    return total


def finish_body(*refs, parts):
    up, down, out, mid, end = [refs[n * parts : (n + 1) * parts] for n in range(5)]
    up_ref, down_ref, out_ref, qkv_ref, head_ref = refs[5 * parts :]
    local = out_ref.shape[0]
    up_ref[...] = rows_total(up)
    out_ref[...] = rows_total(out).T
    down_ref[...] = rows_total(down).T
    for m in range(2):
        qkv_ref[m] = rows_total(mid, slice(m * local, (m + 1) * local))
    qkv_ref[2] = rows_total(end, slice(0, local))
    head_ref[...] = rows_total(end, slice(local, end[0].shape[1])).T[: head_ref.shape[0]]


def finish(groups, local, head_rows):
    up, down = groups[:2]
    block, hidden = up[0].shape
    f32s = lambda *shape: jax.ShapeDtypeStruct(shape, f32)
    return call(
        functools.partial(finish_body, parts=len(up)),
        (
            f32s(block, hidden),
            f32s(hidden, block),
            f32s(local, block),
            f32s(3, block, local),
            f32s(head_rows, block),
        ),
        (0, 8 * 2**20, 0),
    )(*[x for group in groups for x in group])


def finish_late_body(*refs, parts, outs):
    agg, late = (refs[:parts], refs[parts : 2 * parts])
    outs = refs[2 * parts :]
    outs[0][...] = rows_total(agg)
    total = rows_total(late)
    value_ref, patch_ref, bias_ref, query_ref, lead_ref, gain_ref = outs[1:]
    at = value_ref.shape[0]
    value_ref[...] = total[:at]
    my_chans = bias_ref.shape[0]
    patch_ref[...] = total[at : at + 16 * my_chans].reshape(patch_ref.shape)
    bias_ref[...] = total[at + 16 * my_chans : at + 17 * my_chans]
    at += -(-17 * my_chans // 16) * 16
    query_ref[...] = total[at : at + query_ref.shape[0]]
    lead_ref[...] = total[at + 16 : at + 16 + lead_ref.shape[0]]
    gain_ref[...] = total[at + 16 + lead_ref.shape[0] :]


def finish_late(agg, late, local, my_chans, my_heads, leads):
    block = agg[0].shape[1]
    f32s = lambda *shape: jax.ShapeDtypeStruct(shape, f32)
    return call(
        functools.partial(finish_late_body, parts=len(agg), outs=7),
        (
            f32s(agg[0].shape[0], block),
            f32s(local, block),
            f32s(my_chans, 16, block),
            f32s(my_chans, block),
            f32s(my_heads, block),
            f32s(leads, block),
            f32s(8, block),
        ),
        (0, 2**20, 0),
    )(*agg, *late)


def close_body(canvas_ref, before_ref, after_ref, o_ref):
    samples, chans, cols, _ = o_ref.shape
    for s in range(samples):
        for col in range(cols):
            piece = canvas_ref[s, col + 1, :chans]
            if col == 0:
                piece = piece + before_ref[s, :chans].astype(f32)
            if col == cols - 1:
                piece = piece + after_ref[s, :chans].astype(f32)
            o_ref[s, :, col, :] = piece


def close_kernel(canvas, rims, chans):
    samples, wide, _, rows = canvas.shape
    return call(
        close_body,
        jax.ShapeDtypeStruct((samples, chans, wide - 2, rows), f32),
        (0, 2**20, 0),
    )(canvas, *rims)


def attend_gathered(packed, scale):
    head_dim = packed.shape[2] // 3
    whole = lax.all_gather(packed[:, :, head_dim:, :], "sector", axis=0)
    keys, values = (whole[:, :, :, :head_dim], whole[:, :, :, head_dim:])
    scores = (
        jnp.einsum("hsdq,nhsdk->hsqnk", packed[:, :, :head_dim], keys, preferred_element_type=f32)
        * scale
    )
    most = jnp.max(scores, axis=(3, 4), keepdims=True)
    raised = jnp.exp(scores - most)
    total = jnp.sum(raised, axis=(3, 4), keepdims=True)
    probs = (raised / total).astype(bf16)
    out = jnp.einsum("hsqnk,nhsdk->hsdq", probs, values, preferred_element_type=f32)
    return out.astype(bf16), most + jnp.log(total)


def attend_back_gathered(packed, grad, lse, scale):
    head_dim = packed.shape[2] // 3
    query = packed[:, :, :head_dim]
    whole = lax.all_gather(packed[:, :, head_dim:, :], "sector", axis=0)
    keys, values = (whole[:, :, :, :head_dim], whole[:, :, :, head_dim:])
    scores = jnp.einsum("hsdq,nhsdk->hsqnk", query, keys, preferred_element_type=f32) * scale
    probs = jnp.exp(scores - lse)
    grad_probs = jnp.einsum("hsdq,nhsdk->hsqnk", grad, values, preferred_element_type=f32)
    delta = jnp.sum(probs * grad_probs, axis=(3, 4), keepdims=True)
    grad_scores = (probs * (grad_probs - delta)).astype(bf16)
    grad_query = jnp.einsum("hsqnk,nhsdk->hsdq", grad_scores, keys, preferred_element_type=f32)
    grad_keys = jnp.einsum("hsqnk,hsdq->nhsdk", grad_scores, query, preferred_element_type=f32)
    grad_values = jnp.einsum(
        "hsqnk,hsdq->nhsdk", probs.astype(bf16), grad, preferred_element_type=f32
    )
    both = lax.psum_scatter(
        jnp.concatenate([grad_keys * scale, grad_values], axis=3), "sector", scatter_dimension=0
    )
    return jnp.concatenate([grad_query * scale, both], axis=2).astype(bf16)


def swap(x, axis, bit):
    size = lax.axis_size(axis)
    return lax.ppermute(x, axis, [(i, i ^ bit) for i in range(size)])


def rounded(x):
    return lax.reduce_precision(x, 8, 7)


def sum_over_mp(x):
    if lax.axis_size("mp") != 4:
        return lax.psum(x.astype(bf16), "mp").astype(f32)
    half = x.shape[0] // 2
    low, high = (rounded(x[:half]), rounded(x[half:]))
    first = lax.axis_index("mp") % 2 == 0
    mine, other = (jnp.where(first, low, high), jnp.where(first, high, low))
    mine = rounded(mine + swap(other.astype(bf16), "mp", 1).astype(f32))
    mine = rounded(mine + swap(mine.astype(bf16), "mp", 2).astype(f32))
    other = swap(mine.astype(bf16), "mp", 1).astype(f32)
    return jnp.concatenate([jnp.where(first, mine, other), jnp.where(first, other, mine)], axis=0)


def near_sum(mine, other):
    return rounded(mine.astype(f32) + swap(other, "mp", 1).astype(f32)).astype(bf16)


def far_sum(mine, got):
    mine = rounded(mine.astype(f32) + got.astype(f32)).astype(bf16)
    return mine, swap(mine, "mp", 1)


def ring_pair(leading, last):
    size = lax.axis_size("sector")
    up = [(i, (i + 1) % size) for i in range(size)]
    down = [(j, i) for i, j in up]
    return lax.ppermute(last, "sector", up), lax.ppermute(leading, "sector", down)


def split_cols(x, block):
    even = lax.axis_index("sector") % 2 == 0
    pairs = x.shape[1] // (2 * block)
    low = [x[:, 2 * p * block : (2 * p + 1) * block] for p in range(pairs)]
    high = [x[:, (2 * p + 1) * block : (2 * p + 2) * block] for p in range(pairs)]
    mine = [jnp.where(even, a, b) for a, b in zip(low, high)]
    other = [jnp.where(even, b, a) for a, b in zip(low, high)]
    return jnp.concatenate(mine, axis=1), jnp.concatenate(other, axis=1)


def pair_sum(mine, got):
    return (mine.astype(f32) + got.astype(f32)).astype(bf16)


def line_parts(pieces):
    return [pieces[0]] + [swap(pieces[n], "sector", 2 * n) for n in range(1, len(pieces))]


def norm_forward(values, gain_vec):
    row_mean = jnp.mean(values, axis=-1, keepdims=True)
    centered = values - row_mean
    inverse = lax.rsqrt(jnp.mean(centered * centered, axis=-1, keepdims=True) + norm_eps)
    normed = centered * inverse
    return (normed * gain_vec, normed, inverse)


def norm_backward(grad_out, gain_vec, normed, inverse):
    grad_normed = grad_out * gain_vec
    grad_gain = jnp.sum(grad_out * normed, axis=0)
    grad_in = inverse * (
        grad_normed
        - jnp.mean(grad_normed, axis=-1, keepdims=True)
        - normed * jnp.mean(grad_normed * normed, axis=-1, keepdims=True)
    )
    return (grad_in, grad_gain)


def gelu_slope(values):
    return (
        0.5 * (1.0 + lax.erf(values * sqrt_half))
        + values * jnp.exp(-0.5 * values * values) * inv_root_two_pi
    )


def mp_slice(values, axis_dim, mp_index, mp_count):
    piece_len = values.shape[axis_dim] // mp_count
    return lax.dynamic_slice_in_dim(values, mp_index * piece_len, piece_len, axis_dim)


def shards(
    input_field,
    present_mask,
    lead_index,
    patch_weight,
    patch_bias,
    agg_query,
    agg_value,
    agg_out,
    lead_table,
    norm1_gain,
    qkv_weight,
    attn_out_weight,
    norm2_gain,
    up_weight,
    down_weight,
    head_weight,
    pred_cotangent,
):
    samples, chans, pix_rows, pix_cols = input_field.shape
    rows, cols = (pix_rows // 2, pix_cols // 2)
    span = rows * cols
    tokens = samples * span
    width = patch_weight.shape[2]
    heads = agg_query.shape[0]
    head_dim = width // heads
    local_width = qkv_weight.shape[2]
    local_heads = local_width // head_dim
    sectors = lax.axis_size("sector")
    mp_count = lax.axis_size("mp")
    mp_index = lax.axis_index("mp")
    score_scale = head_dim ** (-0.5)
    depth = 17 * chans
    group = 16 if chans % 16 == 0 else chans
    groups = chans // group

    by_head = sectors == local_heads * samples
    block = width // sectors
    fast = by_head and block == 128 and sectors == 8 and mp_count == 4 and samples % 2 == 0 and span % 128 == 0
    exchange = lambda x: lax.all_to_all(
        x.reshape(sectors, x.shape[-2], x.shape[-1]), "sector", 0, 0, tiled=True
    )
    by_pair = lambda x: x.reshape(local_heads, samples, x.shape[1], x.shape[2])
    sector = lax.axis_index("sector")
    core = jnp.stack([mp_index % 2, sector % 2, sector // 2])
    whereabouts = core[1:]
    row_parts = lambda x: line_parts([x[n * block : (n + 1) * block] for n in range(sectors // 2)])
    lane_parts = lambda x: line_parts([x[:, n * block : (n + 1) * block] for n in range(sectors // 2)])
    across = lambda x: swap(x, "mp", 2)
    beside = lambda x: swap(x, "sector", 1)
    barrier = lax.optimization_barrier

    fields = jnp.transpose(input_field, (0, 3, 1, 2))
    cots = jnp.transpose(pred_cotangent, (0, 3, 1, 2))
    before, after = ring_pair(
        jnp.stack([fields[:, 0], cots[:, 0]]), jnp.stack([fields[:, -1], cots[:, -1]])
    )
    haloed = lambda x, n: jnp.concatenate([before[n][:, None], x, after[n][:, None]], axis=1)
    win = windows(haloed(fields, 0), group)

    weight_kv = jnp.concatenate(
        [
            jnp.transpose(patch_weight.reshape(groups, group, 16, width), (0, 2, 1, 3)).reshape(
                16 * chans, width
            ),
            patch_bias,
        ],
        axis=0,
    )
    key_map_t = mm(agg_query, weight_kv, 1, 1)
    value_map = jnp.dot(weight_kv, agg_value, preferred_element_type=f32).astype(bf16)
    mask = jnp.broadcast_to(
        jnp.transpose(present_mask)[:, :, None], (chans, samples, span)
    ).reshape(chans, tokens)
    probs, pooled_t = agg_forward(win, key_map_t, value_map, mask, group)
    lead_hot = (lead_index[:, None] == jnp.arange(lead_table.shape[0])[None, :]).astype(f32)
    lead_rows = jnp.dot(lead_hot, lead_table.astype(f32), precision=highest)

    head_cols = head_weight.shape[1]
    spot = lax.broadcasted_iota(jnp.int32, (head_cols, head_cols), 1)
    source = lax.broadcasted_iota(jnp.int32, (head_cols, head_cols), 0)
    place = (spot % (16 * group)) // group
    shuffle = ((spot // (16 * group) * group + spot % group) * 16 + place == source).astype(bf16)
    head_kv = jnp.dot(head_weight, shuffle, preferred_element_type=f32).astype(bf16)
    grad_head_t = windows(haloed(cots, 1), group)
    grad_end = mm(grad_head_t, head_kv, 0, 1)
    grad_mlp = grad_end.astype(bf16)
    grad_active = mm(grad_mlp, down_weight, 1, 1)

    if fast:
        qkv = jnp.transpose(qkv_weight, (1, 0, 2))
        start_x, normed1_low, packed = enter(
            pooled_t, agg_out, lead_rows, norm1_gain[None], qkv, local_heads
        )
        held = exchange(packed)
        held, grad_active, grad_mlp = barrier((held, grad_active.astype(bf16), grad_mlp))
        att_held, lse = attend(held, score_scale)
        att_t, mine, other = leave(core, by_pair(exchange(att_held)), attn_out_weight)
        mine = near_sum(mine, other)
        mid_x, normed2_low, active_low, grad_hidden, mine, other = feed(
            core,
            start_x,
            *far_sum(mine, across(mine)),
            norm2_gain[None],
            up_weight,
            grad_active,
        )
        mine = near_sum(mine, other)
        down_mine, down_other = strips(whereabouts, (grad_mlp, active_low, 0))
        low = jnp.dot(active_low, down_weight, preferred_element_type=f32).astype(bf16)
        first = mp_index % 2 == 0
        low, high = (low[: tokens // 2], low[tokens // 2 :])
        end_mine = near_sum(jnp.where(first, low, high), jnp.where(first, high, low))
        up_mine, up_other = strips(whereabouts, (normed2_low, grad_hidden, 0))
        down_got = beside(down_other)
        got, down_mine, up_mine, end_mine = barrier((across(mine), down_mine, up_mine, end_mine))
        grad_mid, grad_att, grad_gain_two, grad_heads = feed_back(
            core,
            mid_x,
            *far_sum(mine, got),
            norm2_gain[None],
            grad_mlp,
            attn_out_weight,
            local_heads,
            samples,
        )
        down_pair = pair_sum(down_mine, down_got)
        grad_att_held, down_pair, up_other = barrier(
            (exchange(grad_heads), down_pair, up_other)
        )
        down_parts = row_parts(down_pair)
        up_got = beside(up_other)
        grad_held = attend_back(held, grad_att_held, lse, score_scale)
        end_got, down_parts, up_got, grad_att, grad_held = barrier(
            (across(end_mine), down_parts, up_got, grad_att, grad_held)
        )
        out_mine, out_other = strips(whereabouts, (grad_att, att_t, 1))
        out_got = beside(out_other)
        near, far = far_sum(end_mine, end_got)
        end_x = mid_x + jnp.concatenate(
            [jnp.where(first, near, far), jnp.where(first, far, near)], axis=0
        ).astype(f32)
        grad_packed = exchange(grad_held)
    else:
        start_x = (
            mm(pooled_t, agg_out, 0, 0).reshape(samples, span, width) + lead_rows[:, None, :]
        ).reshape(tokens, width)
        normed1, hat_one, inv_one = norm_forward(start_x, norm1_gain)
        normed1_low = normed1.astype(bf16)
        qkv_t = lax.dot_general(
            qkv_weight, normed1_low, (((0,), (1,)), ((), ())), preferred_element_type=f32
        ).astype(bf16)
        packed = jnp.transpose(
            qkv_t.reshape(3, local_heads, head_dim, samples, span), (1, 3, 0, 2, 4)
        ).reshape(local_heads, samples, 3 * head_dim, span)
        att, lse = attend_gathered(packed, score_scale)
        att_t = jnp.transpose(att, (0, 2, 1, 3)).reshape(local_width, tokens)
        mid_x = start_x + sum_over_mp(mm(att_t, attn_out_weight, 0, 0))
        normed2, hat_two, inv_two = norm_forward(mid_x, norm2_gain)
        normed2_low = normed2.astype(bf16)
        hidden = jnp.dot(normed2_low, up_weight, preferred_element_type=f32)
        active_low = jax.nn.gelu(hidden, approximate=False).astype(bf16)
        grad_hidden = (grad_active * gelu_slope(hidden)).astype(bf16)
        grad_normed2 = sum_over_mp(mm(grad_hidden, up_weight, 1, 1))
        grad_mid_norm, grad_gain_two = norm_backward(grad_normed2, norm2_gain, hat_two, inv_two)
        grad_mid = grad_end + grad_mid_norm
        grad_att = grad_mid.astype(bf16)
        grad_heads_t = mm(attn_out_weight, grad_att, 1, 1).astype(bf16)
        grad_heads = jnp.transpose(
            grad_heads_t.reshape(local_heads, head_dim, samples, span), (0, 2, 1, 3)
        )
        grad_packed = attend_back_gathered(packed, grad_heads, lse, score_scale)
        end_x = mid_x + sum_over_mp(jnp.dot(active_low, down_weight, preferred_element_type=f32))

    end_low = end_x.astype(bf16)
    head_out = mm(head_kv, end_low, 0, 1).astype(bf16)
    canvas, edges = fold(head_out, samples, cols, pix_rows, group)

    def close(canvas, rims):
        inner = canvas[:, 1:-1]
        inner = inner.at[:, 0].add(rims[0].astype(f32))
        return jnp.transpose(inner.at[:, -1].add(rims[1].astype(f32)), (0, 2, 3, 1))

    my_chans = chans // mp_count
    my_heads = heads // mp_count
    spots = lambda var, k: (var // group * 16 + k) * group + var % group

    def ext_place(row):
        main = row < 16 * my_chans
        var = mp_index * my_chans + jnp.where(main, row // 16, row - 16 * my_chans)
        return jnp.where(main, spots(var, row % 16), 16 * chans + var)

    head_rows = -(-16 * my_chans // 128) * 128
    my_head = jnp.dot(
        one_hot(head_rows, 16 * chans, ext_place, lambda row: row < 16 * my_chans),
        grad_head_t,
        preferred_element_type=f32,
    ).astype(bf16)
    my_pooled = mp_slice(pooled_t, 0, mp_index, mp_count)
    leads = lead_table.shape[0]

    if fast:
        joint = lambda *x: jnp.concatenate(x, axis=0)
        up_parts = row_parts(pair_sum(up_mine, up_got))
        rims = ring_pair(edges[0], edges[1])
        grad_packed, rims, out_got = barrier((grad_packed, rims, out_got))
        out_parts = row_parts(pair_sum(out_mine, out_got))
        flat, mine, other = enter_back(core, by_pair(grad_packed), qkv)
        mine = near_sum(mine, other)
        part = 2 * local_width
        mid_mine, mid_other = strips(whereabouts, (normed1_low, flat[:part], 1))
        mid_got = beside(mid_other)
        end_mine, end_other = strips(
            whereabouts, (normed1_low, flat[part:], 1), (end_low, my_head, 1)
        )
        end_got = beside(end_other)
        got, mid_mine, end_mine, up_parts = barrier((across(mine), mid_mine, end_mine, up_parts))
        hot = jnp.zeros((leads + 8, samples), f32).at[:leads].set(jnp.transpose(lead_hot))
        grad_agg, extra, grad_pooled_t, agg_mine, agg_other = pool_back(
            core,
            start_x,
            *far_sum(mine, got),
            norm1_gain[None],
            grad_mid,
            agg_out,
            my_pooled,
            hot,
            grad_gain_two,
        )
        mid_got, out_parts, grad_pooled_t = barrier((mid_got, out_parts, grad_pooled_t))
        mid_parts = row_parts(pair_sum(mid_mine, mid_got))
        grad_canvas, grad_edges, late_mine, late_other = agg_last(
            jnp.stack([mp_index, sector % 2, sector // 2]),
            win,
            probs,
            grad_pooled_t,
            value_map,
            key_map_t,
            weight_kv,
            agg_value,
            agg_query,
            extra,
            samples,
            cols,
            mp_count,
        )
        late_other, grad_edges, mid_parts, end_got = barrier(
            (late_other, grad_edges, mid_parts, end_got)
        )
        end_parts = row_parts(pair_sum(end_mine, end_got))
        grad_rims = ring_pair(grad_edges[0], grad_edges[1])
        late_got, grad_rims = barrier((beside(late_other), grad_rims))
        late_parts = lane_parts(pair_sum(late_mine, late_got))
        agg_parts = lane_parts(pair_sum(agg_mine, beside(agg_other)))
        outs = finish(
            (up_parts, down_parts, out_parts, mid_parts, end_parts), local_width, 16 * my_chans
        )
        prediction = close_kernel(canvas, rims, chans)
        field_grad = close_kernel(grad_canvas, grad_rims, my_chans)
        late_parts, outs, prediction, field_grad, agg_parts = barrier(
            (late_parts, outs, prediction, field_grad, agg_parts)
        )
        up_sum, down_sum, out_sum, qkv_sum, head_sum = outs
        qkv_sum = jnp.transpose(qkv_sum, (1, 0, 2))
        head_sum = jnp.transpose(head_sum)
        prediction, field_grad = [jnp.transpose(x, (0, 1, 3, 2)) for x in (prediction, field_grad)]
        agg_out_sum, value_sum, patch_sum, bias_sum, query_sum, lead_sum, gain_sums = finish_late(
            agg_parts, late_parts, local_width, my_chans, my_heads, leads
        )
        one_sum, two_sum = (gain_sums[6:7], gain_sums[7:8])
    else:
        prediction = close(canvas, ring_pair(edges[0], edges[1]))
        flat = jnp.transpose(
            grad_packed.reshape(local_heads, samples, 3, head_dim, span), (2, 0, 3, 1, 4)
        ).reshape(3 * local_width, tokens)
        grad_normed1 = sum_over_mp(
            lax.dot_general(
                flat.reshape(3, local_width, tokens),
                qkv_weight,
                (((0, 1), (1, 2)), ((), ())),
                preferred_element_type=f32,
            )
        )
        grad_start_norm, grad_gain_one = norm_backward(grad_normed1, norm1_gain, hat_one, inv_one)
        grad_start = grad_mid + grad_start_norm
        grad_agg = grad_start.astype(bf16)
        sample_sums = jnp.sum(grad_start.reshape(samples, span, width), axis=1)
        grad_pooled_t = mm(agg_out, grad_agg, 1, 1).astype(bf16)
        grad_lead = jnp.einsum("sl,sd->ld", lead_hot, sample_sums, precision=highest)
        gains = [x.reshape(1, width) for x in (grad_gain_one, grad_gain_two)]
        grad_win, value_grad_t, key_grad = agg_backward(
            win, probs, grad_pooled_t, value_map, key_map_t
        )
        key_low = key_grad.astype(bf16)
        grad_agg_value = mm(mp_slice(weight_kv, 1, mp_index, mp_count), value_grad_t, 0, 1)
        select = one_hot(17 * my_chans, depth, ext_place)
        my_value = mm(select, value_grad_t, 1, 1).astype(bf16)
        my_key = mm(select, key_low, 1, 1).astype(bf16)
        grad_ext = mm(my_value, agg_value, 1, 1) + jnp.dot(
            my_key, agg_query, preferred_element_type=f32
        )
        grad_agg_query = jnp.dot(
            mp_slice(key_low, 0, mp_index, mp_count), weight_kv, preferred_element_type=f32
        )
        grad_canvas, grad_edges = fold(grad_win, samples, cols, pix_rows, group)
        grad_edges = mp_slice(grad_edges, 2, mp_index, mp_count)
        field_grad = close(
            mp_slice(grad_canvas, 2, mp_index, mp_count), ring_pair(grad_edges[0], grad_edges[1])
        )
        put = lambda x, dim: lax.psum_scatter(x, "sector", scatter_dimension=dim, tiled=True)
        up_sum = put(mm(normed2_low, grad_hidden, 0, 0), 0)
        down_sum = put(mm(active_low, grad_mlp, 0, 0), 1)
        out_sum = put(jnp.dot(att_t, grad_att, preferred_element_type=f32), 1)
        head_sum = put(mm(end_low, my_head[: 16 * my_chans], 0, 1), 0)
        qkv_sum = put(mm(normed1_low, flat, 0, 1), 0).reshape(block, 3, local_width)
        agg_out_sum = put(jnp.dot(my_pooled, grad_agg, preferred_element_type=f32), 1)
        late = [grad_agg_value, grad_ext, grad_agg_query, grad_lead] + gains
        value_sum, ext_sum, query_sum, lead_sum, one_sum, two_sum = [put(x, 1) for x in late]
        patch_sum = ext_sum[: 16 * my_chans].reshape(my_chans, 16, block)
        bias_sum = ext_sum[16 * my_chans :]
    return (
        prediction,
        field_grad,
        patch_sum,
        bias_sum,
        query_sum,
        value_sum,
        agg_out_sum,
        lead_sum,
        one_sum[0],
        qkv_sum,
        out_sum,
        two_sum[0],
        up_sum,
        down_sum,
        head_sum,
    )


def solution(mesh):
    placed = (
        P(None, None, None, "sector"),
        P(),
        P(),
        P(),
        P(),
        P(),
        P(),
        P(),
        P(),
        P(),
        P(None, None, "mp"),
        P("mp", None),
        P(),
        P(None, "mp"),
        P("mp", None),
        P(),
        P(None, None, None, "sector"),
    )
    return jax.shard_map(
        shards,
        mesh=mesh,
        in_specs=placed,
        out_specs=(
            P(None, None, None, "sector"),
            P(None, "mp", None, "sector"),
            P("mp", None, "sector"),
            P("mp", "sector"),
            P("mp", "sector"),
            P("mp", "sector"),
            P("mp", "sector"),
            P(None, "sector"),
            P("sector"),
            P("sector", None, "mp"),
            P("mp", "sector"),
            P("sector"),
            P("sector", "mp"),
            P("mp", "sector"),
            P("sector", "mp"),
        ),
        check_vma=False,
    )
```

```python
import functools

import jax
import jax.numpy as jnp
from jax import lax
from jax.experimental import pallas as pl
from jax.experimental.pallas import tpu as pltpu
from jax.sharding import PartitionSpec as P

bf16 = jnp.bfloat16
f32 = jnp.float32
highest = lax.Precision.HIGHEST
norm_eps = 1e-05
sqrt_half = 0.7071067811865476
inv_root_two_pi = 0.3989422804014327
vmem_most = 32 * 1024 * 1024


def mm(left, right, left_dim, right_dim):
    return lax.dot_general(
        left, right, (((left_dim,), (right_dim,)), ((), ())), preferred_element_type=f32
    )


def call(body, out_shape, cost, scalars=0, tensors=0, scratch=()):
    more = {}
    if scalars:
        more = dict(
            in_specs=[pl.BlockSpec(memory_space=pltpu.SMEM)] * scalars
            + [pl.BlockSpec(memory_space=pltpu.VMEM)] * tensors
        )
    return pl.pallas_call(
        body,
        out_shape=out_shape,
        scratch_shapes=list(scratch),
        compiler_params=pltpu.CompilerParams(vmem_limit_bytes=vmem_most),
        cost_estimate=pl.CostEstimate(
            flops=int(cost[0]) // 64, bytes_accessed=int(cost[1]) // 64, transcendentals=int(cost[2]) // 64
        ),
        **more,
    )


def row_pick(rows, patch_rows, patch_cols):
    span = patch_rows * patch_cols
    lane = lax.broadcasted_iota(jnp.int32, (rows, 4 * span), 1)
    row = lax.broadcasted_iota(jnp.int32, (rows, 4 * span), 0)
    r = lane // span
    rest = lane - r * span
    j = rest // patch_rows
    i = rest - j * patch_rows
    return (row == 2 * i + r - 1), j


def windows_body(x_ref, o_ref, *, group):
    samples, wide, chans, rows = x_ref.shape
    cols, patch_rows = (wide - 2) // 2, rows // 2
    span = cols * patch_rows
    hit, lane_col = row_pick(rows, patch_rows, cols)
    total = None
    for j in range(cols):
        left = jnp.concatenate(
            [x_ref[s, 2 * j + c] for s in range(samples) for c in range(4)], axis=0
        )
        pick = jnp.where(hit & (lane_col == j), 1.0, 0.0).astype(bf16)
        part = jnp.dot(left, pick, preferred_element_type=f32)
        total = part if total is None else total + part
    for s in range(samples):
        for c in range(4):
            for g in range(chans // group):
                at = (s * 4 + c) * chans + g * group
                for r in range(4):
                    to = (g * 16 + r * 4 + c) * group
                    o_ref[to : to + group, s * span : (s + 1) * span] = total[
                        at : at + group, r * span : (r + 1) * span
                    ].astype(o_ref.dtype)


def windows(x, group):
    samples, wide, chans, rows = x.shape
    tokens = samples * (wide - 2) * rows // 4
    return call(
        functools.partial(windows_body, group=group),
        jax.ShapeDtypeStruct((16 * chans, tokens), bf16),
        (2 * 16 * chans * tokens * 512, 4 * 16 * chans * tokens, 0),
    )(x)


def fold_rows(g_ref, o_ref, cols, group):
    samples, _, chans, rows = o_ref.shape
    span = cols * rows // 2
    hit, lane_col = row_pick(rows, rows // 2, cols)

    def block(s, c, r):
        parts = []
        for g in range(chans // group):
            at = (g * 16 + r * 4 + c) * group
            parts.append(g_ref[at : at + group, s * span : (s + 1) * span])
        return jnp.concatenate(parts, axis=0)

    left = jnp.concatenate(
        [
            jnp.concatenate([block(s, c, r) for r in range(4)], axis=1)
            for s in range(samples)
            for c in range(4)
        ],
        axis=0,
    )
    held = [[None] * (2 * cols + 2) for _ in range(samples)]
    for j in range(cols):
        pick = jnp.where(hit & (lane_col == j), 1.0, 0.0).astype(bf16)
        part = mm(left, pick, 1, 1)
        for s in range(samples):
            for c in range(4):
                at = (s * 4 + c) * chans
                piece = part[at : at + chans]
                before = held[s][2 * j + c]
                held[s][2 * j + c] = piece if before is None else before + piece
    for s in range(samples):
        for col in range(2 * cols + 2):
            o_ref[s, col] = held[s][col]


def fold_body(g_ref, o_ref, edge_ref, *, cols, group):
    fold_rows(g_ref, o_ref, cols, group)
    edge_ref[0] = o_ref[:, 0].astype(bf16)
    edge_ref[1] = o_ref[:, 2 * cols + 1].astype(bf16)


def fold(g, samples, cols, rows, group):
    chans, tokens = (g.shape[0] // 16, g.shape[1])
    return call(
        functools.partial(fold_body, cols=cols, group=group),
        (
            jax.ShapeDtypeStruct((samples, 2 * cols + 2, chans, rows), f32),
            jax.ShapeDtypeStruct((2, samples, chans, rows), bf16),
        ),
        (2 * 16 * chans * tokens * 512, 4 * 16 * chans * tokens, 0),
    )(g)


def own_lane(rows, lanes, group):
    row = lax.broadcasted_iota(jnp.int32, (rows, lanes), 0)
    lane = lax.broadcasted_iota(jnp.int32, (rows, lanes), 1)
    return row % group == lane % group


def agg_forward_body(win_ref, key_ref, value_ref, mask_ref, probs_ref, pooled_ref):
    groups, heads, group, lanes = probs_ref.shape
    inner = win_ref.shape[0] // groups
    head_dim = pooled_ref.shape[0] // heads
    own = own_lane(heads * group, inner, group)
    own_bias = own_lane(heads * group, group, group)
    spread = lambda x: jnp.broadcast_to(x[:, None, :], (heads, group, x.shape[1])).reshape(
        heads * group, x.shape[1]
    )
    scores = []
    for g in range(groups):
        keys = spread(key_ref[:, g * inner : (g + 1) * inner])
        keys = jnp.where(own, keys, 0.0)
        high = keys.astype(bf16)
        rest = keys - high.astype(f32)
        mid = rest.astype(bf16)
        least = (rest - mid.astype(f32)).astype(bf16)
        here = win_ref[g * inner : (g + 1) * inner, :]
        at = groups * inner + g * group
        bias = jnp.where(own_bias, spread(key_ref[:, at : at + group]), 0.0)
        scores.append(
            jnp.dot(high, here, preferred_element_type=f32)
            + jnp.dot(mid, here, preferred_element_type=f32)
            + jnp.dot(least, here, preferred_element_type=f32)
            + jnp.sum(bias, axis=1, keepdims=True)
        )
    window = inner // group
    win = win_ref[...].astype(f32).reshape(groups, window, group, lanes)
    pair = 128 // head_dim
    present = mask_ref[...].reshape(groups, group, lanes) > 0
    for h in range(heads):
        score = jnp.stack([x[h * group : (h + 1) * group] for x in scores])
        score = jnp.where(present, score, -1e30)
        most = jnp.max(jnp.max(score, axis=0), axis=0, keepdims=True)
        raised = jnp.exp(score - most[None])
        total = jnp.sum(jnp.sum(raised, axis=0), axis=0, keepdims=True)
        probs = raised * (1.0 / total)[None]
        probs_ref[:, h] = probs
        weighted = (win * probs[:, None]).astype(bf16).reshape(groups * inner, lanes)
        weighted = jnp.concatenate(
            [weighted, probs.astype(bf16).reshape(groups * group, lanes)], axis=0
        )
        if h % pair == 0:
            values = value_ref[:, h * head_dim : (h + pair) * head_dim].T
        at = h % pair * head_dim
        pooled_ref[h * head_dim : (h + 1) * head_dim, :] = jnp.dot(
            values[at : at + head_dim], weighted, preferred_element_type=f32
        ).astype(bf16)


def agg_forward(win, key_map_t, value_map, mask, group):
    rows, tokens = win.shape
    heads = key_map_t.shape[0]
    chans = mask.shape[0]
    depth, width = value_map.shape
    return call(
        agg_forward_body,
        (
            jax.ShapeDtypeStruct((chans // group, heads, group, tokens), f32),
            jax.ShapeDtypeStruct((width, tokens), bf16),
        ),
        (2 * tokens * depth * (width + heads * group), 6 * 2**20, heads * chans * tokens),
    )(win, key_map_t, value_map, mask)


def agg_backward_core(
    win_ref, probs_ref, gp_ref, value_ref, key_ref, gwin_ref, gvmt_ref, gkm_ref, gs_ref, acc_ref
):
    groups, heads, group, lanes = probs_ref.shape
    rows = win_ref.shape[0]
    inner = rows // groups
    window = inner // group
    head_dim = gp_ref.shape[0] // heads
    shape = (groups, window, group, lanes)
    win = win_ref[...].astype(f32).reshape(shape)
    for h in range(heads):
        here = slice(h * head_dim, (h + 1) * head_dim)
        gp = gp_ref[here, :]
        probs = probs_ref[:, h]
        gw = jnp.dot(value_ref[:, here], gp, preferred_element_type=f32)
        main = gw[:rows].reshape(shape)
        grad_probs = jnp.sum(main * win, axis=1) + gw[rows:].reshape(groups, group, lanes)
        delta = jnp.sum(jnp.sum(probs * grad_probs, axis=0), axis=0, keepdims=True)
        gs_ref[:, h * group : (h + 1) * group, :] = (probs * (grad_probs - delta[None])).astype(bf16)
        part = (main * probs[:, None]).reshape(rows, lanes)
        if h == 0:
            acc_ref[...] = part
        else:
            acc_ref[...] += part
        weighted = (win * probs[:, None]).astype(bf16).reshape(rows, lanes)
        weighted = jnp.concatenate(
            [weighted, probs.astype(bf16).reshape(groups * group, lanes)], axis=0
        )
        gvmt_ref[here, :] = mm(gp, weighted, 1, 1).astype(bf16)
    own = own_lane(heads * group, inner, group)
    own_bias = own_lane(heads * group, group, group)
    fold_in = lambda x: jnp.sum(x.reshape(heads, group, x.shape[1]), axis=1)
    for g in range(groups):
        here = slice(g * inner, (g + 1) * inner)
        keys = jnp.broadcast_to(key_ref[:, here][:, None, :], (heads, group, inner)).reshape(
            heads * group, inner
        )
        keys = jnp.where(own, keys, 0.0).astype(bf16)
        gs = gs_ref[g]
        gwin_ref[here, :] = (acc_ref[here, :] + mm(keys, gs, 0, 0)).astype(bf16)
        gkm_ref[:, here] = fold_in(jnp.where(own, mm(gs, win_ref[here, :], 1, 1), 0.0))
        total = jnp.sum(gs.astype(f32), axis=1, keepdims=True)
        at = rows + g * group
        gkm_ref[:, at : at + group] = fold_in(jnp.where(own_bias, total, 0.0))


def agg_backward(win, probs, grad_pooled_t, value_map, key_map_t):
    rows, tokens = win.shape
    groups, heads, group, _ = probs.shape
    depth, width = value_map.shape
    return call(
        agg_backward_core,
        (
            jax.ShapeDtypeStruct(win.shape, bf16),
            jax.ShapeDtypeStruct((width, depth), bf16),
            jax.ShapeDtypeStruct((heads, depth), f32),
        ),
        (4 * tokens * depth * (width + heads * group), 8 * 2**20, 0),
        scratch=(
            pltpu.VMEM((groups, heads * group, tokens), bf16),
            pltpu.VMEM((rows, tokens), f32),
        ),
    )(win, probs, grad_pooled_t, value_map, key_map_t)


def one_hot(rows, cols, place, keep=None):
    row = lax.broadcasted_iota(jnp.int32, (rows, cols), 0)
    hit = lax.broadcasted_iota(jnp.int32, (rows, cols), 1) == place(row)
    if keep is not None:
        hit = hit & keep(row)
    return jnp.where(hit, 1.0, 0.0).astype(bf16)


def agg_last_body(
    at_ref,
    win_ref,
    probs_ref,
    gp_ref,
    value_ref,
    key_ref,
    weight_ref,
    agg_value_ref,
    agg_query_ref,
    extra_ref,
    canvas_ref,
    edge_ref,
    mine_ref,
    other_ref,
    gwin_ref,
    gvmt_ref,
    gkm_ref,
    gs_ref,
    acc_ref,
    my_win_ref,
    late_ref,
    *,
    cols,
    parts,
):
    groups, heads, group, lanes = probs_ref.shape
    chans = groups * group
    my_chans = chans // parts
    depth, width = weight_ref.shape
    mine = width // parts
    part, parity = (at_ref[0], at_ref[1])
    agg_backward_core(
        win_ref, probs_ref, gp_ref, value_ref, key_ref, gwin_ref, gvmt_ref, gkm_ref, gs_ref, acc_ref
    )
    spot = lambda var, k: (var // group * 16 + k) * group + var % group
    pick = one_hot(
        16 * group,
        16 * chans,
        lambda row: spot(part * my_chans + row % group, row // group),
        lambda row: row % group < my_chans,
    )
    my_win_ref[...] = jnp.dot(pick, gwin_ref[...], preferred_element_type=f32).astype(bf16)
    fold_rows(my_win_ref, canvas_ref, cols, group)
    edge_ref[0] = canvas_ref[:, 0].astype(bf16)
    edge_ref[1] = canvas_ref[:, 2 * cols + 1].astype(bf16)
    key_low = gkm_ref[...].astype(bf16)
    late_ref[:mine, :] = mm(
        weight_ref[:, pl.ds(pl.multiple_of(part * mine, 128), mine)], gvmt_ref[...], 0, 1
    ).astype(bf16)
    ext_rows = -(-17 * my_chans // 16) * 16

    def ext_place(row):
        main = row < 16 * my_chans
        var = part * my_chans + jnp.where(main, row // 16, row - 16 * my_chans)
        return jnp.where(main, spot(var, row % 16), 16 * chans + var)

    select = one_hot(ext_rows, depth, ext_place, lambda row: row < 17 * my_chans)
    my_value = mm(select, gvmt_ref[...], 1, 1).astype(bf16)
    my_key = mm(select, key_low, 1, 1).astype(bf16)
    late_ref[mine : mine + ext_rows, :] = (
        mm(my_value, agg_value_ref[...], 1, 1)
        + jnp.dot(my_key, agg_query_ref[...], preferred_element_type=f32)
    ).astype(bf16)
    my_heads = heads // parts
    pick = one_hot(
        16, heads, lambda row: part * my_heads + row, lambda row: row < my_heads
    )
    query = jnp.dot(pick, key_low, preferred_element_type=f32).astype(bf16)
    at = mine + ext_rows
    late_ref[at : at + 16, :] = jnp.dot(
        query, weight_ref[...], preferred_element_type=f32
    ).astype(bf16)
    late_ref[at + 16 :, :] = extra_ref[...].astype(bf16)
    split_into(late_ref, parity, at_ref[2], mine_ref, other_ref)


def split_into(whole_ref, parity, line, mine_ref, other_ref):
    block = 128
    for pair in range(mine_ref.shape[1] // block):
        to = slice(pair * block, (pair + 1) * block)
        for target, side in ((mine_ref, parity), (other_ref, 1 - parity)):
            start = pl.multiple_of((2 * jnp.bitwise_xor(pair, line) + side) * block, block)
            target[:, to] = whole_ref[:, pl.ds(start, block)]


def agg_last(
    at, win, probs, grad_pooled_t, value_map, key_map_t, weight, agg_value, agg_query, extra, samples, cols, parts
):
    rows, tokens = win.shape
    groups, heads, group, _ = probs.shape
    depth, width = value_map.shape
    pix_rows = 2 * tokens // (samples * cols)
    count = width // parts + -(-17 * groups * group // parts // 16) * 16 + 32
    half = jax.ShapeDtypeStruct((count, width // 2), bf16)
    return call(
        functools.partial(agg_last_body, cols=cols, parts=parts),
        (
            jax.ShapeDtypeStruct((samples, 2 * cols + 2, group, pix_rows), f32),
            jax.ShapeDtypeStruct((2, samples, group, pix_rows), bf16),
            half,
            half,
        ),
        (6 * tokens * depth * (width + heads * group), 12 * 2**20, 0),
        1,
        9,
        scratch=(
            pltpu.VMEM(win.shape, bf16),
            pltpu.VMEM((width, depth), bf16),
            pltpu.VMEM((heads, depth), f32),
            pltpu.VMEM((groups, heads * group, tokens), bf16),
            pltpu.VMEM((rows, tokens), f32),
            pltpu.VMEM((16 * group, tokens), bf16),
            pltpu.VMEM((count, width), bf16),
        ),
    )(at, win, probs, grad_pooled_t, value_map, key_map_t, weight, agg_value, agg_query, extra)


def attend_body(x_ref, o_ref, lse_ref, key_ref, value_ref, query_ref, *, scale, wide):
    blocks, triple, span = x_ref.shape
    head_dim = triple // 3
    seq = blocks * span
    for n in range(blocks):
        here = slice(n * span, (n + 1) * span)
        query_ref[:, here] = x_ref[n, :head_dim, :] * jnp.asarray(scale, bf16)
        key_ref[here, :] = x_ref[n, head_dim : 2 * head_dim, :].T
        value_ref[:head_dim, here] = x_ref[n, 2 * head_dim :, :]
    value_ref[head_dim:, :] = jnp.ones((8, seq), bf16)
    for w in range(seq // wide):
        scores = jnp.dot(
            key_ref[...], query_ref[:, w * wide : (w + 1) * wide], preferred_element_type=f32
        )
        most = jnp.max(scores, axis=0, keepdims=True)
        raised = jnp.exp(scores - most).astype(bf16)
        both = jnp.dot(value_ref[...], raised, preferred_element_type=f32)
        total = both[head_dim : head_dim + 1]
        out = (both[:head_dim] * (1.0 / total)).astype(bf16)
        lse = most + jnp.log(total)
        for n in range(wide // span):
            here = slice(n * span, (n + 1) * span)
            o_ref[w * (wide // span) + n] = out[:, here]
            lse_ref[w * (wide // span) + n] = lse[:, here]


def attend(x, scale):
    blocks, triple, span = x.shape
    head_dim = triple // 3
    seq = blocks * span
    return call(
        functools.partial(attend_body, scale=scale, wide=max(span, seq // 2)),
        (
            jax.ShapeDtypeStruct((blocks, head_dim, span), bf16),
            jax.ShapeDtypeStruct((blocks, 1, span), f32),
        ),
        (4 * seq * seq * head_dim, 2 * x.size, seq * seq),
        scratch=(
            pltpu.VMEM((seq, head_dim), bf16),
            pltpu.VMEM((head_dim + 8, seq), bf16),
            pltpu.VMEM((head_dim, seq), bf16),
        ),
    )(x)


def attend_back_body(
    x_ref, do_ref, lse_ref, o_ref, key_ref, keyt_ref, value_ref, dkey_ref, dvalue_ref, *, scale
):
    blocks, triple, span = x_ref.shape
    head_dim = triple // 3
    for n in range(blocks):
        here = slice(n * span, (n + 1) * span)
        key_ref[here, :] = x_ref[n, head_dim : 2 * head_dim, :].T
        keyt_ref[:, here] = x_ref[n, head_dim : 2 * head_dim, :]
        value_ref[here, :] = x_ref[n, 2 * head_dim :, :].T
    for n in range(blocks):
        query = x_ref[n, :head_dim, :] * jnp.asarray(scale, bf16)
        grad = do_ref[n]
        scores = jnp.dot(key_ref[...], query, preferred_element_type=f32)
        probs = jnp.exp(scores - lse_ref[n])
        grad_probs = jnp.dot(value_ref[...], grad, preferred_element_type=f32)
        delta = jnp.sum(probs * grad_probs, axis=0, keepdims=True)
        grad_scores = (probs * (grad_probs - delta)).astype(bf16)
        o_ref[n, :head_dim, :] = (
            jnp.dot(keyt_ref[...], grad_scores, preferred_element_type=f32) * scale
        ).astype(bf16)
        dkey = jnp.dot(grad_scores, query.T, preferred_element_type=f32)
        dvalue = jnp.dot(probs.astype(bf16), grad.T, preferred_element_type=f32)
        if n == 0:
            dkey_ref[...] = dkey
            dvalue_ref[...] = dvalue
        else:
            dkey_ref[...] += dkey
            dvalue_ref[...] += dvalue
    for n in range(blocks):
        here = slice(n * span, (n + 1) * span)
        o_ref[n, head_dim : 2 * head_dim, :] = dkey_ref[here, :].T.astype(bf16)
        o_ref[n, 2 * head_dim :, :] = dvalue_ref[here, :].T.astype(bf16)


def attend_back(x, grad, lse, scale):
    blocks, triple, span = x.shape
    head_dim = triple // 3
    seq = blocks * span
    return call(
        functools.partial(attend_back_body, scale=scale),
        jax.ShapeDtypeStruct(x.shape, bf16),
        (10 * seq * seq * head_dim, 4 * x.size, seq * seq),
        scratch=(
            pltpu.VMEM((seq, head_dim), bf16),
            pltpu.VMEM((head_dim, seq), bf16),
            pltpu.VMEM((seq, head_dim), bf16),
            pltpu.VMEM((seq, head_dim), f32),
            pltpu.VMEM((seq, head_dim), f32),
        ),
    )(x, grad, lse)


def stats(x):
    centered = x - jnp.mean(x, axis=-1, keepdims=True)
    inverse = lax.rsqrt(jnp.mean(centered * centered, axis=-1, keepdims=True) + norm_eps)
    return centered * inverse, inverse


def norm_back(grad_out, gain, hat, inverse):
    grad_hat = grad_out * gain
    return inverse * (
        grad_hat
        - jnp.mean(grad_hat, axis=-1, keepdims=True)
        - hat * jnp.mean(grad_hat * hat, axis=-1, keepdims=True)
    )


def halves(core_ref, part_ref, mine_ref, other_ref):
    half = mine_ref.shape[0]
    core = core_ref[0]
    mine_ref[...] = part_ref[pl.ds(pl.multiple_of(core * half, half), half), :].astype(bf16)
    other_ref[...] = part_ref[pl.ds(pl.multiple_of((1 - core) * half, half), half), :].astype(bf16)


def joined(core_ref, mine_ref, other_ref, whole_ref):
    half = mine_ref.shape[0]
    core = core_ref[0]
    whole_ref[pl.ds(pl.multiple_of(core * half, half), half), :] = mine_ref[...].astype(f32)
    whole_ref[pl.ds(pl.multiple_of((1 - core) * half, half), half), :] = other_ref[...].astype(f32)


def enter_body(pooled_ref, out_ref, lead_ref, gain_ref, qkv_ref, start_ref, normed_ref, packed_ref):
    heads, samples, triple, span = packed_ref.shape
    head_dim = triple // 3
    x = jnp.dot(pooled_ref[...].T, out_ref[...], preferred_element_type=f32)
    for s in range(samples):
        here = slice(s * span, (s + 1) * span)
        start = x[here] + lead_ref[s : s + 1, :]
        start_ref[here, :] = start
        normed_ref[here, :] = (stats(start)[0] * gain_ref[...]).astype(bf16)
    for m in range(3):
        got = jnp.dot(normed_ref[...], qkv_ref[m], preferred_element_type=f32).astype(bf16).T
        for h in range(heads):
            for s in range(samples):
                packed_ref[h, s, m * head_dim : (m + 1) * head_dim, :] = got[
                    h * head_dim : (h + 1) * head_dim, s * span : (s + 1) * span
                ]


def enter(pooled_t, agg_out, lead_rows, gain, qkv, heads):
    width, tokens = pooled_t.shape
    samples = lead_rows.shape[0]
    head_dim = qkv.shape[2] // heads
    return call(
        enter_body,
        (
            jax.ShapeDtypeStruct((tokens, width), f32),
            jax.ShapeDtypeStruct((tokens, width), bf16),
            jax.ShapeDtypeStruct((heads, samples, 3 * head_dim, tokens // samples), bf16),
        ),
        (2 * tokens * width * (width + 3 * qkv.shape[2]), 8 * 2**20, 0),
    )(pooled_t, agg_out, lead_rows, gain, qkv)


def leave_body(core_ref, att_ref, weight_ref, att_t_ref, mine_ref, other_ref, part_ref):
    heads, samples, head_dim, span = att_ref.shape
    for s in range(samples):
        here = slice(s * span, (s + 1) * span)
        for h in range(heads):
            att_t_ref[h * head_dim : (h + 1) * head_dim, here] = att_ref[h, s]
    part_ref[...] = jnp.dot(att_t_ref[...].T, weight_ref[...], preferred_element_type=f32)
    halves(core_ref, part_ref, mine_ref, other_ref)


def leave(core, att, weight):
    heads, samples, head_dim, span = att.shape
    tokens, width = (samples * span, weight.shape[1])
    half = jax.ShapeDtypeStruct((tokens // 2, width), bf16)
    return call(
        leave_body,
        (jax.ShapeDtypeStruct((heads * head_dim, tokens), bf16), half, half),
        (2 * tokens * width * heads * head_dim, 3 * 2**20, 0),
        1,
        2,
        scratch=(pltpu.VMEM((tokens, width), f32),),
    )(core, att, weight)


def feed_body(
    core_ref,
    start_ref,
    mine_ref,
    other_ref,
    gain_ref,
    up_ref,
    grad_active_ref,
    mid_ref,
    normed_ref,
    active_ref,
    grad_hidden_ref,
    out_mine_ref,
    out_other_ref,
    part_ref,
):
    joined(core_ref, mine_ref, other_ref, part_ref)
    step = 128
    for at in range(0, start_ref.shape[0], step):
        here = slice(at, at + step)
        mid = start_ref[here, :] + part_ref[here, :]
        mid_ref[here, :] = mid
        normed = (stats(mid)[0] * gain_ref[...]).astype(bf16)
        normed_ref[here, :] = normed
        hidden = jnp.dot(normed, up_ref[...], preferred_element_type=f32)
        both = 0.5 * (1.0 + lax.erf(hidden * sqrt_half))
        active_ref[here, :] = (hidden * both).astype(bf16)
        slope = both + hidden * jnp.exp(-0.5 * hidden * hidden) * inv_root_two_pi
        grad = (grad_active_ref[here, :].astype(f32) * slope).astype(bf16)
        grad_hidden_ref[here, :] = grad
        part_ref[here, :] = mm(grad, up_ref[...], 1, 1)
    halves(core_ref, part_ref, out_mine_ref, out_other_ref)


def feed(core, start, mine, other, gain, up, grad_active):
    tokens, width = start.shape
    low = jax.ShapeDtypeStruct((tokens, width), bf16)
    wide = jax.ShapeDtypeStruct((tokens, up.shape[1]), bf16)
    half = jax.ShapeDtypeStruct(mine.shape, bf16)
    return call(
        feed_body,
        (jax.ShapeDtypeStruct((tokens, width), f32), low, wide, wide, half, half),
        (4 * tokens * width * up.shape[1], 14 * 2**20, 2 * tokens * up.shape[1]),
        1,
        6,
        scratch=(pltpu.VMEM((tokens, width), f32),),
    )(core, start, mine, other, gain, up, grad_active)


def feed_back_body(
    core_ref,
    mid_ref,
    mine_ref,
    other_ref,
    gain_ref,
    grad_end_ref,
    weight_ref,
    grad_mid_ref,
    grad_att_ref,
    grad_gain_ref,
    packed_ref,
    part_ref,
):
    heads, samples, head_dim, span = packed_ref.shape
    joined(core_ref, mine_ref, other_ref, part_ref)
    grad_gain = jnp.zeros(grad_gain_ref.shape, f32)
    step = 128
    for at in range(0, mid_ref.shape[0], step):
        here = slice(at, at + step)
        hat, inverse = stats(mid_ref[here, :])
        grad_out = part_ref[here, :]
        grad_gain += jnp.sum(grad_out * hat, axis=0, keepdims=True)
        grad = grad_end_ref[here, :].astype(f32) + norm_back(grad_out, gain_ref[...], hat, inverse)
        grad_mid_ref[here, :] = grad
        grad_att_ref[here, :] = grad.astype(bf16)
    grad_gain_ref[...] = grad_gain
    got = mm(weight_ref[...], grad_att_ref[...], 1, 1).astype(bf16)
    for h in range(heads):
        for s in range(samples):
            packed_ref[h, s] = got[h * head_dim : (h + 1) * head_dim, s * span : (s + 1) * span]


def feed_back(core, mid, mine, other, gain, grad_end, weight, heads, samples):
    tokens, width = mid.shape
    return call(
        feed_back_body,
        (
            jax.ShapeDtypeStruct((tokens, width), f32),
            jax.ShapeDtypeStruct((tokens, width), bf16),
            jax.ShapeDtypeStruct((1, width), f32),
            jax.ShapeDtypeStruct(
                (heads, samples, weight.shape[0] // heads, tokens // samples), bf16
            ),
        ),
        (2 * tokens * width * weight.shape[0], 9 * 2**20, 0),
        1,
        6,
        scratch=(pltpu.VMEM((tokens, width), f32),),
    )(core, mid, mine, other, gain, grad_end, weight)


def enter_back_body(core_ref, packed_ref, qkv_ref, flat_ref, mine_ref, other_ref, part_ref):
    heads, samples, triple, span = packed_ref.shape
    head_dim = triple // 3
    width = heads * head_dim
    for m in range(3):
        for h in range(heads):
            for s in range(samples):
                to = m * width + h * head_dim
                flat_ref[to : to + head_dim, s * span : (s + 1) * span] = packed_ref[
                    h, s, m * head_dim : (m + 1) * head_dim, :
                ]
    for m in range(3):
        part = mm(flat_ref[m * width : (m + 1) * width, :].T, qkv_ref[m], 1, 1)
        if m == 0:
            part_ref[...] = part
        else:
            part_ref[...] += part
    halves(core_ref, part_ref, mine_ref, other_ref)


def enter_back(core, packed, qkv):
    heads, samples, triple, span = packed.shape
    tokens, width = (samples * span, qkv.shape[1])
    half = jax.ShapeDtypeStruct((tokens // 2, width), bf16)
    return call(
        enter_back_body,
        (jax.ShapeDtypeStruct((heads * triple, tokens), bf16), half, half),
        (2 * tokens * width * heads * triple, 5 * 2**20, 0),
        1,
        2,
        scratch=(pltpu.VMEM((tokens, width), f32),),
    )(core, packed, qkv)


def pool_back_body(
    at_ref,
    start_ref,
    mine_ref,
    other_ref,
    gain_ref,
    grad_mid_ref,
    out_ref,
    my_pooled_ref,
    hot_ref,
    gain_two_ref,
    grad_agg_ref,
    extra_ref,
    pooled_ref,
    out_mine_ref,
    out_other_ref,
    part_ref,
    grad_out_ref,
):
    samples = hot_ref.shape[1]
    tokens, width = start_ref.shape
    joined(at_ref, mine_ref, other_ref, part_ref)
    grad_gain = jnp.zeros((1, width), f32)
    step = min(128, tokens // samples)
    sums = [jnp.zeros((1, width), f32) for _ in range(samples)]
    for at in range(0, tokens, step):
        here = slice(at, at + step)
        hat, inverse = stats(start_ref[here, :])
        grad_out = part_ref[here, :]
        grad_gain += jnp.sum(grad_out * hat, axis=0, keepdims=True)
        grad = grad_mid_ref[here, :] + norm_back(grad_out, gain_ref[...], hat, inverse)
        sums[at * samples // tokens] += jnp.sum(grad, axis=0, keepdims=True)
        grad_agg_ref[here, :] = grad.astype(bf16)
    leads = hot_ref.shape[0]
    row = lax.broadcasted_iota(jnp.int32, (leads, width), 0)
    extra = jnp.where(row == leads - 2, grad_gain, 0.0)
    extra = extra + jnp.where(row == leads - 1, gain_two_ref[...], 0.0)
    for s in range(samples):
        extra = extra + hot_ref[:, s : s + 1] * sums[s]
    extra_ref[...] = extra
    pooled_ref[...] = mm(out_ref[...], grad_agg_ref[...], 1, 1).astype(bf16)
    grad_out_ref[...] = jnp.dot(
        my_pooled_ref[...], grad_agg_ref[...], preferred_element_type=f32
    ).astype(bf16)
    split_into(grad_out_ref, at_ref[1], at_ref[2], out_mine_ref, out_other_ref)


def pool_back(at, start, mine, other, gain, grad_mid, agg_out, my_pooled, hot, gain_two):
    tokens, width = start.shape
    half = jax.ShapeDtypeStruct((my_pooled.shape[0], width // 2), bf16)
    return call(
        pool_back_body,
        (
            jax.ShapeDtypeStruct((tokens, width), bf16),
            jax.ShapeDtypeStruct((hot.shape[0], width), f32),
            jax.ShapeDtypeStruct((width, tokens), bf16),
            half,
            half,
        ),
        (3 * tokens * width * width, 9 * 2**20, 0),
        1,
        9,
        scratch=(
            pltpu.VMEM((tokens, width), f32),
            pltpu.VMEM((my_pooled.shape[0], width), bf16),
        ),
    )(at, start, mine, other, gain, grad_mid, agg_out, my_pooled, hot, gain_two)


def strips_body(place_ref, *refs, dims):
    mine_ref, other_ref = refs[-2:]
    step = pl.program_id(0)
    count = pl.num_programs(0) // 2

    def fill(o_ref):
        at = 0
        for left_ref, right_ref, dim in zip(refs[:-2:2], refs[1:-2:2], dims):
            wide = right_ref.shape[1 - dim]
            o_ref[:, at : at + wide] = mm(left_ref[...], right_ref[...], 0, dim).astype(bf16)
            at += wide

    @pl.when(step < count)
    def _():
        fill(other_ref)

    @pl.when(step >= count)
    def _():
        fill(mine_ref)


def strips(place, *pairs):
    tokens, width = pairs[0][0].shape
    block = 128
    count = width // block // 2
    wide = sum(right.shape[1 - dim] for _, right, dim in pairs)

    def left_map(i, place_ref):
        own = i // count
        side = place_ref[0] * own + (1 - place_ref[0]) * (1 - own)
        return (0, 2 * jnp.bitwise_xor(i % count, place_ref[1]) + side)

    specs = []
    for left, right, _ in pairs:
        specs.append(pl.BlockSpec((tokens, block), left_map))
        specs.append(pl.BlockSpec(right.shape, lambda i, place_ref: (0, 0)))
    half = jax.ShapeDtypeStruct((width // 2, wide), bf16)
    return pl.pallas_call(
        functools.partial(strips_body, dims=[dim for _, _, dim in pairs]),
        out_shape=(half, half),
        grid_spec=pltpu.PrefetchScalarGridSpec(
            num_scalar_prefetch=1,
            grid=(2 * count,),
            in_specs=specs,
            out_specs=(
                pl.BlockSpec((block, wide), lambda i, p: (jnp.maximum(i - count, 0), 0)),
                pl.BlockSpec((block, wide), lambda i, p: (jnp.minimum(i, count - 1), 0)),
            ),
        ),
        compiler_params=pltpu.CompilerParams(vmem_limit_bytes=vmem_most),
        cost_estimate=pl.CostEstimate(
            flops=tokens * width * wide // 32, bytes_accessed=width * wide // 16, transcendentals=0
        ),
    )(place, *[x for pair in pairs for x in pair[:2]])


def rows_total(refs, columns=slice(None)):
    total = refs[0][:, columns].astype(f32)
    for ref in refs[1:]:
        total = total + ref[:, columns].astype(f32)
    return total


def finish_body(*refs, parts):
    up, down, mid, end = [refs[n * parts : (n + 1) * parts] for n in range(4)]
    up_ref, down_ref, out_ref, qkv_ref, head_ref = refs[4 * parts :]
    local = out_ref.shape[0]
    up_ref[...] = rows_total(up)
    out_ref[...] = rows_total(mid, slice(2 * local, 3 * local)).T
    down_ref[...] = rows_total(down).T
    for m in range(2):
        qkv_ref[m] = rows_total(mid, slice(m * local, (m + 1) * local))
    qkv_ref[2] = rows_total(end, slice(0, local))
    head_ref[...] = rows_total(end, slice(local, end[0].shape[1])).T[: head_ref.shape[0]]


def finish(groups, local, head_rows):
    up, down = groups[:2]
    block, hidden = up[0].shape
    f32s = lambda *shape: jax.ShapeDtypeStruct(shape, f32)
    return call(
        functools.partial(finish_body, parts=len(up)),
        (
            f32s(block, hidden),
            f32s(hidden, block),
            f32s(local, block),
            f32s(3, block, local),
            f32s(head_rows, block),
        ),
        (0, 8 * 2**20, 0),
    )(*[x for group in groups for x in group])


def finish_late_body(*refs, parts):
    agg_ref, value_ref, patch_ref, bias_ref, query_ref, lead_ref, gain_ref = refs[parts:]
    total = rows_total(refs[:parts])
    at = agg_ref.shape[0]
    agg_ref[...] = total[:at]
    value_ref[...] = total[at : at + value_ref.shape[0]]
    at += value_ref.shape[0]
    my_chans = bias_ref.shape[0]
    patch_ref[...] = total[at : at + 16 * my_chans].reshape(patch_ref.shape)
    bias_ref[...] = total[at + 16 * my_chans : at + 17 * my_chans]
    at += -(-17 * my_chans // 16) * 16
    query_ref[...] = total[at : at + query_ref.shape[0]]
    lead_ref[...] = total[at + 16 : at + 16 + lead_ref.shape[0]]
    gain_ref[...] = total[at + 16 + lead_ref.shape[0] :]


def finish_late(late, local, my_chans, my_heads, leads):
    block = late[0].shape[1]
    f32s = lambda *shape: jax.ShapeDtypeStruct(shape, f32)
    return call(
        functools.partial(finish_late_body, parts=len(late)),
        (
            f32s(local, block),
            f32s(local, block),
            f32s(my_chans, 16, block),
            f32s(my_chans, block),
            f32s(my_heads, block),
            f32s(leads, block),
            f32s(8, block),
        ),
        (0, 2**20, 0),
    )(*late)


def close_body(canvas_ref, before_ref, after_ref, o_ref):
    samples, chans, cols, _ = o_ref.shape
    for s in range(samples):
        for col in range(cols):
            piece = canvas_ref[s, col + 1, :chans]
            if col == 0:
                piece = piece + before_ref[s, :chans].astype(f32)
            if col == cols - 1:
                piece = piece + after_ref[s, :chans].astype(f32)
            o_ref[s, :, col, :] = piece


def close_kernel(canvas, rims, chans):
    samples, wide, _, rows = canvas.shape
    return call(
        close_body,
        jax.ShapeDtypeStruct((samples, chans, wide - 2, rows), f32),
        (0, 2**20, 0),
    )(canvas, *rims)


def attend_gathered(packed, scale):
    head_dim = packed.shape[2] // 3
    whole = lax.all_gather(packed[:, :, head_dim:, :], "sector", axis=0)
    keys, values = (whole[:, :, :, :head_dim], whole[:, :, :, head_dim:])
    scores = (
        jnp.einsum("hsdq,nhsdk->hsqnk", packed[:, :, :head_dim], keys, preferred_element_type=f32)
        * scale
    )
    most = jnp.max(scores, axis=(3, 4), keepdims=True)
    raised = jnp.exp(scores - most)
    total = jnp.sum(raised, axis=(3, 4), keepdims=True)
    probs = (raised / total).astype(bf16)
    out = jnp.einsum("hsqnk,nhsdk->hsdq", probs, values, preferred_element_type=f32)
    return out.astype(bf16), most + jnp.log(total)


def attend_back_gathered(packed, grad, lse, scale):
    head_dim = packed.shape[2] // 3
    query = packed[:, :, :head_dim]
    whole = lax.all_gather(packed[:, :, head_dim:, :], "sector", axis=0)
    keys, values = (whole[:, :, :, :head_dim], whole[:, :, :, head_dim:])
    scores = jnp.einsum("hsdq,nhsdk->hsqnk", query, keys, preferred_element_type=f32) * scale
    probs = jnp.exp(scores - lse)
    grad_probs = jnp.einsum("hsdq,nhsdk->hsqnk", grad, values, preferred_element_type=f32)
    delta = jnp.sum(probs * grad_probs, axis=(3, 4), keepdims=True)
    grad_scores = (probs * (grad_probs - delta)).astype(bf16)
    grad_query = jnp.einsum("hsqnk,nhsdk->hsdq", grad_scores, keys, preferred_element_type=f32)
    grad_keys = jnp.einsum("hsqnk,hsdq->nhsdk", grad_scores, query, preferred_element_type=f32)
    grad_values = jnp.einsum(
        "hsqnk,hsdq->nhsdk", probs.astype(bf16), grad, preferred_element_type=f32
    )
    both = lax.psum_scatter(
        jnp.concatenate([grad_keys * scale, grad_values], axis=3), "sector", scatter_dimension=0
    )
    return jnp.concatenate([grad_query * scale, both], axis=2).astype(bf16)


def swap(x, axis, bit):
    size = lax.axis_size(axis)
    return lax.ppermute(x, axis, [(i, i ^ bit) for i in range(size)])


def rounded(x):
    return lax.reduce_precision(x, 8, 7)


def sum_over_mp(x):
    if lax.axis_size("mp") != 4:
        return lax.psum(x.astype(bf16), "mp").astype(f32)
    half = x.shape[0] // 2
    low, high = (rounded(x[:half]), rounded(x[half:]))
    first = lax.axis_index("mp") % 2 == 0
    mine, other = (jnp.where(first, low, high), jnp.where(first, high, low))
    mine = rounded(mine + swap(other.astype(bf16), "mp", 1).astype(f32))
    mine = rounded(mine + swap(mine.astype(bf16), "mp", 2).astype(f32))
    other = swap(mine.astype(bf16), "mp", 1).astype(f32)
    return jnp.concatenate([jnp.where(first, mine, other), jnp.where(first, other, mine)], axis=0)


def near_sum(mine, other):
    return rounded(mine.astype(f32) + swap(other, "mp", 1).astype(f32)).astype(bf16)


def far_sum(mine, got):
    mine = rounded(mine.astype(f32) + got.astype(f32)).astype(bf16)
    return mine, swap(mine, "mp", 1)


def ring_pair(leading, last):
    size = lax.axis_size("sector")
    up = [(i, (i + 1) % size) for i in range(size)]
    down = [(j, i) for i, j in up]
    return lax.ppermute(last, "sector", up), lax.ppermute(leading, "sector", down)


def split_cols(x, block):
    even = lax.axis_index("sector") % 2 == 0
    pairs = x.shape[1] // (2 * block)
    low = [x[:, 2 * p * block : (2 * p + 1) * block] for p in range(pairs)]
    high = [x[:, (2 * p + 1) * block : (2 * p + 2) * block] for p in range(pairs)]
    mine = [jnp.where(even, a, b) for a, b in zip(low, high)]
    other = [jnp.where(even, b, a) for a, b in zip(low, high)]
    return jnp.concatenate(mine, axis=1), jnp.concatenate(other, axis=1)


def pair_sum(mine, got):
    return (mine.astype(f32) + got.astype(f32)).astype(bf16)


def line_parts(pieces):
    return [pieces[0]] + [swap(pieces[n], "sector", 2 * n) for n in range(1, len(pieces))]


def norm_forward(values, gain_vec):
    row_mean = jnp.mean(values, axis=-1, keepdims=True)
    centered = values - row_mean
    inverse = lax.rsqrt(jnp.mean(centered * centered, axis=-1, keepdims=True) + norm_eps)
    normed = centered * inverse
    return (normed * gain_vec, normed, inverse)


def norm_backward(grad_out, gain_vec, normed, inverse):
    grad_normed = grad_out * gain_vec
    grad_gain = jnp.sum(grad_out * normed, axis=0)
    grad_in = inverse * (
        grad_normed
        - jnp.mean(grad_normed, axis=-1, keepdims=True)
        - normed * jnp.mean(grad_normed * normed, axis=-1, keepdims=True)
    )
    return (grad_in, grad_gain)


def gelu_slope(values):
    return (
        0.5 * (1.0 + lax.erf(values * sqrt_half))
        + values * jnp.exp(-0.5 * values * values) * inv_root_two_pi
    )


def mp_slice(values, axis_dim, mp_index, mp_count):
    piece_len = values.shape[axis_dim] // mp_count
    return lax.dynamic_slice_in_dim(values, mp_index * piece_len, piece_len, axis_dim)


def shards(
    input_field,
    present_mask,
    lead_index,
    patch_weight,
    patch_bias,
    agg_query,
    agg_value,
    agg_out,
    lead_table,
    norm1_gain,
    qkv_weight,
    attn_out_weight,
    norm2_gain,
    up_weight,
    down_weight,
    head_weight,
    pred_cotangent,
):
    samples, chans, pix_rows, pix_cols = input_field.shape
    rows, cols = (pix_rows // 2, pix_cols // 2)
    span = rows * cols
    tokens = samples * span
    width = patch_weight.shape[2]
    heads = agg_query.shape[0]
    head_dim = width // heads
    local_width = qkv_weight.shape[2]
    local_heads = local_width // head_dim
    sectors = lax.axis_size("sector")
    mp_count = lax.axis_size("mp")
    mp_index = lax.axis_index("mp")
    score_scale = head_dim ** (-0.5)
    depth = 17 * chans
    group = 16 if chans % 16 == 0 else chans
    groups = chans // group

    by_head = sectors == local_heads * samples
    block = width // sectors
    fast = by_head and block == 128 and sectors == 8 and mp_count == 4 and samples % 2 == 0 and span % 128 == 0
    exchange = lambda x: lax.all_to_all(
        x.reshape(sectors, x.shape[-2], x.shape[-1]), "sector", 0, 0, tiled=True
    )
    by_pair = lambda x: x.reshape(local_heads, samples, x.shape[1], x.shape[2])
    sector = lax.axis_index("sector")
    core = jnp.stack([mp_index % 2, sector % 2, sector // 2])
    whereabouts = core[1:]
    counts = range(width // block // 2)
    row_sums = lambda a, b: [
        pair_sum(a[n * block : (n + 1) * block], b[n * block : (n + 1) * block]) for n in counts
    ]
    lane_sums = lambda a, b: [
        pair_sum(a[:, n * block : (n + 1) * block], b[:, n * block : (n + 1) * block])
        for n in counts
    ]
    across = lambda x: swap(x, "mp", 2)
    beside = lambda x: swap(x, "sector", 1)
    barrier = lax.optimization_barrier

    fields = jnp.transpose(input_field, (0, 3, 1, 2))
    cots = jnp.transpose(pred_cotangent, (0, 3, 1, 2))
    before, after = ring_pair(
        jnp.stack([fields[:, 0], cots[:, 0]]), jnp.stack([fields[:, -1], cots[:, -1]])
    )
    haloed = lambda x, n: jnp.concatenate([before[n][:, None], x, after[n][:, None]], axis=1)
    win = windows(haloed(fields, 0), group)

    weight_kv = jnp.concatenate(
        [
            jnp.transpose(patch_weight.reshape(groups, group, 16, width), (0, 2, 1, 3)).reshape(
                16 * chans, width
            ),
            patch_bias,
        ],
        axis=0,
    )
    key_map_t = mm(agg_query, weight_kv, 1, 1)
    value_map = jnp.dot(weight_kv, agg_value, preferred_element_type=f32).astype(bf16)
    mask = jnp.broadcast_to(
        jnp.transpose(present_mask)[:, :, None], (chans, samples, span)
    ).reshape(chans, tokens)
    probs, pooled_t = agg_forward(win, key_map_t, value_map, mask, group)
    lead_hot = (lead_index[:, None] == jnp.arange(lead_table.shape[0])[None, :]).astype(f32)
    lead_rows = jnp.dot(lead_hot, lead_table.astype(f32), precision=highest)

    head_cols = head_weight.shape[1]
    spot = lax.broadcasted_iota(jnp.int32, (head_cols, head_cols), 1)
    source = lax.broadcasted_iota(jnp.int32, (head_cols, head_cols), 0)
    place = (spot % (16 * group)) // group
    shuffle = ((spot // (16 * group) * group + spot % group) * 16 + place == source).astype(bf16)
    head_kv = jnp.dot(head_weight, shuffle, preferred_element_type=f32).astype(bf16)
    grad_head_t = windows(haloed(cots, 1), group)
    grad_end = mm(grad_head_t, head_kv, 0, 1)
    grad_mlp = grad_end.astype(bf16)
    grad_active = mm(grad_mlp, down_weight, 1, 1)

    my_chans = chans // mp_count
    my_heads = heads // mp_count
    spots = lambda var, k: (var // group * 16 + k) * group + var % group

    def ext_place(row):
        main = row < 16 * my_chans
        var = mp_index * my_chans + jnp.where(main, row // 16, row - 16 * my_chans)
        return jnp.where(main, spots(var, row % 16), 16 * chans + var)

    head_rows = -(-16 * my_chans // 128) * 128
    my_head = jnp.dot(
        one_hot(head_rows, 16 * chans, ext_place, lambda row: row < 16 * my_chans),
        grad_head_t,
        preferred_element_type=f32,
    ).astype(bf16)
    my_pooled = mp_slice(pooled_t, 0, mp_index, mp_count)

    if fast:
        qkv = jnp.transpose(qkv_weight, (1, 0, 2))
        start_x, normed1_low, packed = enter(
            pooled_t, agg_out, lead_rows, norm1_gain[None], qkv, local_heads
        )
        held = exchange(packed)
        held, grad_active, grad_mlp, my_pooled = barrier(
            (held, grad_active.astype(bf16), grad_mlp, my_pooled)
        )
        att_held, lse = attend(held, score_scale)
        att_t, mine, other = leave(core, by_pair(exchange(att_held)), attn_out_weight)
        mine = near_sum(mine, other)
        mid_x, normed2_low, active_low, grad_hidden, mine, other = feed(
            core,
            start_x,
            *far_sum(mine, across(mine)),
            norm2_gain[None],
            up_weight,
            grad_active,
        )
        mine = near_sum(mine, other)
        down_mine, down_other = strips(whereabouts, (grad_mlp, active_low, 0))
        low = jnp.dot(active_low, down_weight, preferred_element_type=f32).astype(bf16)
        first = mp_index % 2 == 0
        low, high = (low[: tokens // 2], low[tokens // 2 :])
        end_mine = near_sum(jnp.where(first, low, high), jnp.where(first, high, low))
        up_mine, up_other = strips(whereabouts, (normed2_low, grad_hidden, 0))
        down_got = beside(down_other)
        got, down_mine, up_mine, end_mine = barrier((across(mine), down_mine, up_mine, end_mine))
        grad_mid, grad_att, grad_gain_two, grad_heads = feed_back(
            core,
            mid_x,
            *far_sum(mine, got),
            norm2_gain[None],
            grad_mlp,
            attn_out_weight,
            local_heads,
            samples,
        )
        down_pair = row_sums(down_mine, down_got)
        grad_att_held, down_pair, up_other = barrier(
            (exchange(grad_heads), down_pair, up_other)
        )
        down_parts = line_parts(down_pair)
        up_got = beside(up_other)
        grad_held = attend_back(held, grad_att_held, lse, score_scale)
        end_got, down_parts, up_got, grad_att, grad_held = barrier(
            (across(end_mine), down_parts, up_got, grad_att, grad_held)
        )
        out_mine, out_other = strips(whereabouts, (grad_att, att_t, 1))
        out_got = beside(out_other)
        near, far = far_sum(end_mine, end_got)
        end_x = mid_x + jnp.concatenate(
            [jnp.where(first, near, far), jnp.where(first, far, near)], axis=0
        ).astype(f32)
        grad_packed = exchange(grad_held)
    else:
        start_x = (
            mm(pooled_t, agg_out, 0, 0).reshape(samples, span, width) + lead_rows[:, None, :]
        ).reshape(tokens, width)
        normed1, hat_one, inv_one = norm_forward(start_x, norm1_gain)
        normed1_low = normed1.astype(bf16)
        qkv_t = lax.dot_general(
            qkv_weight, normed1_low, (((0,), (1,)), ((), ())), preferred_element_type=f32
        ).astype(bf16)
        packed = jnp.transpose(
            qkv_t.reshape(3, local_heads, head_dim, samples, span), (1, 3, 0, 2, 4)
        ).reshape(local_heads, samples, 3 * head_dim, span)
        att, lse = attend_gathered(packed, score_scale)
        att_t = jnp.transpose(att, (0, 2, 1, 3)).reshape(local_width, tokens)
        mid_x = start_x + sum_over_mp(mm(att_t, attn_out_weight, 0, 0))
        normed2, hat_two, inv_two = norm_forward(mid_x, norm2_gain)
        normed2_low = normed2.astype(bf16)
        hidden = jnp.dot(normed2_low, up_weight, preferred_element_type=f32)
        active_low = jax.nn.gelu(hidden, approximate=False).astype(bf16)
        grad_hidden = (grad_active * gelu_slope(hidden)).astype(bf16)
        grad_normed2 = sum_over_mp(mm(grad_hidden, up_weight, 1, 1))
        grad_mid_norm, grad_gain_two = norm_backward(grad_normed2, norm2_gain, hat_two, inv_two)
        grad_mid = grad_end + grad_mid_norm
        grad_att = grad_mid.astype(bf16)
        grad_heads_t = mm(attn_out_weight, grad_att, 1, 1).astype(bf16)
        grad_heads = jnp.transpose(
            grad_heads_t.reshape(local_heads, head_dim, samples, span), (0, 2, 1, 3)
        )
        grad_packed = attend_back_gathered(packed, grad_heads, lse, score_scale)
        end_x = mid_x + sum_over_mp(jnp.dot(active_low, down_weight, preferred_element_type=f32))

    end_low = end_x.astype(bf16)
    head_out = mm(head_kv, end_low, 0, 1).astype(bf16)
    canvas, edges = fold(head_out, samples, cols, pix_rows, group)

    def close(canvas, rims):
        inner = canvas[:, 1:-1]
        inner = inner.at[:, 0].add(rims[0].astype(f32))
        return jnp.transpose(inner.at[:, -1].add(rims[1].astype(f32)), (0, 2, 3, 1))

    leads = lead_table.shape[0]

    if fast:
        joint = lambda *x: jnp.concatenate(x, axis=0)
        up_parts = line_parts(row_sums(up_mine, up_got))
        rims = ring_pair(edges[0], edges[1])
        grad_packed, rims, out_got = barrier((grad_packed, rims, out_got))
        out_pair = row_sums(out_mine, out_got)
        flat, mine, other = enter_back(core, by_pair(grad_packed), qkv)
        mine = near_sum(mine, other)
        part = 2 * local_width
        mid_mine, mid_other = strips(whereabouts, (normed1_low, flat[:part], 1))
        mid_got = beside(mid_other)
        end_mine, end_other = strips(
            whereabouts, (normed1_low, flat[part:], 1), (end_low, my_head, 1)
        )
        end_got = beside(end_other)
        got, mid_mine, end_mine, up_parts = barrier((across(mine), mid_mine, end_mine, up_parts))
        hot = jnp.zeros((leads + 8, samples), f32).at[:leads].set(jnp.transpose(lead_hot))
        grad_agg, extra, grad_pooled_t, agg_mine, agg_other = pool_back(
            core,
            start_x,
            *far_sum(mine, got),
            norm1_gain[None],
            grad_mid,
            agg_out,
            my_pooled,
            hot,
            grad_gain_two,
        )
        mid_got, out_pair, grad_pooled_t = barrier((mid_got, out_pair, grad_pooled_t))
        mid_pair = [
            jnp.concatenate(x, axis=1) for x in zip(row_sums(mid_mine, mid_got), out_pair)
        ]
        mid_parts = line_parts(mid_pair)
        grad_canvas, grad_edges, late_mine, late_other = agg_last(
            jnp.stack([mp_index, sector % 2, sector // 2]),
            win,
            probs,
            grad_pooled_t,
            value_map,
            key_map_t,
            weight_kv,
            agg_value,
            agg_query,
            extra,
            samples,
            cols,
            mp_count,
        )
        late_other, grad_edges, mid_parts, end_got = barrier(
            (late_other, grad_edges, mid_parts, end_got)
        )
        end_parts = line_parts(row_sums(end_mine, end_got))
        grad_rims = ring_pair(grad_edges[0], grad_edges[1])
        late_got, grad_rims = barrier((beside(late_other), grad_rims))
        agg_pair = lane_sums(agg_mine, beside(agg_other))
        late_pair = lane_sums(late_mine, late_got)
        late_parts = line_parts([jnp.concatenate(x, axis=0) for x in zip(agg_pair, late_pair)])
        outs = finish(
            (up_parts, down_parts, mid_parts, end_parts), local_width, 16 * my_chans
        )
        prediction = close_kernel(canvas, rims, chans)
        field_grad = close_kernel(grad_canvas, grad_rims, my_chans)
        late_parts, outs, prediction, field_grad = barrier(
            (late_parts, outs, prediction, field_grad)
        )
        up_sum, down_sum, out_sum, qkv_sum, head_sum = outs
        qkv_sum = jnp.transpose(qkv_sum, (1, 0, 2))
        head_sum = jnp.transpose(head_sum)
        prediction, field_grad = [jnp.transpose(x, (0, 1, 3, 2)) for x in (prediction, field_grad)]
        agg_out_sum, value_sum, patch_sum, bias_sum, query_sum, lead_sum, gain_sums = finish_late(
            late_parts, local_width, my_chans, my_heads, leads
        )
        one_sum, two_sum = (gain_sums[6:7], gain_sums[7:8])
    else:
        prediction = close(canvas, ring_pair(edges[0], edges[1]))
        flat = jnp.transpose(
            grad_packed.reshape(local_heads, samples, 3, head_dim, span), (2, 0, 3, 1, 4)
        ).reshape(3 * local_width, tokens)
        grad_normed1 = sum_over_mp(
            lax.dot_general(
                flat.reshape(3, local_width, tokens),
                qkv_weight,
                (((0, 1), (1, 2)), ((), ())),
                preferred_element_type=f32,
            )
        )
        grad_start_norm, grad_gain_one = norm_backward(grad_normed1, norm1_gain, hat_one, inv_one)
        grad_start = grad_mid + grad_start_norm
        grad_agg = grad_start.astype(bf16)
        sample_sums = jnp.sum(grad_start.reshape(samples, span, width), axis=1)
        grad_pooled_t = mm(agg_out, grad_agg, 1, 1).astype(bf16)
        grad_lead = jnp.einsum("sl,sd->ld", lead_hot, sample_sums, precision=highest)
        gains = [x.reshape(1, width) for x in (grad_gain_one, grad_gain_two)]
        grad_win, value_grad_t, key_grad = agg_backward(
            win, probs, grad_pooled_t, value_map, key_map_t
        )
        key_low = key_grad.astype(bf16)
        grad_agg_value = mm(mp_slice(weight_kv, 1, mp_index, mp_count), value_grad_t, 0, 1)
        select = one_hot(17 * my_chans, depth, ext_place)
        my_value = mm(select, value_grad_t, 1, 1).astype(bf16)
        my_key = mm(select, key_low, 1, 1).astype(bf16)
        grad_ext = mm(my_value, agg_value, 1, 1) + jnp.dot(
            my_key, agg_query, preferred_element_type=f32
        )
        grad_agg_query = jnp.dot(
            mp_slice(key_low, 0, mp_index, mp_count), weight_kv, preferred_element_type=f32
        )
        grad_canvas, grad_edges = fold(grad_win, samples, cols, pix_rows, group)
        grad_edges = mp_slice(grad_edges, 2, mp_index, mp_count)
        field_grad = close(
            mp_slice(grad_canvas, 2, mp_index, mp_count), ring_pair(grad_edges[0], grad_edges[1])
        )
        put = lambda x, dim: lax.psum_scatter(x, "sector", scatter_dimension=dim, tiled=True)
        up_sum = put(mm(normed2_low, grad_hidden, 0, 0), 0)
        down_sum = put(mm(active_low, grad_mlp, 0, 0), 1)
        out_sum = put(jnp.dot(att_t, grad_att, preferred_element_type=f32), 1)
        head_sum = put(mm(end_low, my_head[: 16 * my_chans], 0, 1), 0)
        qkv_sum = put(mm(normed1_low, flat, 0, 1), 0).reshape(block, 3, local_width)
        agg_out_sum = put(jnp.dot(my_pooled, grad_agg, preferred_element_type=f32), 1)
        late = [grad_agg_value, grad_ext, grad_agg_query, grad_lead] + gains
        value_sum, ext_sum, query_sum, lead_sum, one_sum, two_sum = [put(x, 1) for x in late]
        patch_sum = ext_sum[: 16 * my_chans].reshape(my_chans, 16, block)
        bias_sum = ext_sum[16 * my_chans :]
    return (
        prediction,
        field_grad,
        patch_sum,
        bias_sum,
        query_sum,
        value_sum,
        agg_out_sum,
        lead_sum,
        one_sum[0],
        qkv_sum,
        out_sum,
        two_sum[0],
        up_sum,
        down_sum,
        head_sum,
    )


def solution(mesh):
    placed = (
        P(None, None, None, "sector"),
        P(),
        P(),
        P(),
        P(),
        P(),
        P(),
        P(),
        P(),
        P(),
        P(None, None, "mp"),
        P("mp", None),
        P(),
        P(None, "mp"),
        P("mp", None),
        P(),
        P(None, None, None, "sector"),
    )
    return jax.shard_map(
        shards,
        mesh=mesh,
        in_specs=placed,
        out_specs=(
            P(None, None, None, "sector"),
            P(None, "mp", None, "sector"),
            P("mp", None, "sector"),
            P("mp", "sector"),
            P("mp", "sector"),
            P("mp", "sector"),
            P("mp", "sector"),
            P(None, "sector"),
            P("sector"),
            P("sector", None, "mp"),
            P("mp", "sector"),
            P("sector"),
            P("sector", "mp"),
            P("mp", "sector"),
            P("sector", "mp"),
        ),
        check_vma=False,
    )
```

```python
import functools

import jax
import jax.numpy as jnp
from jax import lax
from jax.experimental import pallas as pl
from jax.experimental.pallas import tpu as pltpu
from jax.sharding import PartitionSpec as P

bf16 = jnp.bfloat16
f32 = jnp.float32
highest = lax.Precision.HIGHEST
norm_eps = 1e-05
sqrt_half = 0.7071067811865476
inv_root_two_pi = 0.3989422804014327
vmem_most = 44 * 1024 * 1024


def mm(left, right, left_dim, right_dim):
    return lax.dot_general(
        left, right, (((left_dim,), (right_dim,)), ((), ())), preferred_element_type=f32
    )


def call(body, out_shape, cost, scalars=0, tensors=0, scratch=()):
    more = {}
    if scalars:
        more = dict(
            in_specs=[pl.BlockSpec(memory_space=pltpu.SMEM)] * scalars
            + [pl.BlockSpec(memory_space=pltpu.VMEM)] * tensors
        )
    return pl.pallas_call(
        body,
        out_shape=out_shape,
        scratch_shapes=list(scratch),
        compiler_params=pltpu.CompilerParams(vmem_limit_bytes=vmem_most),
        cost_estimate=pl.CostEstimate(
            flops=int(cost[0]) // 64, bytes_accessed=int(cost[1]) // 64, transcendentals=int(cost[2]) // 64
        ),
        **more,
    )


def row_pick(rows, patch_rows, patch_cols):
    span = patch_rows * patch_cols
    lane = lax.broadcasted_iota(jnp.int32, (rows, 4 * span), 1)
    row = lax.broadcasted_iota(jnp.int32, (rows, 4 * span), 0)
    r = lane // span
    rest = lane - r * span
    j = rest // patch_rows
    i = rest - j * patch_rows
    return (row == 2 * i + r - 1), j


def windows_body(x_ref, o_ref, *, group):
    samples, wide, chans, rows = x_ref.shape
    cols, patch_rows = (wide - 2) // 2, rows // 2
    span = cols * patch_rows
    hit, lane_col = row_pick(rows, patch_rows, cols)
    total = None
    for j in range(cols):
        left = jnp.concatenate(
            [x_ref[s, 2 * j + c] for s in range(samples) for c in range(4)], axis=0
        )
        pick = jnp.where(hit & (lane_col == j), 1.0, 0.0).astype(bf16)
        part = jnp.dot(left, pick, preferred_element_type=f32)
        total = part if total is None else total + part
    for s in range(samples):
        for c in range(4):
            for g in range(chans // group):
                at = (s * 4 + c) * chans + g * group
                for r in range(4):
                    to = (g * 16 + r * 4 + c) * group
                    o_ref[to : to + group, s * span : (s + 1) * span] = total[
                        at : at + group, r * span : (r + 1) * span
                    ].astype(o_ref.dtype)


def windows(x, group):
    samples, wide, chans, rows = x.shape
    tokens = samples * (wide - 2) * rows // 4
    return call(
        functools.partial(windows_body, group=group),
        jax.ShapeDtypeStruct((16 * chans, tokens), bf16),
        (2 * 16 * chans * tokens * 512, 4 * 16 * chans * tokens, 0),
    )(x)


def fold_rows(g_ref, o_ref, cols, group):
    samples, _, chans, rows = o_ref.shape
    span = cols * rows // 2
    hit, lane_col = row_pick(rows, rows // 2, cols)

    def block(s, c, r):
        parts = []
        for g in range(chans // group):
            at = (g * 16 + r * 4 + c) * group
            parts.append(g_ref[at : at + group, s * span : (s + 1) * span])
        return jnp.concatenate(parts, axis=0)

    left = jnp.concatenate(
        [
            jnp.concatenate([block(s, c, r) for r in range(4)], axis=1)
            for s in range(samples)
            for c in range(4)
        ],
        axis=0,
    )
    held = [[None] * (2 * cols + 2) for _ in range(samples)]
    for j in range(cols):
        pick = jnp.where(hit & (lane_col == j), 1.0, 0.0).astype(bf16)
        part = mm(left, pick, 1, 1)
        for s in range(samples):
            for c in range(4):
                at = (s * 4 + c) * chans
                piece = part[at : at + chans]
                before = held[s][2 * j + c]
                held[s][2 * j + c] = piece if before is None else before + piece
    for s in range(samples):
        for col in range(2 * cols + 2):
            o_ref[s, col] = held[s][col]


def fold_body(g_ref, o_ref, edge_ref, *, cols, group):
    fold_rows(g_ref, o_ref, cols, group)
    edge_ref[0] = o_ref[:, 0].astype(bf16)
    edge_ref[1] = o_ref[:, 2 * cols + 1].astype(bf16)


def fold(g, samples, cols, rows, group):
    chans, tokens = (g.shape[0] // 16, g.shape[1])
    return call(
        functools.partial(fold_body, cols=cols, group=group),
        (
            jax.ShapeDtypeStruct((samples, 2 * cols + 2, chans, rows), f32),
            jax.ShapeDtypeStruct((2, samples, chans, rows), bf16),
        ),
        (2 * 16 * chans * tokens * 512, 4 * 16 * chans * tokens, 0),
    )(g)


def own_lane(rows, lanes, group):
    row = lax.broadcasted_iota(jnp.int32, (rows, lanes), 0)
    lane = lax.broadcasted_iota(jnp.int32, (rows, lanes), 1)
    return row % group == lane % group


def agg_forward_body(win_ref, key_ref, value_ref, mask_ref, probs_ref, pooled_ref):
    groups, heads, group, lanes = probs_ref.shape
    inner = win_ref.shape[0] // groups
    head_dim = pooled_ref.shape[0] // heads
    own = own_lane(heads * group, inner, group)
    own_bias = own_lane(heads * group, group, group)
    spread = lambda x: jnp.broadcast_to(x[:, None, :], (heads, group, x.shape[1])).reshape(
        heads * group, x.shape[1]
    )
    scores = []
    for g in range(groups):
        keys = spread(key_ref[:, g * inner : (g + 1) * inner])
        keys = jnp.where(own, keys, 0.0)
        high = keys.astype(bf16)
        rest = keys - high.astype(f32)
        mid = rest.astype(bf16)
        least = (rest - mid.astype(f32)).astype(bf16)
        here = win_ref[g * inner : (g + 1) * inner, :]
        at = groups * inner + g * group
        bias = jnp.where(own_bias, spread(key_ref[:, at : at + group]), 0.0)
        scores.append(
            jnp.dot(high, here, preferred_element_type=f32)
            + jnp.dot(mid, here, preferred_element_type=f32)
            + jnp.dot(least, here, preferred_element_type=f32)
            + jnp.sum(bias, axis=1, keepdims=True)
        )
    window = inner // group
    win = win_ref[...].astype(f32).reshape(groups, window, group, lanes)
    pair = 128 // head_dim
    present = mask_ref[...].reshape(groups, group, lanes) > 0
    for h in range(heads):
        score = jnp.stack([x[h * group : (h + 1) * group] for x in scores])
        score = jnp.where(present, score, -1e30)
        most = jnp.max(jnp.max(score, axis=0), axis=0, keepdims=True)
        raised = jnp.exp(score - most[None])
        total = jnp.sum(jnp.sum(raised, axis=0), axis=0, keepdims=True)
        probs = raised * (1.0 / total)[None]
        probs_ref[:, h] = probs
        weighted = (win * probs[:, None]).astype(bf16).reshape(groups * inner, lanes)
        weighted = jnp.concatenate(
            [weighted, probs.astype(bf16).reshape(groups * group, lanes)], axis=0
        )
        if h % pair == 0:
            values = value_ref[:, h * head_dim : (h + pair) * head_dim].T
        at = h % pair * head_dim
        pooled_ref[h * head_dim : (h + 1) * head_dim, :] = jnp.dot(
            values[at : at + head_dim], weighted, preferred_element_type=f32
        ).astype(bf16)


def agg_forward(win, key_map_t, value_map, mask, group):
    rows, tokens = win.shape
    heads = key_map_t.shape[0]
    chans = mask.shape[0]
    depth, width = value_map.shape
    return call(
        agg_forward_body,
        (
            jax.ShapeDtypeStruct((chans // group, heads, group, tokens), f32),
            jax.ShapeDtypeStruct((width, tokens), bf16),
        ),
        (2 * tokens * depth * (width + heads * group), 6 * 2**20, heads * chans * tokens),
    )(win, key_map_t, value_map, mask)


def agg_backward_core(
    win_ref, probs_ref, gp_ref, value_ref, key_ref, gwin_ref, gvmt_ref, gkm_ref, gs_ref, acc_ref
):
    groups, heads, group, lanes = probs_ref.shape
    rows = win_ref.shape[0]
    inner = rows // groups
    window = inner // group
    head_dim = gp_ref.shape[0] // heads
    shape = (groups, window, group, lanes)
    win = win_ref[...].astype(f32).reshape(shape)
    for h in range(heads):
        here = slice(h * head_dim, (h + 1) * head_dim)
        gp = gp_ref[here, :]
        probs = probs_ref[:, h]
        gw = jnp.dot(value_ref[:, here], gp, preferred_element_type=f32)
        main = gw[:rows].reshape(shape)
        grad_probs = jnp.sum(main * win, axis=1) + gw[rows:].reshape(groups, group, lanes)
        delta = jnp.sum(jnp.sum(probs * grad_probs, axis=0), axis=0, keepdims=True)
        gs_ref[:, h * group : (h + 1) * group, :] = (probs * (grad_probs - delta[None])).astype(bf16)
        part = (main * probs[:, None]).reshape(rows, lanes)
        if h == 0:
            acc_ref[...] = part
        else:
            acc_ref[...] += part
        weighted = (win * probs[:, None]).astype(bf16).reshape(rows, lanes)
        weighted = jnp.concatenate(
            [weighted, probs.astype(bf16).reshape(groups * group, lanes)], axis=0
        )
        gvmt_ref[here, :] = mm(gp, weighted, 1, 1).astype(bf16)
    own = own_lane(heads * group, inner, group)
    own_bias = own_lane(heads * group, group, group)
    fold_in = lambda x: jnp.sum(x.reshape(heads, group, x.shape[1]), axis=1)
    for g in range(groups):
        here = slice(g * inner, (g + 1) * inner)
        keys = jnp.broadcast_to(key_ref[:, here][:, None, :], (heads, group, inner)).reshape(
            heads * group, inner
        )
        keys = jnp.where(own, keys, 0.0).astype(bf16)
        gs = gs_ref[g]
        gwin_ref[here, :] = (acc_ref[here, :] + mm(keys, gs, 0, 0)).astype(bf16)
        gkm_ref[:, here] = fold_in(jnp.where(own, mm(gs, win_ref[here, :], 1, 1), 0.0))
        total = jnp.sum(gs.astype(f32), axis=1, keepdims=True)
        at = rows + g * group
        gkm_ref[:, at : at + group] = fold_in(jnp.where(own_bias, total, 0.0))


def agg_backward(win, probs, grad_pooled_t, value_map, key_map_t):
    rows, tokens = win.shape
    groups, heads, group, _ = probs.shape
    depth, width = value_map.shape
    return call(
        agg_backward_core,
        (
            jax.ShapeDtypeStruct(win.shape, bf16),
            jax.ShapeDtypeStruct((width, depth), bf16),
            jax.ShapeDtypeStruct((heads, depth), f32),
        ),
        (4 * tokens * depth * (width + heads * group), 8 * 2**20, 0),
        scratch=(
            pltpu.VMEM((groups, heads * group, tokens), bf16),
            pltpu.VMEM((rows, tokens), f32),
        ),
    )(win, probs, grad_pooled_t, value_map, key_map_t)


def one_hot(rows, cols, place, keep=None):
    row = lax.broadcasted_iota(jnp.int32, (rows, cols), 0)
    hit = lax.broadcasted_iota(jnp.int32, (rows, cols), 1) == place(row)
    if keep is not None:
        hit = hit & keep(row)
    return jnp.where(hit, 1.0, 0.0).astype(bf16)


def agg_last_body(
    at_ref,
    win_ref,
    probs_ref,
    gp_ref,
    value_ref,
    key_ref,
    weight_ref,
    agg_value_ref,
    agg_query_ref,
    extra_ref,
    canvas_ref,
    edge_ref,
    mine_ref,
    other_ref,
    gwin_ref,
    gvmt_ref,
    gkm_ref,
    gs_ref,
    acc_ref,
    my_win_ref,
    late_ref,
    *,
    cols,
    parts,
):
    groups, heads, group, lanes = probs_ref.shape
    chans = groups * group
    my_chans = chans // parts
    depth, width = weight_ref.shape
    mine = width // parts
    part, parity = (at_ref[0], at_ref[1])
    agg_backward_core(
        win_ref, probs_ref, gp_ref, value_ref, key_ref, gwin_ref, gvmt_ref, gkm_ref, gs_ref, acc_ref
    )
    spot = lambda var, k: (var // group * 16 + k) * group + var % group
    pick = one_hot(
        16 * group,
        16 * chans,
        lambda row: spot(part * my_chans + row % group, row // group),
        lambda row: row % group < my_chans,
    )
    my_win_ref[...] = jnp.dot(pick, gwin_ref[...], preferred_element_type=f32).astype(bf16)
    fold_rows(my_win_ref, canvas_ref, cols, group)
    edge_ref[0] = canvas_ref[:, 0].astype(bf16)
    edge_ref[1] = canvas_ref[:, 2 * cols + 1].astype(bf16)
    key_low = gkm_ref[...].astype(bf16)
    late_ref[:mine, :] = mm(
        weight_ref[:, pl.ds(pl.multiple_of(part * mine, 128), mine)], gvmt_ref[...], 0, 1
    ).astype(bf16)
    ext_rows = -(-17 * my_chans // 16) * 16

    def ext_place(row):
        main = row < 16 * my_chans
        var = part * my_chans + jnp.where(main, row // 16, row - 16 * my_chans)
        return jnp.where(main, spot(var, row % 16), 16 * chans + var)

    select = one_hot(ext_rows, depth, ext_place, lambda row: row < 17 * my_chans)
    my_value = mm(select, gvmt_ref[...], 1, 1).astype(bf16)
    my_key = mm(select, key_low, 1, 1).astype(bf16)
    late_ref[mine : mine + ext_rows, :] = (
        mm(my_value, agg_value_ref[...], 1, 1)
        + jnp.dot(my_key, agg_query_ref[...], preferred_element_type=f32)
    ).astype(bf16)
    my_heads = heads // parts
    pick = one_hot(
        16, heads, lambda row: part * my_heads + row, lambda row: row < my_heads
    )
    query = jnp.dot(pick, key_low, preferred_element_type=f32).astype(bf16)
    at = mine + ext_rows
    late_ref[at : at + 16, :] = jnp.dot(
        query, weight_ref[...], preferred_element_type=f32
    ).astype(bf16)
    late_ref[at + 16 :, :] = extra_ref[...].astype(bf16)
    split_into(late_ref, parity, at_ref[2], mine_ref, other_ref)


def split_into(whole_ref, parity, line, mine_ref, other_ref):
    block = 128
    for pair in range(mine_ref.shape[1] // block):
        to = slice(pair * block, (pair + 1) * block)
        for target, side in ((mine_ref, parity), (other_ref, 1 - parity)):
            start = pl.multiple_of((2 * jnp.bitwise_xor(pair, line) + side) * block, block)
            target[:, to] = whole_ref[:, pl.ds(start, block)]


def agg_last(
    at, win, probs, grad_pooled_t, value_map, key_map_t, weight, agg_value, agg_query, extra, samples, cols, parts
):
    rows, tokens = win.shape
    groups, heads, group, _ = probs.shape
    depth, width = value_map.shape
    pix_rows = 2 * tokens // (samples * cols)
    count = width // parts + -(-17 * groups * group // parts // 16) * 16 + 32
    half = jax.ShapeDtypeStruct((count, width // 2), bf16)
    return call(
        functools.partial(agg_last_body, cols=cols, parts=parts),
        (
            jax.ShapeDtypeStruct((samples, 2 * cols + 2, group, pix_rows), f32),
            jax.ShapeDtypeStruct((2, samples, group, pix_rows), bf16),
            half,
            half,
        ),
        (6 * tokens * depth * (width + heads * group), 12 * 2**20, 0),
        1,
        9,
        scratch=(
            pltpu.VMEM(win.shape, bf16),
            pltpu.VMEM((width, depth), bf16),
            pltpu.VMEM((heads, depth), f32),
            pltpu.VMEM((groups, heads * group, tokens), bf16),
            pltpu.VMEM((rows, tokens), f32),
            pltpu.VMEM((16 * group, tokens), bf16),
            pltpu.VMEM((count, width), bf16),
        ),
    )(at, win, probs, grad_pooled_t, value_map, key_map_t, weight, agg_value, agg_query, extra)


def attend_body(x_ref, o_ref, lse_ref, key_ref, value_ref, query_ref, *, scale, wide):
    blocks, triple, span = x_ref.shape
    head_dim = triple // 3
    seq = blocks * span
    for n in range(blocks):
        here = slice(n * span, (n + 1) * span)
        query_ref[:, here] = x_ref[n, :head_dim, :] * jnp.asarray(scale, bf16)
        key_ref[here, :] = x_ref[n, head_dim : 2 * head_dim, :].T
        value_ref[:head_dim, here] = x_ref[n, 2 * head_dim :, :]
    value_ref[head_dim:, :] = jnp.ones((8, seq), bf16)
    for w in range(seq // wide):
        scores = jnp.dot(
            key_ref[...], query_ref[:, w * wide : (w + 1) * wide], preferred_element_type=f32
        )
        most = jnp.max(scores, axis=0, keepdims=True)
        raised = jnp.exp(scores - most).astype(bf16)
        both = jnp.dot(value_ref[...], raised, preferred_element_type=f32)
        total = both[head_dim : head_dim + 1]
        out = (both[:head_dim] * (1.0 / total)).astype(bf16)
        lse = most + jnp.log(total)
        for n in range(wide // span):
            here = slice(n * span, (n + 1) * span)
            o_ref[w * (wide // span) + n] = out[:, here]
            lse_ref[w * (wide // span) + n] = lse[:, here]


def attend(x, scale):
    blocks, triple, span = x.shape
    head_dim = triple // 3
    seq = blocks * span
    return call(
        functools.partial(attend_body, scale=scale, wide=max(span, seq // 2)),
        (
            jax.ShapeDtypeStruct((blocks, head_dim, span), bf16),
            jax.ShapeDtypeStruct((blocks, 1, span), f32),
        ),
        (4 * seq * seq * head_dim, 2 * x.size, seq * seq),
        scratch=(
            pltpu.VMEM((seq, head_dim), bf16),
            pltpu.VMEM((head_dim + 8, seq), bf16),
            pltpu.VMEM((head_dim, seq), bf16),
        ),
    )(x)


def attend_back_body(
    x_ref, do_ref, lse_ref, o_ref, key_ref, keyt_ref, value_ref, dkey_ref, dvalue_ref, *, scale
):
    blocks, triple, span = x_ref.shape
    head_dim = triple // 3
    for n in range(blocks):
        here = slice(n * span, (n + 1) * span)
        key_ref[here, :] = x_ref[n, head_dim : 2 * head_dim, :].T
        keyt_ref[:, here] = x_ref[n, head_dim : 2 * head_dim, :]
        value_ref[here, :] = x_ref[n, 2 * head_dim :, :].T
    for n in range(blocks):
        query = x_ref[n, :head_dim, :] * jnp.asarray(scale, bf16)
        grad = do_ref[n]
        scores = jnp.dot(key_ref[...], query, preferred_element_type=f32)
        probs = jnp.exp(scores - lse_ref[n])
        grad_probs = jnp.dot(value_ref[...], grad, preferred_element_type=f32)
        delta = jnp.sum(probs * grad_probs, axis=0, keepdims=True)
        grad_scores = (probs * (grad_probs - delta)).astype(bf16)
        o_ref[n, :head_dim, :] = (
            jnp.dot(keyt_ref[...], grad_scores, preferred_element_type=f32) * scale
        ).astype(bf16)
        dkey = jnp.dot(grad_scores, query.T, preferred_element_type=f32)
        dvalue = jnp.dot(probs.astype(bf16), grad.T, preferred_element_type=f32)
        if n == 0:
            dkey_ref[...] = dkey
            dvalue_ref[...] = dvalue
        else:
            dkey_ref[...] += dkey
            dvalue_ref[...] += dvalue
    for n in range(blocks):
        here = slice(n * span, (n + 1) * span)
        o_ref[n, head_dim : 2 * head_dim, :] = dkey_ref[here, :].T.astype(bf16)
        o_ref[n, 2 * head_dim :, :] = dvalue_ref[here, :].T.astype(bf16)


def attend_back(x, grad, lse, scale):
    blocks, triple, span = x.shape
    head_dim = triple // 3
    seq = blocks * span
    return call(
        functools.partial(attend_back_body, scale=scale),
        jax.ShapeDtypeStruct(x.shape, bf16),
        (10 * seq * seq * head_dim, 4 * x.size, seq * seq),
        scratch=(
            pltpu.VMEM((seq, head_dim), bf16),
            pltpu.VMEM((head_dim, seq), bf16),
            pltpu.VMEM((seq, head_dim), bf16),
            pltpu.VMEM((seq, head_dim), f32),
            pltpu.VMEM((seq, head_dim), f32),
        ),
    )(x, grad, lse)


def stats(x):
    centered = x - jnp.mean(x, axis=-1, keepdims=True)
    inverse = lax.rsqrt(jnp.mean(centered * centered, axis=-1, keepdims=True) + norm_eps)
    return centered * inverse, inverse


def norm_back(grad_out, gain, hat, inverse):
    grad_hat = grad_out * gain
    return inverse * (
        grad_hat
        - jnp.mean(grad_hat, axis=-1, keepdims=True)
        - hat * jnp.mean(grad_hat * hat, axis=-1, keepdims=True)
    )


def halves(core_ref, part_ref, mine_ref, other_ref):
    half = mine_ref.shape[0]
    core = core_ref[0]
    mine_ref[...] = part_ref[pl.ds(pl.multiple_of(core * half, half), half), :].astype(bf16)
    other_ref[...] = part_ref[pl.ds(pl.multiple_of((1 - core) * half, half), half), :].astype(bf16)


def joined(core_ref, mine_ref, other_ref, whole_ref):
    half = mine_ref.shape[0]
    core = core_ref[0]
    whole_ref[pl.ds(pl.multiple_of(core * half, half), half), :] = mine_ref[...].astype(f32)
    whole_ref[pl.ds(pl.multiple_of((1 - core) * half, half), half), :] = other_ref[...].astype(f32)


def enter_body(pooled_ref, out_ref, lead_ref, gain_ref, qkv_ref, start_ref, normed_ref, packed_ref):
    heads, samples, triple, span = packed_ref.shape
    head_dim = triple // 3
    x = jnp.dot(pooled_ref[...].T, out_ref[...], preferred_element_type=f32)
    for s in range(samples):
        here = slice(s * span, (s + 1) * span)
        start = x[here] + lead_ref[s : s + 1, :]
        start_ref[here, :] = start
        normed_ref[here, :] = (stats(start)[0] * gain_ref[...]).astype(bf16)
    for m in range(3):
        got = jnp.dot(normed_ref[...], qkv_ref[m], preferred_element_type=f32).astype(bf16).T
        for h in range(heads):
            for s in range(samples):
                packed_ref[h, s, m * head_dim : (m + 1) * head_dim, :] = got[
                    h * head_dim : (h + 1) * head_dim, s * span : (s + 1) * span
                ]


def enter(pooled_t, agg_out, lead_rows, gain, qkv, heads):
    width, tokens = pooled_t.shape
    samples = lead_rows.shape[0]
    head_dim = qkv.shape[2] // heads
    return call(
        enter_body,
        (
            jax.ShapeDtypeStruct((tokens, width), f32),
            jax.ShapeDtypeStruct((tokens, width), bf16),
            jax.ShapeDtypeStruct((heads, samples, 3 * head_dim, tokens // samples), bf16),
        ),
        (2 * tokens * width * (width + 3 * qkv.shape[2]), 8 * 2**20, 0),
    )(pooled_t, agg_out, lead_rows, gain, qkv)


def leave_body(core_ref, att_ref, weight_ref, att_t_ref, mine_ref, other_ref, part_ref):
    heads, samples, head_dim, span = att_ref.shape
    for s in range(samples):
        here = slice(s * span, (s + 1) * span)
        for h in range(heads):
            att_t_ref[h * head_dim : (h + 1) * head_dim, here] = att_ref[h, s]
    part_ref[...] = jnp.dot(att_t_ref[...].T, weight_ref[...], preferred_element_type=f32)
    halves(core_ref, part_ref, mine_ref, other_ref)


def leave(core, att, weight):
    heads, samples, head_dim, span = att.shape
    tokens, width = (samples * span, weight.shape[1])
    half = jax.ShapeDtypeStruct((tokens // 2, width), bf16)
    return call(
        leave_body,
        (jax.ShapeDtypeStruct((heads * head_dim, tokens), bf16), half, half),
        (2 * tokens * width * heads * head_dim, 3 * 2**20, 0),
        1,
        2,
        scratch=(pltpu.VMEM((tokens, width), f32),),
    )(core, att, weight)


def feed_body(
    core_ref,
    start_ref,
    mine_ref,
    other_ref,
    gain_ref,
    up_ref,
    grad_active_ref,
    mid_ref,
    normed_ref,
    active_ref,
    grad_hidden_ref,
    out_mine_ref,
    out_other_ref,
    part_ref,
):
    joined(core_ref, mine_ref, other_ref, part_ref)
    step = 128
    for at in range(0, start_ref.shape[0], step):
        here = slice(at, at + step)
        mid = start_ref[here, :] + part_ref[here, :]
        mid_ref[here, :] = mid
        normed = (stats(mid)[0] * gain_ref[...]).astype(bf16)
        normed_ref[here, :] = normed
        hidden = jnp.dot(normed, up_ref[...], preferred_element_type=f32)
        both = 0.5 * (1.0 + lax.erf(hidden * sqrt_half))
        active_ref[here, :] = (hidden * both).astype(bf16)
        slope = both + hidden * jnp.exp(-0.5 * hidden * hidden) * inv_root_two_pi
        grad = (grad_active_ref[here, :].astype(f32) * slope).astype(bf16)
        grad_hidden_ref[here, :] = grad
        part_ref[here, :] = mm(grad, up_ref[...], 1, 1)
    halves(core_ref, part_ref, out_mine_ref, out_other_ref)


def feed(core, start, mine, other, gain, up, grad_active):
    tokens, width = start.shape
    low = jax.ShapeDtypeStruct((tokens, width), bf16)
    wide = jax.ShapeDtypeStruct((tokens, up.shape[1]), bf16)
    half = jax.ShapeDtypeStruct(mine.shape, bf16)
    return call(
        feed_body,
        (jax.ShapeDtypeStruct((tokens, width), f32), low, wide, wide, half, half),
        (4 * tokens * width * up.shape[1], 14 * 2**20, 2 * tokens * up.shape[1]),
        1,
        6,
        scratch=(pltpu.VMEM((tokens, width), f32),),
    )(core, start, mine, other, gain, up, grad_active)


def feed_back_body(
    core_ref,
    mid_ref,
    mine_ref,
    other_ref,
    gain_ref,
    grad_end_ref,
    weight_ref,
    grad_mid_ref,
    grad_att_ref,
    grad_gain_ref,
    packed_ref,
    part_ref,
):
    heads, samples, head_dim, span = packed_ref.shape
    joined(core_ref, mine_ref, other_ref, part_ref)
    grad_gain = jnp.zeros(grad_gain_ref.shape, f32)
    step = 128
    for at in range(0, mid_ref.shape[0], step):
        here = slice(at, at + step)
        hat, inverse = stats(mid_ref[here, :])
        grad_out = part_ref[here, :]
        grad_gain += jnp.sum(grad_out * hat, axis=0, keepdims=True)
        grad = grad_end_ref[here, :].astype(f32) + norm_back(grad_out, gain_ref[...], hat, inverse)
        grad_mid_ref[here, :] = grad
        grad_att_ref[here, :] = grad.astype(bf16)
    grad_gain_ref[...] = grad_gain
    got = mm(weight_ref[...], grad_att_ref[...], 1, 1).astype(bf16)
    for h in range(heads):
        for s in range(samples):
            packed_ref[h, s] = got[h * head_dim : (h + 1) * head_dim, s * span : (s + 1) * span]


def feed_back(core, mid, mine, other, gain, grad_end, weight, heads, samples):
    tokens, width = mid.shape
    return call(
        feed_back_body,
        (
            jax.ShapeDtypeStruct((tokens, width), f32),
            jax.ShapeDtypeStruct((tokens, width), bf16),
            jax.ShapeDtypeStruct((1, width), f32),
            jax.ShapeDtypeStruct(
                (heads, samples, weight.shape[0] // heads, tokens // samples), bf16
            ),
        ),
        (2 * tokens * width * weight.shape[0], 9 * 2**20, 0),
        1,
        6,
        scratch=(pltpu.VMEM((tokens, width), f32),),
    )(core, mid, mine, other, gain, grad_end, weight)


def enter_back_body(core_ref, packed_ref, qkv_ref, flat_ref, mine_ref, other_ref, part_ref):
    heads, samples, triple, span = packed_ref.shape
    head_dim = triple // 3
    width = heads * head_dim
    for m in range(3):
        for h in range(heads):
            for s in range(samples):
                to = m * width + h * head_dim
                flat_ref[to : to + head_dim, s * span : (s + 1) * span] = packed_ref[
                    h, s, m * head_dim : (m + 1) * head_dim, :
                ]
    for m in range(3):
        part = mm(flat_ref[m * width : (m + 1) * width, :].T, qkv_ref[m], 1, 1)
        if m == 0:
            part_ref[...] = part
        else:
            part_ref[...] += part
    halves(core_ref, part_ref, mine_ref, other_ref)


def enter_back(core, packed, qkv):
    heads, samples, triple, span = packed.shape
    tokens, width = (samples * span, qkv.shape[1])
    half = jax.ShapeDtypeStruct((tokens // 2, width), bf16)
    return call(
        enter_back_body,
        (jax.ShapeDtypeStruct((heads * triple, tokens), bf16), half, half),
        (2 * tokens * width * heads * triple, 5 * 2**20, 0),
        1,
        2,
        scratch=(pltpu.VMEM((tokens, width), f32),),
    )(core, packed, qkv)


def pool_back_body(
    at_ref,
    start_ref,
    mine_ref,
    other_ref,
    gain_ref,
    grad_mid_ref,
    out_ref,
    my_pooled_ref,
    hot_ref,
    gain_two_ref,
    grad_agg_ref,
    extra_ref,
    pooled_ref,
    out_mine_ref,
    out_other_ref,
    part_ref,
    grad_out_ref,
):
    samples = hot_ref.shape[1]
    tokens, width = start_ref.shape
    joined(at_ref, mine_ref, other_ref, part_ref)
    grad_gain = jnp.zeros((1, width), f32)
    step = min(128, tokens // samples)
    sums = [jnp.zeros((1, width), f32) for _ in range(samples)]
    for at in range(0, tokens, step):
        here = slice(at, at + step)
        hat, inverse = stats(start_ref[here, :])
        grad_out = part_ref[here, :]
        grad_gain += jnp.sum(grad_out * hat, axis=0, keepdims=True)
        grad = grad_mid_ref[here, :] + norm_back(grad_out, gain_ref[...], hat, inverse)
        sums[at * samples // tokens] += jnp.sum(grad, axis=0, keepdims=True)
        grad_agg_ref[here, :] = grad.astype(bf16)
    leads = hot_ref.shape[0]
    row = lax.broadcasted_iota(jnp.int32, (leads, width), 0)
    extra = jnp.where(row == leads - 2, grad_gain, 0.0)
    extra = extra + jnp.where(row == leads - 1, gain_two_ref[...], 0.0)
    for s in range(samples):
        extra = extra + hot_ref[:, s : s + 1] * sums[s]
    extra_ref[...] = extra
    pooled_ref[...] = mm(out_ref[...], grad_agg_ref[...], 1, 1).astype(bf16)
    grad_out_ref[...] = jnp.dot(
        my_pooled_ref[...], grad_agg_ref[...], preferred_element_type=f32
    ).astype(bf16)
    split_into(grad_out_ref, at_ref[1], at_ref[2], out_mine_ref, out_other_ref)


def pool_back(at, start, mine, other, gain, grad_mid, agg_out, my_pooled, hot, gain_two):
    tokens, width = start.shape
    half = jax.ShapeDtypeStruct((my_pooled.shape[0], width // 2), bf16)
    return call(
        pool_back_body,
        (
            jax.ShapeDtypeStruct((tokens, width), bf16),
            jax.ShapeDtypeStruct((hot.shape[0], width), f32),
            jax.ShapeDtypeStruct((width, tokens), bf16),
            half,
            half,
        ),
        (3 * tokens * width * width, 9 * 2**20, 0),
        1,
        9,
        scratch=(
            pltpu.VMEM((tokens, width), f32),
            pltpu.VMEM((my_pooled.shape[0], width), bf16),
        ),
    )(at, start, mine, other, gain, grad_mid, agg_out, my_pooled, hot, gain_two)


def strips_body(place_ref, *refs, dims):
    mine_ref, other_ref = refs[-2:]
    step = pl.program_id(0)
    count = pl.num_programs(0) // 2

    def fill(o_ref):
        at = 0
        for left_ref, right_ref, dim in zip(refs[:-2:2], refs[1:-2:2], dims):
            wide = right_ref.shape[1 - dim]
            o_ref[:, at : at + wide] = mm(left_ref[...], right_ref[...], 0, dim).astype(bf16)
            at += wide

    @pl.when(step < count)
    def _():
        fill(other_ref)

    @pl.when(step >= count)
    def _():
        fill(mine_ref)


def strips(place, *pairs):
    tokens, width = pairs[0][0].shape
    block = 128
    count = width // block // 2
    wide = sum(right.shape[1 - dim] for _, right, dim in pairs)

    def left_map(i, place_ref):
        own = i // count
        side = place_ref[0] * own + (1 - place_ref[0]) * (1 - own)
        return (0, 2 * jnp.bitwise_xor(i % count, place_ref[1]) + side)

    specs = []
    for left, right, _ in pairs:
        specs.append(pl.BlockSpec((tokens, block), left_map))
        specs.append(pl.BlockSpec(right.shape, lambda i, place_ref: (0, 0)))
    half = jax.ShapeDtypeStruct((width // 2, wide), bf16)
    return pl.pallas_call(
        functools.partial(strips_body, dims=[dim for _, _, dim in pairs]),
        out_shape=(half, half),
        grid_spec=pltpu.PrefetchScalarGridSpec(
            num_scalar_prefetch=1,
            grid=(2 * count,),
            in_specs=specs,
            out_specs=(
                pl.BlockSpec((block, wide), lambda i, p: (jnp.maximum(i - count, 0), 0)),
                pl.BlockSpec((block, wide), lambda i, p: (jnp.minimum(i, count - 1), 0)),
            ),
        ),
        compiler_params=pltpu.CompilerParams(vmem_limit_bytes=vmem_most),
        cost_estimate=pl.CostEstimate(
            flops=tokens * width * wide // 32, bytes_accessed=width * wide // 16, transcendentals=0
        ),
    )(place, *[x for pair in pairs for x in pair[:2]])


def rows_total(refs, columns=slice(None)):
    total = refs[0][:, columns].astype(f32)
    for ref in refs[1:]:
        total = total + ref[:, columns].astype(f32)
    return total


def finish_body(*refs, parts):
    up, down, mid, end = [refs[n * parts : (n + 1) * parts] for n in range(4)]
    up_ref, down_ref, out_ref, qkv_ref, head_ref = refs[4 * parts :]
    local = out_ref.shape[0]
    up_ref[...] = rows_total(up)
    out_ref[...] = rows_total(mid, slice(2 * local, 3 * local)).T
    down_ref[...] = rows_total(down).T
    for m in range(2):
        qkv_ref[m] = rows_total(mid, slice(m * local, (m + 1) * local))
    qkv_ref[2] = rows_total(end, slice(0, local))
    head_ref[...] = rows_total(end, slice(local, end[0].shape[1])).T[: head_ref.shape[0]]


def finish(groups, local, head_rows):
    up, down = groups[:2]
    block, hidden = up[0].shape
    f32s = lambda *shape: jax.ShapeDtypeStruct(shape, f32)
    return call(
        functools.partial(finish_body, parts=len(up)),
        (
            f32s(block, hidden),
            f32s(hidden, block),
            f32s(local, block),
            f32s(3, block, local),
            f32s(head_rows, block),
        ),
        (0, 8 * 2**20, 0),
    )(*[x for group in groups for x in group])


def finish_late_body(*refs, parts):
    agg_ref, value_ref, patch_ref, bias_ref, query_ref, lead_ref, gain_ref = refs[parts:]
    total = rows_total(refs[:parts])
    at = agg_ref.shape[0]
    agg_ref[...] = total[:at]
    value_ref[...] = total[at : at + value_ref.shape[0]]
    at += value_ref.shape[0]
    my_chans = bias_ref.shape[0]
    patch_ref[...] = total[at : at + 16 * my_chans].reshape(patch_ref.shape)
    bias_ref[...] = total[at + 16 * my_chans : at + 17 * my_chans]
    at += -(-17 * my_chans // 16) * 16
    query_ref[...] = total[at : at + query_ref.shape[0]]
    lead_ref[...] = total[at + 16 : at + 16 + lead_ref.shape[0]]
    gain_ref[...] = total[at + 16 + lead_ref.shape[0] :]


def finish_late(late, local, my_chans, my_heads, leads):
    block = late[0].shape[1]
    f32s = lambda *shape: jax.ShapeDtypeStruct(shape, f32)
    return call(
        functools.partial(finish_late_body, parts=len(late)),
        (
            f32s(local, block),
            f32s(local, block),
            f32s(my_chans, 16, block),
            f32s(my_chans, block),
            f32s(my_heads, block),
            f32s(leads, block),
            f32s(8, block),
        ),
        (0, 2**20, 0),
    )(*late)


def close_body(canvas_ref, before_ref, after_ref, o_ref):
    samples, chans, cols, _ = o_ref.shape
    for s in range(samples):
        for col in range(cols):
            piece = canvas_ref[s, col + 1, :chans]
            if col == 0:
                piece = piece + before_ref[s, :chans].astype(f32)
            if col == cols - 1:
                piece = piece + after_ref[s, :chans].astype(f32)
            o_ref[s, :, col, :] = piece


def close_kernel(canvas, rims, chans):
    samples, wide, _, rows = canvas.shape
    return call(
        close_body,
        jax.ShapeDtypeStruct((samples, chans, wide - 2, rows), f32),
        (0, 2**20, 0),
    )(canvas, *rims)


def attend_gathered(packed, scale):
    head_dim = packed.shape[2] // 3
    whole = lax.all_gather(packed[:, :, head_dim:, :], "sector", axis=0)
    keys, values = (whole[:, :, :, :head_dim], whole[:, :, :, head_dim:])
    scores = (
        jnp.einsum("hsdq,nhsdk->hsqnk", packed[:, :, :head_dim], keys, preferred_element_type=f32)
        * scale
    )
    most = jnp.max(scores, axis=(3, 4), keepdims=True)
    raised = jnp.exp(scores - most)
    total = jnp.sum(raised, axis=(3, 4), keepdims=True)
    probs = (raised / total).astype(bf16)
    out = jnp.einsum("hsqnk,nhsdk->hsdq", probs, values, preferred_element_type=f32)
    return out.astype(bf16), most + jnp.log(total)


def attend_back_gathered(packed, grad, lse, scale):
    head_dim = packed.shape[2] // 3
    query = packed[:, :, :head_dim]
    whole = lax.all_gather(packed[:, :, head_dim:, :], "sector", axis=0)
    keys, values = (whole[:, :, :, :head_dim], whole[:, :, :, head_dim:])
    scores = jnp.einsum("hsdq,nhsdk->hsqnk", query, keys, preferred_element_type=f32) * scale
    probs = jnp.exp(scores - lse)
    grad_probs = jnp.einsum("hsdq,nhsdk->hsqnk", grad, values, preferred_element_type=f32)
    delta = jnp.sum(probs * grad_probs, axis=(3, 4), keepdims=True)
    grad_scores = (probs * (grad_probs - delta)).astype(bf16)
    grad_query = jnp.einsum("hsqnk,nhsdk->hsdq", grad_scores, keys, preferred_element_type=f32)
    grad_keys = jnp.einsum("hsqnk,hsdq->nhsdk", grad_scores, query, preferred_element_type=f32)
    grad_values = jnp.einsum(
        "hsqnk,hsdq->nhsdk", probs.astype(bf16), grad, preferred_element_type=f32
    )
    both = lax.psum_scatter(
        jnp.concatenate([grad_keys * scale, grad_values], axis=3), "sector", scatter_dimension=0
    )
    return jnp.concatenate([grad_query * scale, both], axis=2).astype(bf16)


def swap(x, axis, bit):
    size = lax.axis_size(axis)
    return lax.ppermute(x, axis, [(i, i ^ bit) for i in range(size)])


def rounded(x):
    return lax.reduce_precision(x, 8, 7)


def sum_over_mp(x):
    if lax.axis_size("mp") != 4:
        return lax.psum(x.astype(bf16), "mp").astype(f32)
    half = x.shape[0] // 2
    low, high = (rounded(x[:half]), rounded(x[half:]))
    first = lax.axis_index("mp") % 2 == 0
    mine, other = (jnp.where(first, low, high), jnp.where(first, high, low))
    mine = rounded(mine + swap(other.astype(bf16), "mp", 1).astype(f32))
    mine = rounded(mine + swap(mine.astype(bf16), "mp", 2).astype(f32))
    other = swap(mine.astype(bf16), "mp", 1).astype(f32)
    return jnp.concatenate([jnp.where(first, mine, other), jnp.where(first, other, mine)], axis=0)


def near_sum(mine, other):
    return rounded(mine.astype(f32) + swap(other, "mp", 1).astype(f32)).astype(bf16)


def far_sum(mine, got):
    mine = rounded(mine.astype(f32) + got.astype(f32)).astype(bf16)
    return mine, swap(mine, "mp", 1)


def ring_pair(leading, last):
    size = lax.axis_size("sector")
    up = [(i, (i + 1) % size) for i in range(size)]
    down = [(j, i) for i, j in up]
    return lax.ppermute(last, "sector", up), lax.ppermute(leading, "sector", down)


def split_cols(x, block):
    even = lax.axis_index("sector") % 2 == 0
    pairs = x.shape[1] // (2 * block)
    low = [x[:, 2 * p * block : (2 * p + 1) * block] for p in range(pairs)]
    high = [x[:, (2 * p + 1) * block : (2 * p + 2) * block] for p in range(pairs)]
    mine = [jnp.where(even, a, b) for a, b in zip(low, high)]
    other = [jnp.where(even, b, a) for a, b in zip(low, high)]
    return jnp.concatenate(mine, axis=1), jnp.concatenate(other, axis=1)


def pair_sum(mine, got):
    return (mine.astype(f32) + got.astype(f32)).astype(bf16)


def line_parts(pieces):
    return [pieces[0]] + [swap(pieces[n], "sector", 2 * n) for n in range(1, len(pieces))]


def norm_forward(values, gain_vec):
    row_mean = jnp.mean(values, axis=-1, keepdims=True)
    centered = values - row_mean
    inverse = lax.rsqrt(jnp.mean(centered * centered, axis=-1, keepdims=True) + norm_eps)
    normed = centered * inverse
    return (normed * gain_vec, normed, inverse)


def norm_backward(grad_out, gain_vec, normed, inverse):
    grad_normed = grad_out * gain_vec
    grad_gain = jnp.sum(grad_out * normed, axis=0)
    grad_in = inverse * (
        grad_normed
        - jnp.mean(grad_normed, axis=-1, keepdims=True)
        - normed * jnp.mean(grad_normed * normed, axis=-1, keepdims=True)
    )
    return (grad_in, grad_gain)


def gelu_slope(values):
    return (
        0.5 * (1.0 + lax.erf(values * sqrt_half))
        + values * jnp.exp(-0.5 * values * values) * inv_root_two_pi
    )


def mp_slice(values, axis_dim, mp_index, mp_count):
    piece_len = values.shape[axis_dim] // mp_count
    return lax.dynamic_slice_in_dim(values, mp_index * piece_len, piece_len, axis_dim)


def shards(
    input_field,
    present_mask,
    lead_index,
    patch_weight,
    patch_bias,
    agg_query,
    agg_value,
    agg_out,
    lead_table,
    norm1_gain,
    qkv_weight,
    attn_out_weight,
    norm2_gain,
    up_weight,
    down_weight,
    head_weight,
    pred_cotangent,
):
    samples, chans, pix_rows, pix_cols = input_field.shape
    rows, cols = (pix_rows // 2, pix_cols // 2)
    span = rows * cols
    tokens = samples * span
    width = patch_weight.shape[2]
    heads = agg_query.shape[0]
    head_dim = width // heads
    local_width = qkv_weight.shape[2]
    local_heads = local_width // head_dim
    sectors = lax.axis_size("sector")
    mp_count = lax.axis_size("mp")
    mp_index = lax.axis_index("mp")
    score_scale = head_dim ** (-0.5)
    depth = 17 * chans
    group = 16 if chans % 16 == 0 else chans
    groups = chans // group

    by_head = sectors == local_heads * samples
    block = width // sectors
    fast = by_head and block == 128 and sectors == 8 and mp_count == 4 and samples % 2 == 0 and span % 128 == 0
    exchange = lambda x: lax.all_to_all(
        x.reshape(sectors, x.shape[-2], x.shape[-1]), "sector", 0, 0, tiled=True
    )
    by_pair = lambda x: x.reshape(local_heads, samples, x.shape[1], x.shape[2])
    sector = lax.axis_index("sector")
    core = jnp.stack([mp_index % 2, sector % 2, sector // 2])
    whereabouts = core[1:]
    counts = range(width // block // 2)
    row_sums = lambda a, b: [
        pair_sum(a[n * block : (n + 1) * block], b[n * block : (n + 1) * block]) for n in counts
    ]
    lane_sums = lambda a, b: [
        pair_sum(a[:, n * block : (n + 1) * block], b[:, n * block : (n + 1) * block])
        for n in counts
    ]
    across = lambda x: swap(x, "mp", 2)
    beside = lambda x: swap(x, "sector", 1)
    barrier = lax.optimization_barrier

    fields = jnp.transpose(input_field, (0, 3, 1, 2))
    cots = jnp.transpose(pred_cotangent, (0, 3, 1, 2))
    before, after = ring_pair(
        jnp.stack([fields[:, 0], cots[:, 0]]), jnp.stack([fields[:, -1], cots[:, -1]])
    )
    haloed = lambda x, n: jnp.concatenate([before[n][:, None], x, after[n][:, None]], axis=1)
    win = windows(haloed(fields, 0), group)

    weight_kv = jnp.concatenate(
        [
            jnp.transpose(patch_weight.reshape(groups, group, 16, width), (0, 2, 1, 3)).reshape(
                16 * chans, width
            ),
            patch_bias,
        ],
        axis=0,
    )
    key_map_t = mm(agg_query, weight_kv, 1, 1)
    value_map = jnp.dot(weight_kv, agg_value, preferred_element_type=f32).astype(bf16)
    mask = jnp.broadcast_to(
        jnp.transpose(present_mask)[:, :, None], (chans, samples, span)
    ).reshape(chans, tokens)
    probs, pooled_t = agg_forward(win, key_map_t, value_map, mask, group)
    lead_hot = (lead_index[:, None] == jnp.arange(lead_table.shape[0])[None, :]).astype(f32)
    lead_rows = jnp.dot(lead_hot, lead_table.astype(f32), precision=highest)

    head_cols = head_weight.shape[1]
    spot = lax.broadcasted_iota(jnp.int32, (head_cols, head_cols), 1)
    source = lax.broadcasted_iota(jnp.int32, (head_cols, head_cols), 0)
    place = (spot % (16 * group)) // group
    shuffle = ((spot // (16 * group) * group + spot % group) * 16 + place == source).astype(bf16)
    head_kv = jnp.dot(head_weight, shuffle, preferred_element_type=f32).astype(bf16)
    grad_head_t = windows(haloed(cots, 1), group)
    grad_end = mm(grad_head_t, head_kv, 0, 1)
    grad_mlp = grad_end.astype(bf16)
    grad_active = mm(grad_mlp, down_weight, 1, 1)

    my_chans = chans // mp_count
    my_heads = heads // mp_count
    spots = lambda var, k: (var // group * 16 + k) * group + var % group

    def ext_place(row):
        main = row < 16 * my_chans
        var = mp_index * my_chans + jnp.where(main, row // 16, row - 16 * my_chans)
        return jnp.where(main, spots(var, row % 16), 16 * chans + var)

    head_rows = -(-16 * my_chans // 128) * 128
    my_head = jnp.dot(
        one_hot(head_rows, 16 * chans, ext_place, lambda row: row < 16 * my_chans),
        grad_head_t,
        preferred_element_type=f32,
    ).astype(bf16)
    my_pooled = mp_slice(pooled_t, 0, mp_index, mp_count)

    if fast:
        qkv = jnp.transpose(qkv_weight, (1, 0, 2))
        start_x, normed1_low, packed = enter(
            pooled_t, agg_out, lead_rows, norm1_gain[None], qkv, local_heads
        )
        held = exchange(packed)
        held, grad_active, grad_mlp, my_pooled = barrier(
            (held, grad_active.astype(bf16), grad_mlp, my_pooled)
        )
        att_held, lse = attend(held, score_scale)
        att_t, mine, other = leave(core, by_pair(exchange(att_held)), attn_out_weight)
        mine = near_sum(mine, other)
        mid_x, normed2_low, active_low, grad_hidden, mine, other = feed(
            core,
            start_x,
            *far_sum(mine, across(mine)),
            norm2_gain[None],
            up_weight,
            grad_active,
        )
        mine = near_sum(mine, other)
        down_mine, down_other = strips(whereabouts, (grad_mlp, active_low, 0))
        low = jnp.dot(active_low, down_weight, preferred_element_type=f32).astype(bf16)
        first = mp_index % 2 == 0
        low, high = (low[: tokens // 2], low[tokens // 2 :])
        end_mine = near_sum(jnp.where(first, low, high), jnp.where(first, high, low))
        up_mine, up_other = strips(whereabouts, (normed2_low, grad_hidden, 0))
        down_got = beside(down_other)
        got, down_mine, up_mine, end_mine = barrier((across(mine), down_mine, up_mine, end_mine))
        grad_mid, grad_att, grad_gain_two, grad_heads = feed_back(
            core,
            mid_x,
            *far_sum(mine, got),
            norm2_gain[None],
            grad_mlp,
            attn_out_weight,
            local_heads,
            samples,
        )
        down_pair = row_sums(down_mine, down_got)
        grad_att_held, down_pair, up_other = barrier(
            (exchange(grad_heads), down_pair, up_other)
        )
        down_parts = line_parts(down_pair)
        up_got = beside(up_other)
        grad_held = attend_back(held, grad_att_held, lse, score_scale)
        end_got, down_parts, up_got, grad_att, grad_held = barrier(
            (across(end_mine), down_parts, up_got, grad_att, grad_held)
        )
        out_mine, out_other = strips(whereabouts, (grad_att, att_t, 1))
        out_got = beside(out_other)
        near, far = far_sum(end_mine, end_got)
        end_x = mid_x + jnp.concatenate(
            [jnp.where(first, near, far), jnp.where(first, far, near)], axis=0
        ).astype(f32)
        grad_packed = exchange(grad_held)
    else:
        start_x = (
            mm(pooled_t, agg_out, 0, 0).reshape(samples, span, width) + lead_rows[:, None, :]
        ).reshape(tokens, width)
        normed1, hat_one, inv_one = norm_forward(start_x, norm1_gain)
        normed1_low = normed1.astype(bf16)
        qkv_t = lax.dot_general(
            qkv_weight, normed1_low, (((0,), (1,)), ((), ())), preferred_element_type=f32
        ).astype(bf16)
        packed = jnp.transpose(
            qkv_t.reshape(3, local_heads, head_dim, samples, span), (1, 3, 0, 2, 4)
        ).reshape(local_heads, samples, 3 * head_dim, span)
        att, lse = attend_gathered(packed, score_scale)
        att_t = jnp.transpose(att, (0, 2, 1, 3)).reshape(local_width, tokens)
        mid_x = start_x + sum_over_mp(mm(att_t, attn_out_weight, 0, 0))
        normed2, hat_two, inv_two = norm_forward(mid_x, norm2_gain)
        normed2_low = normed2.astype(bf16)
        hidden = jnp.dot(normed2_low, up_weight, preferred_element_type=f32)
        active_low = jax.nn.gelu(hidden, approximate=False).astype(bf16)
        grad_hidden = (grad_active * gelu_slope(hidden)).astype(bf16)
        grad_normed2 = sum_over_mp(mm(grad_hidden, up_weight, 1, 1))
        grad_mid_norm, grad_gain_two = norm_backward(grad_normed2, norm2_gain, hat_two, inv_two)
        grad_mid = grad_end + grad_mid_norm
        grad_att = grad_mid.astype(bf16)
        grad_heads_t = mm(attn_out_weight, grad_att, 1, 1).astype(bf16)
        grad_heads = jnp.transpose(
            grad_heads_t.reshape(local_heads, head_dim, samples, span), (0, 2, 1, 3)
        )
        grad_packed = attend_back_gathered(packed, grad_heads, lse, score_scale)
        end_x = mid_x + sum_over_mp(jnp.dot(active_low, down_weight, preferred_element_type=f32))

    end_low = end_x.astype(bf16)
    head_out = mm(head_kv, end_low, 0, 1).astype(bf16)
    canvas, edges = fold(head_out, samples, cols, pix_rows, group)

    def close(canvas, rims):
        inner = canvas[:, 1:-1]
        inner = inner.at[:, 0].add(rims[0].astype(f32))
        return jnp.transpose(inner.at[:, -1].add(rims[1].astype(f32)), (0, 2, 3, 1))

    leads = lead_table.shape[0]

    if fast:
        joint = lambda *x: jnp.concatenate(x, axis=0)
        up_parts = line_parts(row_sums(up_mine, up_got))
        rims = ring_pair(edges[0], edges[1])
        grad_packed, rims, out_got = barrier((grad_packed, rims, out_got))
        out_pair = row_sums(out_mine, out_got)
        flat, mine, other = enter_back(core, by_pair(grad_packed), qkv)
        mine = near_sum(mine, other)
        part = 2 * local_width
        mid_mine, mid_other = strips(whereabouts, (normed1_low, flat[:part], 1))
        mid_got = beside(mid_other)
        end_mine, end_other = strips(
            whereabouts, (normed1_low, flat[part:], 1), (end_low, my_head, 1)
        )
        end_got = beside(end_other)
        got, mid_mine, end_mine, up_parts = barrier((across(mine), mid_mine, end_mine, up_parts))
        hot = jnp.zeros((leads + 8, samples), f32).at[:leads].set(jnp.transpose(lead_hot))
        grad_agg, extra, grad_pooled_t, agg_mine, agg_other = pool_back(
            core,
            start_x,
            *far_sum(mine, got),
            norm1_gain[None],
            grad_mid,
            agg_out,
            my_pooled,
            hot,
            grad_gain_two,
        )
        mid_got, out_pair, grad_pooled_t = barrier((mid_got, out_pair, grad_pooled_t))
        mid_pair = [
            jnp.concatenate(x, axis=1) for x in zip(row_sums(mid_mine, mid_got), out_pair)
        ]
        mid_parts = line_parts(mid_pair)
        grad_canvas, grad_edges, late_mine, late_other = agg_last(
            jnp.stack([mp_index, sector % 2, sector // 2]),
            win,
            probs,
            grad_pooled_t,
            value_map,
            key_map_t,
            weight_kv,
            agg_value,
            agg_query,
            extra,
            samples,
            cols,
            mp_count,
        )
        late_other, grad_edges, mid_parts, end_got = barrier(
            (late_other, grad_edges, mid_parts, end_got)
        )
        end_parts = line_parts(row_sums(end_mine, end_got))
        grad_rims = ring_pair(grad_edges[0], grad_edges[1])
        late_got, grad_rims = barrier((beside(late_other), grad_rims))
        agg_pair = lane_sums(agg_mine, beside(agg_other))
        late_pair = lane_sums(late_mine, late_got)
        late_parts = line_parts([jnp.concatenate(x, axis=0) for x in zip(agg_pair, late_pair)])
        outs = finish(
            (up_parts, down_parts, mid_parts, end_parts), local_width, 16 * my_chans
        )
        prediction = close_kernel(canvas, rims, chans)
        field_grad = close_kernel(grad_canvas, grad_rims, my_chans)
        late_parts, outs, prediction, field_grad = barrier(
            (late_parts, outs, prediction, field_grad)
        )
        up_sum, down_sum, out_sum, qkv_sum, head_sum = outs
        qkv_sum = jnp.transpose(qkv_sum, (1, 0, 2))
        head_sum = jnp.transpose(head_sum)
        prediction, field_grad = [jnp.transpose(x, (0, 1, 3, 2)) for x in (prediction, field_grad)]
        agg_out_sum, value_sum, patch_sum, bias_sum, query_sum, lead_sum, gain_sums = finish_late(
            late_parts, local_width, my_chans, my_heads, leads
        )
        one_sum, two_sum = (gain_sums[6:7], gain_sums[7:8])
    else:
        prediction = close(canvas, ring_pair(edges[0], edges[1]))
        flat = jnp.transpose(
            grad_packed.reshape(local_heads, samples, 3, head_dim, span), (2, 0, 3, 1, 4)
        ).reshape(3 * local_width, tokens)
        grad_normed1 = sum_over_mp(
            lax.dot_general(
                flat.reshape(3, local_width, tokens),
                qkv_weight,
                (((0, 1), (1, 2)), ((), ())),
                preferred_element_type=f32,
            )
        )
        grad_start_norm, grad_gain_one = norm_backward(grad_normed1, norm1_gain, hat_one, inv_one)
        grad_start = grad_mid + grad_start_norm
        grad_agg = grad_start.astype(bf16)
        sample_sums = jnp.sum(grad_start.reshape(samples, span, width), axis=1)
        grad_pooled_t = mm(agg_out, grad_agg, 1, 1).astype(bf16)
        grad_lead = jnp.einsum("sl,sd->ld", lead_hot, sample_sums, precision=highest)
        gains = [x.reshape(1, width) for x in (grad_gain_one, grad_gain_two)]
        grad_win, value_grad_t, key_grad = agg_backward(
            win, probs, grad_pooled_t, value_map, key_map_t
        )
        key_low = key_grad.astype(bf16)
        grad_agg_value = mm(mp_slice(weight_kv, 1, mp_index, mp_count), value_grad_t, 0, 1)
        select = one_hot(17 * my_chans, depth, ext_place)
        my_value = mm(select, value_grad_t, 1, 1).astype(bf16)
        my_key = mm(select, key_low, 1, 1).astype(bf16)
        grad_ext = mm(my_value, agg_value, 1, 1) + jnp.dot(
            my_key, agg_query, preferred_element_type=f32
        )
        grad_agg_query = jnp.dot(
            mp_slice(key_low, 0, mp_index, mp_count), weight_kv, preferred_element_type=f32
        )
        grad_canvas, grad_edges = fold(grad_win, samples, cols, pix_rows, group)
        grad_edges = mp_slice(grad_edges, 2, mp_index, mp_count)
        field_grad = close(
            mp_slice(grad_canvas, 2, mp_index, mp_count), ring_pair(grad_edges[0], grad_edges[1])
        )
        put = lambda x, dim: lax.psum_scatter(x, "sector", scatter_dimension=dim, tiled=True)
        up_sum = put(mm(normed2_low, grad_hidden, 0, 0), 0)
        down_sum = put(mm(active_low, grad_mlp, 0, 0), 1)
        out_sum = put(jnp.dot(att_t, grad_att, preferred_element_type=f32), 1)
        head_sum = put(mm(end_low, my_head[: 16 * my_chans], 0, 1), 0)
        qkv_sum = put(mm(normed1_low, flat, 0, 1), 0).reshape(block, 3, local_width)
        agg_out_sum = put(jnp.dot(my_pooled, grad_agg, preferred_element_type=f32), 1)
        late = [grad_agg_value, grad_ext, grad_agg_query, grad_lead] + gains
        value_sum, ext_sum, query_sum, lead_sum, one_sum, two_sum = [put(x, 1) for x in late]
        patch_sum = ext_sum[: 16 * my_chans].reshape(my_chans, 16, block)
        bias_sum = ext_sum[16 * my_chans :]
    return (
        prediction,
        field_grad,
        patch_sum,
        bias_sum,
        query_sum,
        value_sum,
        agg_out_sum,
        lead_sum,
        one_sum[0],
        qkv_sum,
        out_sum,
        two_sum[0],
        up_sum,
        down_sum,
        head_sum,
    )


def solution(mesh):
    placed = (
        P(None, None, None, "sector"),
        P(),
        P(),
        P(),
        P(),
        P(),
        P(),
        P(),
        P(),
        P(),
        P(None, None, "mp"),
        P("mp", None),
        P(),
        P(None, "mp"),
        P("mp", None),
        P(),
        P(None, None, None, "sector"),
    )
    return jax.shard_map(
        shards,
        mesh=mesh,
        in_specs=placed,
        out_specs=(
            P(None, None, None, "sector"),
            P(None, "mp", None, "sector"),
            P("mp", None, "sector"),
            P("mp", "sector"),
            P("mp", "sector"),
            P("mp", "sector"),
            P("mp", "sector"),
            P(None, "sector"),
            P("sector"),
            P("sector", None, "mp"),
            P("mp", "sector"),
            P("sector"),
            P("sector", "mp"),
            P("mp", "sector"),
            P("sector", "mp"),
        ),
        check_vma=False,
    )
```

```python
import functools

import jax
import jax.numpy as jnp
from jax import lax
from jax.experimental import pallas as pl
from jax.experimental.pallas import tpu as pltpu
from jax.sharding import PartitionSpec as P

bf16 = jnp.bfloat16
f32 = jnp.float32
highest = lax.Precision.HIGHEST
norm_eps = 1e-05
sqrt_half = 0.7071067811865476
inv_root_two_pi = 0.3989422804014327
vmem_most = 44 * 1024 * 1024


def mm(left, right, left_dim, right_dim):
    return lax.dot_general(
        left, right, (((left_dim,), (right_dim,)), ((), ())), preferred_element_type=f32
    )


def call(body, out_shape, cost, scalars=0, tensors=0, scratch=()):
    more = {}
    if scalars:
        more = dict(
            in_specs=[pl.BlockSpec(memory_space=pltpu.SMEM)] * scalars
            + [pl.BlockSpec(memory_space=pltpu.VMEM)] * tensors
        )
    return pl.pallas_call(
        body,
        out_shape=out_shape,
        scratch_shapes=list(scratch),
        compiler_params=pltpu.CompilerParams(vmem_limit_bytes=vmem_most),
        cost_estimate=pl.CostEstimate(
            flops=int(cost[0]) // 64, bytes_accessed=int(cost[1]) // 64, transcendentals=int(cost[2]) // 64
        ),
        **more,
    )


def row_pick(rows, patch_rows, patch_cols):
    span = patch_rows * patch_cols
    lane = lax.broadcasted_iota(jnp.int32, (rows, 4 * span), 1)
    row = lax.broadcasted_iota(jnp.int32, (rows, 4 * span), 0)
    r = lane // span
    rest = lane - r * span
    j = rest // patch_rows
    i = rest - j * patch_rows
    return (row == 2 * i + r - 1), j


def windows_body(x_ref, o_ref, *, group):
    samples, wide, chans, rows = x_ref.shape
    cols, patch_rows = (wide - 2) // 2, rows // 2
    span = cols * patch_rows
    hit, lane_col = row_pick(rows, patch_rows, cols)
    total = None
    for j in range(cols):
        left = jnp.concatenate(
            [x_ref[s, 2 * j + c] for s in range(samples) for c in range(4)], axis=0
        )
        pick = jnp.where(hit & (lane_col == j), 1.0, 0.0).astype(bf16)
        part = jnp.dot(left, pick, preferred_element_type=f32)
        total = part if total is None else total + part
    for s in range(samples):
        for c in range(4):
            for g in range(chans // group):
                at = (s * 4 + c) * chans + g * group
                for r in range(4):
                    to = (g * 16 + r * 4 + c) * group
                    o_ref[to : to + group, s * span : (s + 1) * span] = total[
                        at : at + group, r * span : (r + 1) * span
                    ].astype(o_ref.dtype)


def windows(x, group):
    samples, wide, chans, rows = x.shape
    tokens = samples * (wide - 2) * rows // 4
    return call(
        functools.partial(windows_body, group=group),
        jax.ShapeDtypeStruct((16 * chans, tokens), bf16),
        (2 * 16 * chans * tokens * 512, 4 * 16 * chans * tokens, 0),
    )(x)


def fold_rows(g_ref, o_ref, cols, group):
    samples, _, chans, rows = o_ref.shape
    span = cols * rows // 2
    hit, lane_col = row_pick(rows, rows // 2, cols)

    def block(s, c, r):
        parts = []
        for g in range(chans // group):
            at = (g * 16 + r * 4 + c) * group
            parts.append(g_ref[at : at + group, s * span : (s + 1) * span])
        return jnp.concatenate(parts, axis=0)

    left = jnp.concatenate(
        [
            jnp.concatenate([block(s, c, r) for r in range(4)], axis=1)
            for s in range(samples)
            for c in range(4)
        ],
        axis=0,
    )
    held = [[None] * (2 * cols + 2) for _ in range(samples)]
    for j in range(cols):
        pick = jnp.where(hit & (lane_col == j), 1.0, 0.0).astype(bf16)
        part = mm(left, pick, 1, 1)
        for s in range(samples):
            for c in range(4):
                at = (s * 4 + c) * chans
                piece = part[at : at + chans]
                before = held[s][2 * j + c]
                held[s][2 * j + c] = piece if before is None else before + piece
    for s in range(samples):
        for col in range(2 * cols + 2):
            o_ref[s, col] = held[s][col]


def fold_body(g_ref, o_ref, edge_ref, *, cols, group):
    fold_rows(g_ref, o_ref, cols, group)
    edge_ref[0] = o_ref[:, 0].astype(bf16)
    edge_ref[1] = o_ref[:, 2 * cols + 1].astype(bf16)


def fold(g, samples, cols, rows, group):
    chans, tokens = (g.shape[0] // 16, g.shape[1])
    return call(
        functools.partial(fold_body, cols=cols, group=group),
        (
            jax.ShapeDtypeStruct((samples, 2 * cols + 2, chans, rows), f32),
            jax.ShapeDtypeStruct((2, samples, chans, rows), bf16),
        ),
        (2 * 16 * chans * tokens * 512, 4 * 16 * chans * tokens, 0),
    )(g)


def own_lane(rows, lanes, group):
    row = lax.broadcasted_iota(jnp.int32, (rows, lanes), 0)
    lane = lax.broadcasted_iota(jnp.int32, (rows, lanes), 1)
    return row % group == lane % group


def agg_forward_body(win_ref, key_ref, value_ref, mask_ref, probs_ref, pooled_ref):
    groups, heads, group, lanes = probs_ref.shape
    inner = win_ref.shape[0] // groups
    head_dim = pooled_ref.shape[0] // heads
    own = own_lane(heads * group, inner, group)
    own_bias = own_lane(heads * group, group, group)
    spread = lambda x: jnp.broadcast_to(x[:, None, :], (heads, group, x.shape[1])).reshape(
        heads * group, x.shape[1]
    )
    scores = []
    for g in range(groups):
        keys = spread(key_ref[:, g * inner : (g + 1) * inner])
        keys = jnp.where(own, keys, 0.0)
        high = keys.astype(bf16)
        rest = keys - high.astype(f32)
        mid = rest.astype(bf16)
        least = (rest - mid.astype(f32)).astype(bf16)
        here = win_ref[g * inner : (g + 1) * inner, :]
        at = groups * inner + g * group
        bias = jnp.where(own_bias, spread(key_ref[:, at : at + group]), 0.0)
        scores.append(
            jnp.dot(high, here, preferred_element_type=f32)
            + jnp.dot(mid, here, preferred_element_type=f32)
            + jnp.dot(least, here, preferred_element_type=f32)
            + jnp.sum(bias, axis=1, keepdims=True)
        )
    window = inner // group
    win = win_ref[...].astype(f32).reshape(groups, window, group, lanes)
    pair = 128 // head_dim
    present = mask_ref[...].reshape(groups, group, lanes) > 0
    for h in range(heads):
        score = jnp.stack([x[h * group : (h + 1) * group] for x in scores])
        score = jnp.where(present, score, -1e30)
        most = jnp.max(jnp.max(score, axis=0), axis=0, keepdims=True)
        raised = jnp.exp(score - most[None])
        total = jnp.sum(jnp.sum(raised, axis=0), axis=0, keepdims=True)
        probs = raised * (1.0 / total)[None]
        probs_ref[:, h] = probs
        weighted = (win * probs[:, None]).astype(bf16).reshape(groups * inner, lanes)
        weighted = jnp.concatenate(
            [weighted, probs.astype(bf16).reshape(groups * group, lanes)], axis=0
        )
        if h % pair == 0:
            values = value_ref[:, h * head_dim : (h + pair) * head_dim].T
        at = h % pair * head_dim
        pooled_ref[h * head_dim : (h + 1) * head_dim, :] = jnp.dot(
            values[at : at + head_dim], weighted, preferred_element_type=f32
        ).astype(bf16)


def agg_forward(win, key_map_t, value_map, mask, group):
    rows, tokens = win.shape
    heads = key_map_t.shape[0]
    chans = mask.shape[0]
    depth, width = value_map.shape
    return call(
        agg_forward_body,
        (
            jax.ShapeDtypeStruct((chans // group, heads, group, tokens), f32),
            jax.ShapeDtypeStruct((width, tokens), bf16),
        ),
        (2 * tokens * depth * (width + heads * group), 6 * 2**20, heads * chans * tokens),
    )(win, key_map_t, value_map, mask)


def agg_backward_core(
    win_ref, probs_ref, gp_ref, value_ref, key_ref, gwin_ref, gvmt_ref, gkm_ref, gs_ref, acc_ref
):
    groups, heads, group, lanes = probs_ref.shape
    rows = win_ref.shape[0]
    inner = rows // groups
    window = inner // group
    head_dim = gp_ref.shape[0] // heads
    shape = (groups, window, group, lanes)
    win = win_ref[...].astype(f32).reshape(shape)
    for h in range(heads):
        here = slice(h * head_dim, (h + 1) * head_dim)
        gp = gp_ref[here, :]
        probs = probs_ref[:, h]
        gw = jnp.dot(value_ref[:, here], gp, preferred_element_type=f32)
        main = gw[:rows].reshape(shape)
        grad_probs = jnp.sum(main * win, axis=1) + gw[rows:].reshape(groups, group, lanes)
        delta = jnp.sum(jnp.sum(probs * grad_probs, axis=0), axis=0, keepdims=True)
        gs_ref[:, h * group : (h + 1) * group, :] = (probs * (grad_probs - delta[None])).astype(bf16)
        part = (main * probs[:, None]).reshape(rows, lanes)
        if h == 0:
            acc_ref[...] = part
        else:
            acc_ref[...] += part
        weighted = (win * probs[:, None]).astype(bf16).reshape(rows, lanes)
        weighted = jnp.concatenate(
            [weighted, probs.astype(bf16).reshape(groups * group, lanes)], axis=0
        )
        gvmt_ref[here, :] = mm(gp, weighted, 1, 1).astype(bf16)
    own = own_lane(heads * group, inner, group)
    own_bias = own_lane(heads * group, group, group)
    fold_in = lambda x: jnp.sum(x.reshape(heads, group, x.shape[1]), axis=1)
    for g in range(groups):
        here = slice(g * inner, (g + 1) * inner)
        keys = jnp.broadcast_to(key_ref[:, here][:, None, :], (heads, group, inner)).reshape(
            heads * group, inner
        )
        keys = jnp.where(own, keys, 0.0).astype(bf16)
        gs = gs_ref[g]
        gwin_ref[here, :] = (acc_ref[here, :] + mm(keys, gs, 0, 0)).astype(bf16)
        gkm_ref[:, here] = fold_in(jnp.where(own, mm(gs, win_ref[here, :], 1, 1), 0.0))
        total = jnp.sum(gs.astype(f32), axis=1, keepdims=True)
        at = rows + g * group
        gkm_ref[:, at : at + group] = fold_in(jnp.where(own_bias, total, 0.0))


def agg_backward(win, probs, grad_pooled_t, value_map, key_map_t):
    rows, tokens = win.shape
    groups, heads, group, _ = probs.shape
    depth, width = value_map.shape
    return call(
        agg_backward_core,
        (
            jax.ShapeDtypeStruct(win.shape, bf16),
            jax.ShapeDtypeStruct((width, depth), bf16),
            jax.ShapeDtypeStruct((heads, depth), f32),
        ),
        (4 * tokens * depth * (width + heads * group), 8 * 2**20, 0),
        scratch=(
            pltpu.VMEM((groups, heads * group, tokens), bf16),
            pltpu.VMEM((rows, tokens), f32),
        ),
    )(win, probs, grad_pooled_t, value_map, key_map_t)


def one_hot(rows, cols, place, keep=None):
    row = lax.broadcasted_iota(jnp.int32, (rows, cols), 0)
    hit = lax.broadcasted_iota(jnp.int32, (rows, cols), 1) == place(row)
    if keep is not None:
        hit = hit & keep(row)
    return jnp.where(hit, 1.0, 0.0).astype(bf16)


def agg_last_body(
    at_ref,
    win_ref,
    probs_ref,
    gp_ref,
    value_ref,
    key_ref,
    weight_ref,
    agg_value_ref,
    agg_query_ref,
    extra_ref,
    canvas_ref,
    edge_ref,
    mine_ref,
    other_ref,
    gwin_ref,
    gvmt_ref,
    gkm_ref,
    gs_ref,
    acc_ref,
    my_win_ref,
    late_ref,
    *,
    cols,
    parts,
):
    groups, heads, group, lanes = probs_ref.shape
    chans = groups * group
    my_chans = chans // parts
    depth, width = weight_ref.shape
    mine = width // parts
    part, parity = (at_ref[0], at_ref[1])
    agg_backward_core(
        win_ref, probs_ref, gp_ref, value_ref, key_ref, gwin_ref, gvmt_ref, gkm_ref, gs_ref, acc_ref
    )
    spot = lambda var, k: (var // group * 16 + k) * group + var % group
    pick = one_hot(
        16 * group,
        16 * chans,
        lambda row: spot(part * my_chans + row % group, row // group),
        lambda row: row % group < my_chans,
    )
    my_win_ref[...] = jnp.dot(pick, gwin_ref[...], preferred_element_type=f32).astype(bf16)
    fold_rows(my_win_ref, canvas_ref, cols, group)
    edge_ref[0] = canvas_ref[:, 0].astype(bf16)
    edge_ref[1] = canvas_ref[:, 2 * cols + 1].astype(bf16)
    key_low = gkm_ref[...].astype(bf16)
    late_ref[:mine, :] = mm(
        weight_ref[:, pl.ds(pl.multiple_of(part * mine, 128), mine)], gvmt_ref[...], 0, 1
    ).astype(bf16)
    ext_rows = -(-17 * my_chans // 16) * 16

    def ext_place(row):
        main = row < 16 * my_chans
        var = part * my_chans + jnp.where(main, row // 16, row - 16 * my_chans)
        return jnp.where(main, spot(var, row % 16), 16 * chans + var)

    select = one_hot(ext_rows, depth, ext_place, lambda row: row < 17 * my_chans)
    my_value = mm(select, gvmt_ref[...], 1, 1).astype(bf16)
    my_key = mm(select, key_low, 1, 1).astype(bf16)
    late_ref[mine : mine + ext_rows, :] = (
        mm(my_value, agg_value_ref[...], 1, 1)
        + jnp.dot(my_key, agg_query_ref[...], preferred_element_type=f32)
    ).astype(bf16)
    my_heads = heads // parts
    pick = one_hot(
        16, heads, lambda row: part * my_heads + row, lambda row: row < my_heads
    )
    query = jnp.dot(pick, key_low, preferred_element_type=f32).astype(bf16)
    at = mine + ext_rows
    late_ref[at : at + 16, :] = jnp.dot(
        query, weight_ref[...], preferred_element_type=f32
    ).astype(bf16)
    late_ref[at + 16 :, :] = extra_ref[...].astype(bf16)
    split_into(late_ref, parity, at_ref[2], mine_ref, other_ref)


def split_into(whole_ref, parity, line, mine_ref, other_ref):
    block = 128
    for pair in range(mine_ref.shape[1] // block):
        to = slice(pair * block, (pair + 1) * block)
        for target, side in ((mine_ref, parity), (other_ref, 1 - parity)):
            start = pl.multiple_of((2 * jnp.bitwise_xor(pair, line) + side) * block, block)
            target[:, to] = whole_ref[:, pl.ds(start, block)]


def agg_last(
    at, win, probs, grad_pooled_t, value_map, key_map_t, weight, agg_value, agg_query, extra, samples, cols, parts
):
    rows, tokens = win.shape
    groups, heads, group, _ = probs.shape
    depth, width = value_map.shape
    pix_rows = 2 * tokens // (samples * cols)
    count = width // parts + -(-17 * groups * group // parts // 16) * 16 + 32
    half = jax.ShapeDtypeStruct((count, width // 2), bf16)
    return call(
        functools.partial(agg_last_body, cols=cols, parts=parts),
        (
            jax.ShapeDtypeStruct((samples, 2 * cols + 2, group, pix_rows), f32),
            jax.ShapeDtypeStruct((2, samples, group, pix_rows), bf16),
            half,
            half,
        ),
        (6 * tokens * depth * (width + heads * group), 12 * 2**20, 0),
        1,
        9,
        scratch=(
            pltpu.VMEM(win.shape, bf16),
            pltpu.VMEM((width, depth), bf16),
            pltpu.VMEM((heads, depth), f32),
            pltpu.VMEM((groups, heads * group, tokens), bf16),
            pltpu.VMEM((rows, tokens), f32),
            pltpu.VMEM((16 * group, tokens), bf16),
            pltpu.VMEM((count, width), bf16),
        ),
    )(at, win, probs, grad_pooled_t, value_map, key_map_t, weight, agg_value, agg_query, extra)


def attend_body(x_ref, o_ref, lse_ref, key_ref, value_ref, query_ref, *, scale, wide):
    blocks, triple, span = x_ref.shape
    head_dim = triple // 3
    seq = blocks * span
    for n in range(blocks):
        here = slice(n * span, (n + 1) * span)
        query_ref[:, here] = x_ref[n, :head_dim, :] * jnp.asarray(scale, bf16)
        key_ref[here, :] = x_ref[n, head_dim : 2 * head_dim, :].T
        value_ref[:head_dim, here] = x_ref[n, 2 * head_dim :, :]
    value_ref[head_dim:, :] = jnp.ones((8, seq), bf16)
    for w in range(seq // wide):
        scores = jnp.dot(
            key_ref[...], query_ref[:, w * wide : (w + 1) * wide], preferred_element_type=f32
        )
        most = jnp.max(scores, axis=0, keepdims=True)
        raised = jnp.exp(scores - most).astype(bf16)
        both = jnp.dot(value_ref[...], raised, preferred_element_type=f32)
        total = both[head_dim : head_dim + 1]
        out = (both[:head_dim] * (1.0 / total)).astype(bf16)
        lse = most + jnp.log(total)
        for n in range(wide // span):
            here = slice(n * span, (n + 1) * span)
            o_ref[w * (wide // span) + n] = out[:, here]
            lse_ref[w * (wide // span) + n] = lse[:, here]


def attend(x, scale):
    blocks, triple, span = x.shape
    head_dim = triple // 3
    seq = blocks * span
    return call(
        functools.partial(attend_body, scale=scale, wide=max(span, seq // 2)),
        (
            jax.ShapeDtypeStruct((blocks, head_dim, span), bf16),
            jax.ShapeDtypeStruct((blocks, 1, span), f32),
        ),
        (4 * seq * seq * head_dim, 2 * x.size, seq * seq),
        scratch=(
            pltpu.VMEM((seq, head_dim), bf16),
            pltpu.VMEM((head_dim + 8, seq), bf16),
            pltpu.VMEM((head_dim, seq), bf16),
        ),
    )(x)


def attend_back_body(
    x_ref, do_ref, lse_ref, o_ref, key_ref, keyt_ref, value_ref, dkey_ref, dvalue_ref, *, scale
):
    blocks, triple, span = x_ref.shape
    head_dim = triple // 3
    for n in range(blocks):
        here = slice(n * span, (n + 1) * span)
        key_ref[here, :] = x_ref[n, head_dim : 2 * head_dim, :].T
        keyt_ref[:, here] = x_ref[n, head_dim : 2 * head_dim, :]
        value_ref[here, :] = x_ref[n, 2 * head_dim :, :].T
    for n in range(blocks):
        query = x_ref[n, :head_dim, :] * jnp.asarray(scale, bf16)
        grad = do_ref[n]
        scores = jnp.dot(key_ref[...], query, preferred_element_type=f32)
        probs = jnp.exp(scores - lse_ref[n])
        grad_probs = jnp.dot(value_ref[...], grad, preferred_element_type=f32)
        delta = jnp.sum(probs * grad_probs, axis=0, keepdims=True)
        grad_scores = (probs * (grad_probs - delta)).astype(bf16)
        o_ref[n, :head_dim, :] = (
            jnp.dot(keyt_ref[...], grad_scores, preferred_element_type=f32) * scale
        ).astype(bf16)
        dkey = jnp.dot(grad_scores, query.T, preferred_element_type=f32)
        dvalue = jnp.dot(probs.astype(bf16), grad.T, preferred_element_type=f32)
        if n == 0:
            dkey_ref[...] = dkey
            dvalue_ref[...] = dvalue
        else:
            dkey_ref[...] += dkey
            dvalue_ref[...] += dvalue
    for n in range(blocks):
        here = slice(n * span, (n + 1) * span)
        o_ref[n, head_dim : 2 * head_dim, :] = dkey_ref[here, :].T.astype(bf16)
        o_ref[n, 2 * head_dim :, :] = dvalue_ref[here, :].T.astype(bf16)


def attend_back(x, grad, lse, scale):
    blocks, triple, span = x.shape
    head_dim = triple // 3
    seq = blocks * span
    return call(
        functools.partial(attend_back_body, scale=scale),
        jax.ShapeDtypeStruct(x.shape, bf16),
        (10 * seq * seq * head_dim, 4 * x.size, seq * seq),
        scratch=(
            pltpu.VMEM((seq, head_dim), bf16),
            pltpu.VMEM((head_dim, seq), bf16),
            pltpu.VMEM((seq, head_dim), bf16),
            pltpu.VMEM((seq, head_dim), f32),
            pltpu.VMEM((seq, head_dim), f32),
        ),
    )(x, grad, lse)


def stats(x):
    centered = x - jnp.mean(x, axis=-1, keepdims=True)
    inverse = lax.rsqrt(jnp.mean(centered * centered, axis=-1, keepdims=True) + norm_eps)
    return centered * inverse, inverse


def norm_back(grad_out, gain, hat, inverse):
    grad_hat = grad_out * gain
    return inverse * (
        grad_hat
        - jnp.mean(grad_hat, axis=-1, keepdims=True)
        - hat * jnp.mean(grad_hat * hat, axis=-1, keepdims=True)
    )


def halves(core_ref, part_ref, mine_ref, other_ref):
    half = mine_ref.shape[0]
    core = core_ref[0]
    mine_ref[...] = part_ref[pl.ds(pl.multiple_of(core * half, half), half), :].astype(bf16)
    other_ref[...] = part_ref[pl.ds(pl.multiple_of((1 - core) * half, half), half), :].astype(bf16)


def joined(core_ref, mine_ref, other_ref, whole_ref):
    half = mine_ref.shape[0]
    core = core_ref[0]
    whole_ref[pl.ds(pl.multiple_of(core * half, half), half), :] = mine_ref[...].astype(f32)
    whole_ref[pl.ds(pl.multiple_of((1 - core) * half, half), half), :] = other_ref[...].astype(f32)


def enter_body(pooled_ref, out_ref, lead_ref, gain_ref, qkv_ref, start_ref, normed_ref, packed_ref):
    heads, samples, triple, span = packed_ref.shape
    head_dim = triple // 3
    x = jnp.dot(pooled_ref[...].T, out_ref[...], preferred_element_type=f32)
    for s in range(samples):
        here = slice(s * span, (s + 1) * span)
        start = x[here] + lead_ref[s : s + 1, :]
        start_ref[here, :] = start
        normed_ref[here, :] = (stats(start)[0] * gain_ref[...]).astype(bf16)
    for m in range(3):
        got = jnp.dot(normed_ref[...], qkv_ref[m], preferred_element_type=f32).astype(bf16).T
        for h in range(heads):
            for s in range(samples):
                packed_ref[h, s, m * head_dim : (m + 1) * head_dim, :] = got[
                    h * head_dim : (h + 1) * head_dim, s * span : (s + 1) * span
                ]


def enter(pooled_t, agg_out, lead_rows, gain, qkv, heads):
    width, tokens = pooled_t.shape
    samples = lead_rows.shape[0]
    head_dim = qkv.shape[2] // heads
    return call(
        enter_body,
        (
            jax.ShapeDtypeStruct((tokens, width), f32),
            jax.ShapeDtypeStruct((tokens, width), bf16),
            jax.ShapeDtypeStruct((heads, samples, 3 * head_dim, tokens // samples), bf16),
        ),
        (2 * tokens * width * (width + 3 * qkv.shape[2]), 8 * 2**20, 0),
    )(pooled_t, agg_out, lead_rows, gain, qkv)


def leave_body(core_ref, att_ref, weight_ref, att_t_ref, mine_ref, other_ref, part_ref):
    heads, samples, head_dim, span = att_ref.shape
    for s in range(samples):
        here = slice(s * span, (s + 1) * span)
        for h in range(heads):
            att_t_ref[h * head_dim : (h + 1) * head_dim, here] = att_ref[h, s]
    part_ref[...] = jnp.dot(att_t_ref[...].T, weight_ref[...], preferred_element_type=f32)
    halves(core_ref, part_ref, mine_ref, other_ref)


def leave(core, att, weight):
    heads, samples, head_dim, span = att.shape
    tokens, width = (samples * span, weight.shape[1])
    half = jax.ShapeDtypeStruct((tokens // 2, width), bf16)
    return call(
        leave_body,
        (jax.ShapeDtypeStruct((heads * head_dim, tokens), bf16), half, half),
        (2 * tokens * width * heads * head_dim, 3 * 2**20, 0),
        1,
        2,
        scratch=(pltpu.VMEM((tokens, width), f32),),
    )(core, att, weight)


def feed_body(
    core_ref,
    start_ref,
    mine_ref,
    other_ref,
    gain_ref,
    up_ref,
    grad_active_ref,
    mid_ref,
    normed_ref,
    active_ref,
    grad_hidden_ref,
    out_mine_ref,
    out_other_ref,
    part_ref,
):
    joined(core_ref, mine_ref, other_ref, part_ref)
    step = 128
    for at in range(0, start_ref.shape[0], step):
        here = slice(at, at + step)
        mid = start_ref[here, :] + part_ref[here, :]
        mid_ref[here, :] = mid
        normed = (stats(mid)[0] * gain_ref[...]).astype(bf16)
        normed_ref[here, :] = normed
        hidden = jnp.dot(normed, up_ref[...], preferred_element_type=f32)
        both = 0.5 * (1.0 + lax.erf(hidden * sqrt_half))
        active_ref[here, :] = (hidden * both).astype(bf16)
        slope = both + hidden * jnp.exp(-0.5 * hidden * hidden) * inv_root_two_pi
        grad = (grad_active_ref[here, :].astype(f32) * slope).astype(bf16)
        grad_hidden_ref[here, :] = grad
        part_ref[here, :] = mm(grad, up_ref[...], 1, 1)
    halves(core_ref, part_ref, out_mine_ref, out_other_ref)


def feed(core, start, mine, other, gain, up, grad_active):
    tokens, width = start.shape
    low = jax.ShapeDtypeStruct((tokens, width), bf16)
    wide = jax.ShapeDtypeStruct((tokens, up.shape[1]), bf16)
    half = jax.ShapeDtypeStruct(mine.shape, bf16)
    return call(
        feed_body,
        (jax.ShapeDtypeStruct((tokens, width), f32), low, wide, wide, half, half),
        (4 * tokens * width * up.shape[1], 14 * 2**20, 2 * tokens * up.shape[1]),
        1,
        6,
        scratch=(pltpu.VMEM((tokens, width), f32),),
    )(core, start, mine, other, gain, up, grad_active)


def feed_back_body(
    core_ref,
    mid_ref,
    mine_ref,
    other_ref,
    gain_ref,
    grad_end_ref,
    weight_ref,
    grad_mid_ref,
    grad_att_ref,
    grad_gain_ref,
    packed_ref,
    part_ref,
):
    heads, samples, head_dim, span = packed_ref.shape
    joined(core_ref, mine_ref, other_ref, part_ref)
    grad_gain = jnp.zeros(grad_gain_ref.shape, f32)
    step = 128
    for at in range(0, mid_ref.shape[0], step):
        here = slice(at, at + step)
        hat, inverse = stats(mid_ref[here, :])
        grad_out = part_ref[here, :]
        grad_gain += jnp.sum(grad_out * hat, axis=0, keepdims=True)
        grad = grad_end_ref[here, :].astype(f32) + norm_back(grad_out, gain_ref[...], hat, inverse)
        grad_mid_ref[here, :] = grad
        grad_att_ref[here, :] = grad.astype(bf16)
    grad_gain_ref[...] = grad_gain
    got = mm(weight_ref[...], grad_att_ref[...], 1, 1).astype(bf16)
    for h in range(heads):
        for s in range(samples):
            packed_ref[h, s] = got[h * head_dim : (h + 1) * head_dim, s * span : (s + 1) * span]


def feed_back(core, mid, mine, other, gain, grad_end, weight, heads, samples):
    tokens, width = mid.shape
    return call(
        feed_back_body,
        (
            jax.ShapeDtypeStruct((tokens, width), f32),
            jax.ShapeDtypeStruct((tokens, width), bf16),
            jax.ShapeDtypeStruct((1, width), f32),
            jax.ShapeDtypeStruct(
                (heads, samples, weight.shape[0] // heads, tokens // samples), bf16
            ),
        ),
        (2 * tokens * width * weight.shape[0], 9 * 2**20, 0),
        1,
        6,
        scratch=(pltpu.VMEM((tokens, width), f32),),
    )(core, mid, mine, other, gain, grad_end, weight)


def enter_back_body(core_ref, packed_ref, qkv_ref, flat_ref, mine_ref, other_ref, part_ref):
    heads, samples, triple, span = packed_ref.shape
    head_dim = triple // 3
    width = heads * head_dim
    for m in range(3):
        for h in range(heads):
            for s in range(samples):
                to = m * width + h * head_dim
                flat_ref[to : to + head_dim, s * span : (s + 1) * span] = packed_ref[
                    h, s, m * head_dim : (m + 1) * head_dim, :
                ]
    for m in range(3):
        part = mm(flat_ref[m * width : (m + 1) * width, :].T, qkv_ref[m], 1, 1)
        if m == 0:
            part_ref[...] = part
        else:
            part_ref[...] += part
    halves(core_ref, part_ref, mine_ref, other_ref)


def enter_back(core, packed, qkv):
    heads, samples, triple, span = packed.shape
    tokens, width = (samples * span, qkv.shape[1])
    half = jax.ShapeDtypeStruct((tokens // 2, width), bf16)
    return call(
        enter_back_body,
        (jax.ShapeDtypeStruct((heads * triple, tokens), bf16), half, half),
        (2 * tokens * width * heads * triple, 5 * 2**20, 0),
        1,
        2,
        scratch=(pltpu.VMEM((tokens, width), f32),),
    )(core, packed, qkv)


def pool_back_body(
    at_ref,
    start_ref,
    mine_ref,
    other_ref,
    gain_ref,
    grad_mid_ref,
    out_ref,
    my_pooled_ref,
    hot_ref,
    gain_two_ref,
    grad_agg_ref,
    extra_ref,
    pooled_ref,
    out_mine_ref,
    out_other_ref,
    part_ref,
    grad_out_ref,
):
    samples = hot_ref.shape[1]
    tokens, width = start_ref.shape
    joined(at_ref, mine_ref, other_ref, part_ref)
    grad_gain = jnp.zeros((1, width), f32)
    step = min(128, tokens // samples)
    sums = [jnp.zeros((1, width), f32) for _ in range(samples)]
    for at in range(0, tokens, step):
        here = slice(at, at + step)
        hat, inverse = stats(start_ref[here, :])
        grad_out = part_ref[here, :]
        grad_gain += jnp.sum(grad_out * hat, axis=0, keepdims=True)
        grad = grad_mid_ref[here, :] + norm_back(grad_out, gain_ref[...], hat, inverse)
        sums[at * samples // tokens] += jnp.sum(grad, axis=0, keepdims=True)
        grad_agg_ref[here, :] = grad.astype(bf16)
    leads = hot_ref.shape[0]
    row = lax.broadcasted_iota(jnp.int32, (leads, width), 0)
    extra = jnp.where(row == leads - 2, grad_gain, 0.0)
    extra = extra + jnp.where(row == leads - 1, gain_two_ref[...], 0.0)
    for s in range(samples):
        extra = extra + hot_ref[:, s : s + 1] * sums[s]
    extra_ref[...] = extra
    pooled_ref[...] = mm(out_ref[...], grad_agg_ref[...], 1, 1).astype(bf16)
    grad_out_ref[...] = jnp.dot(
        my_pooled_ref[...], grad_agg_ref[...], preferred_element_type=f32
    ).astype(bf16)
    split_into(grad_out_ref, at_ref[1], at_ref[2], out_mine_ref, out_other_ref)


def pool_back(at, start, mine, other, gain, grad_mid, agg_out, my_pooled, hot, gain_two):
    tokens, width = start.shape
    half = jax.ShapeDtypeStruct((my_pooled.shape[0], width // 2), bf16)
    return call(
        pool_back_body,
        (
            jax.ShapeDtypeStruct((tokens, width), bf16),
            jax.ShapeDtypeStruct((hot.shape[0], width), f32),
            jax.ShapeDtypeStruct((width, tokens), bf16),
            half,
            half,
        ),
        (3 * tokens * width * width, 9 * 2**20, 0),
        1,
        9,
        scratch=(
            pltpu.VMEM((tokens, width), f32),
            pltpu.VMEM((my_pooled.shape[0], width), bf16),
        ),
    )(at, start, mine, other, gain, grad_mid, agg_out, my_pooled, hot, gain_two)


def strips_body(place_ref, *refs, dims):
    mine_ref, other_ref = refs[-2:]
    step = pl.program_id(0)
    count = pl.num_programs(0) // 2

    def fill(o_ref):
        at = 0
        for left_ref, right_ref, dim in zip(refs[:-2:2], refs[1:-2:2], dims):
            wide = right_ref.shape[1 - dim]
            o_ref[:, at : at + wide] = mm(left_ref[...], right_ref[...], 0, dim).astype(bf16)
            at += wide

    @pl.when(step < count)
    def _():
        fill(other_ref)

    @pl.when(step >= count)
    def _():
        fill(mine_ref)


def strips(place, *pairs):
    tokens, width = pairs[0][0].shape
    block = 128
    count = width // block // 2
    wide = sum(right.shape[1 - dim] for _, right, dim in pairs)

    def left_map(i, place_ref):
        own = i // count
        side = place_ref[0] * own + (1 - place_ref[0]) * (1 - own)
        return (0, 2 * jnp.bitwise_xor(i % count, place_ref[1]) + side)

    specs = []
    for left, right, _ in pairs:
        specs.append(pl.BlockSpec((tokens, block), left_map))
        specs.append(pl.BlockSpec(right.shape, lambda i, place_ref: (0, 0)))
    half = jax.ShapeDtypeStruct((width // 2, wide), bf16)
    return pl.pallas_call(
        functools.partial(strips_body, dims=[dim for _, _, dim in pairs]),
        out_shape=(half, half),
        grid_spec=pltpu.PrefetchScalarGridSpec(
            num_scalar_prefetch=1,
            grid=(2 * count,),
            in_specs=specs,
            out_specs=(
                pl.BlockSpec((block, wide), lambda i, p: (jnp.maximum(i - count, 0), 0)),
                pl.BlockSpec((block, wide), lambda i, p: (jnp.minimum(i, count - 1), 0)),
            ),
        ),
        compiler_params=pltpu.CompilerParams(vmem_limit_bytes=vmem_most),
        cost_estimate=pl.CostEstimate(
            flops=tokens * width * wide // 32, bytes_accessed=width * wide // 16, transcendentals=0
        ),
    )(place, *[x for pair in pairs for x in pair[:2]])


def rows_total(refs, columns=slice(None)):
    total = refs[0][:, columns].astype(f32)
    for ref in refs[1:]:
        total = total + ref[:, columns].astype(f32)
    return total


def finish_body(*refs, parts):
    up, down, mid, end = [refs[n * parts : (n + 1) * parts] for n in range(4)]
    up_ref, down_ref, out_ref, qkv_ref, head_ref = refs[4 * parts :]
    local = out_ref.shape[0]
    up_ref[...] = rows_total(up)
    out_ref[...] = rows_total(mid, slice(2 * local, 3 * local)).T
    down_ref[...] = rows_total(down).T
    for m in range(2):
        qkv_ref[m] = rows_total(mid, slice(m * local, (m + 1) * local))
    qkv_ref[2] = rows_total(end, slice(0, local))
    head_ref[...] = rows_total(end, slice(local, end[0].shape[1])).T[: head_ref.shape[0]]


def finish(groups, local, head_rows):
    up, down = groups[:2]
    block, hidden = up[0].shape
    f32s = lambda *shape: jax.ShapeDtypeStruct(shape, f32)
    return call(
        functools.partial(finish_body, parts=len(up)),
        (
            f32s(block, hidden),
            f32s(hidden, block),
            f32s(local, block),
            f32s(3, block, local),
            f32s(head_rows, block),
        ),
        (0, 8 * 2**20, 0),
    )(*[x for group in groups for x in group])


def finish_late_body(*refs, parts):
    agg_ref, value_ref, patch_ref, bias_ref, query_ref, lead_ref, gain_ref = refs[parts:]
    total = rows_total(refs[:parts])
    at = agg_ref.shape[0]
    agg_ref[...] = total[:at]
    value_ref[...] = total[at : at + value_ref.shape[0]]
    at += value_ref.shape[0]
    my_chans = bias_ref.shape[0]
    patch_ref[...] = total[at : at + 16 * my_chans].reshape(patch_ref.shape)
    bias_ref[...] = total[at + 16 * my_chans : at + 17 * my_chans]
    at += -(-17 * my_chans // 16) * 16
    query_ref[...] = total[at : at + query_ref.shape[0]]
    lead_ref[...] = total[at + 16 : at + 16 + lead_ref.shape[0]]
    gain_ref[...] = total[at + 16 + lead_ref.shape[0] :]


def finish_late(late, local, my_chans, my_heads, leads):
    block = late[0].shape[1]
    f32s = lambda *shape: jax.ShapeDtypeStruct(shape, f32)
    return call(
        functools.partial(finish_late_body, parts=len(late)),
        (
            f32s(local, block),
            f32s(local, block),
            f32s(my_chans, 16, block),
            f32s(my_chans, block),
            f32s(my_heads, block),
            f32s(leads, block),
            f32s(8, block),
        ),
        (0, 2**20, 0),
    )(*late)


def close_body(canvas_ref, before_ref, after_ref, o_ref):
    samples, chans, cols, _ = o_ref.shape
    for s in range(samples):
        for col in range(cols):
            piece = canvas_ref[s, col + 1, :chans]
            if col == 0:
                piece = piece + before_ref[s, :chans].astype(f32)
            if col == cols - 1:
                piece = piece + after_ref[s, :chans].astype(f32)
            o_ref[s, :, col, :] = piece


def close_kernel(canvas, rims, chans):
    samples, wide, _, rows = canvas.shape
    return call(
        close_body,
        jax.ShapeDtypeStruct((samples, chans, wide - 2, rows), f32),
        (0, 2**20, 0),
    )(canvas, *rims)


def attend_gathered(packed, scale):
    head_dim = packed.shape[2] // 3
    whole = lax.all_gather(packed[:, :, head_dim:, :], "sector", axis=0)
    keys, values = (whole[:, :, :, :head_dim], whole[:, :, :, head_dim:])
    scores = (
        jnp.einsum("hsdq,nhsdk->hsqnk", packed[:, :, :head_dim], keys, preferred_element_type=f32)
        * scale
    )
    most = jnp.max(scores, axis=(3, 4), keepdims=True)
    raised = jnp.exp(scores - most)
    total = jnp.sum(raised, axis=(3, 4), keepdims=True)
    probs = (raised / total).astype(bf16)
    out = jnp.einsum("hsqnk,nhsdk->hsdq", probs, values, preferred_element_type=f32)
    return out.astype(bf16), most + jnp.log(total)


def attend_back_gathered(packed, grad, lse, scale):
    head_dim = packed.shape[2] // 3
    query = packed[:, :, :head_dim]
    whole = lax.all_gather(packed[:, :, head_dim:, :], "sector", axis=0)
    keys, values = (whole[:, :, :, :head_dim], whole[:, :, :, head_dim:])
    scores = jnp.einsum("hsdq,nhsdk->hsqnk", query, keys, preferred_element_type=f32) * scale
    probs = jnp.exp(scores - lse)
    grad_probs = jnp.einsum("hsdq,nhsdk->hsqnk", grad, values, preferred_element_type=f32)
    delta = jnp.sum(probs * grad_probs, axis=(3, 4), keepdims=True)
    grad_scores = (probs * (grad_probs - delta)).astype(bf16)
    grad_query = jnp.einsum("hsqnk,nhsdk->hsdq", grad_scores, keys, preferred_element_type=f32)
    grad_keys = jnp.einsum("hsqnk,hsdq->nhsdk", grad_scores, query, preferred_element_type=f32)
    grad_values = jnp.einsum(
        "hsqnk,hsdq->nhsdk", probs.astype(bf16), grad, preferred_element_type=f32
    )
    both = lax.psum_scatter(
        jnp.concatenate([grad_keys * scale, grad_values], axis=3), "sector", scatter_dimension=0
    )
    return jnp.concatenate([grad_query * scale, both], axis=2).astype(bf16)


def swap(x, axis, bit):
    size = lax.axis_size(axis)
    return lax.ppermute(x, axis, [(i, i ^ bit) for i in range(size)])


def rounded(x):
    return lax.reduce_precision(x, 8, 7)


def sum_over_mp(x):
    if lax.axis_size("mp") != 4:
        return lax.psum(x.astype(bf16), "mp").astype(f32)
    half = x.shape[0] // 2
    low, high = (rounded(x[:half]), rounded(x[half:]))
    first = lax.axis_index("mp") % 2 == 0
    mine, other = (jnp.where(first, low, high), jnp.where(first, high, low))
    mine = rounded(mine + swap(other.astype(bf16), "mp", 1).astype(f32))
    mine = rounded(mine + swap(mine.astype(bf16), "mp", 2).astype(f32))
    other = swap(mine.astype(bf16), "mp", 1).astype(f32)
    return jnp.concatenate([jnp.where(first, mine, other), jnp.where(first, other, mine)], axis=0)


def near_sum(mine, other):
    return rounded(mine.astype(f32) + swap(other, "mp", 1).astype(f32)).astype(bf16)


def far_sum(mine, got):
    mine = rounded(mine.astype(f32) + got.astype(f32)).astype(bf16)
    return mine, swap(mine, "mp", 1)


def ring_pair(leading, last):
    size = lax.axis_size("sector")
    up = [(i, (i + 1) % size) for i in range(size)]
    down = [(j, i) for i, j in up]
    return lax.ppermute(last, "sector", up), lax.ppermute(leading, "sector", down)


def split_cols(x, block):
    even = lax.axis_index("sector") % 2 == 0
    pairs = x.shape[1] // (2 * block)
    low = [x[:, 2 * p * block : (2 * p + 1) * block] for p in range(pairs)]
    high = [x[:, (2 * p + 1) * block : (2 * p + 2) * block] for p in range(pairs)]
    mine = [jnp.where(even, a, b) for a, b in zip(low, high)]
    other = [jnp.where(even, b, a) for a, b in zip(low, high)]
    return jnp.concatenate(mine, axis=1), jnp.concatenate(other, axis=1)


def pair_sum(mine, got):
    return (mine.astype(f32) + got.astype(f32)).astype(bf16)


def line_parts(pieces):
    return [pieces[0]] + [swap(pieces[n], "sector", 2 * n) for n in range(1, len(pieces))]


def norm_forward(values, gain_vec):
    row_mean = jnp.mean(values, axis=-1, keepdims=True)
    centered = values - row_mean
    inverse = lax.rsqrt(jnp.mean(centered * centered, axis=-1, keepdims=True) + norm_eps)
    normed = centered * inverse
    return (normed * gain_vec, normed, inverse)


def norm_backward(grad_out, gain_vec, normed, inverse):
    grad_normed = grad_out * gain_vec
    grad_gain = jnp.sum(grad_out * normed, axis=0)
    grad_in = inverse * (
        grad_normed
        - jnp.mean(grad_normed, axis=-1, keepdims=True)
        - normed * jnp.mean(grad_normed * normed, axis=-1, keepdims=True)
    )
    return (grad_in, grad_gain)


def gelu_slope(values):
    return (
        0.5 * (1.0 + lax.erf(values * sqrt_half))
        + values * jnp.exp(-0.5 * values * values) * inv_root_two_pi
    )


def mp_slice(values, axis_dim, mp_index, mp_count):
    piece_len = values.shape[axis_dim] // mp_count
    return lax.dynamic_slice_in_dim(values, mp_index * piece_len, piece_len, axis_dim)


def shards(
    input_field,
    present_mask,
    lead_index,
    patch_weight,
    patch_bias,
    agg_query,
    agg_value,
    agg_out,
    lead_table,
    norm1_gain,
    qkv_weight,
    attn_out_weight,
    norm2_gain,
    up_weight,
    down_weight,
    head_weight,
    pred_cotangent,
):
    samples, chans, pix_rows, pix_cols = input_field.shape
    rows, cols = (pix_rows // 2, pix_cols // 2)
    span = rows * cols
    tokens = samples * span
    width = patch_weight.shape[2]
    heads = agg_query.shape[0]
    head_dim = width // heads
    local_width = qkv_weight.shape[2]
    local_heads = local_width // head_dim
    sectors = lax.axis_size("sector")
    mp_count = lax.axis_size("mp")
    mp_index = lax.axis_index("mp")
    score_scale = head_dim ** (-0.5)
    depth = 17 * chans
    group = 16 if chans % 16 == 0 else chans
    groups = chans // group

    by_head = sectors == local_heads * samples
    block = width // sectors
    fast = by_head and block == 128 and sectors == 8 and mp_count == 4 and samples % 2 == 0 and span % 128 == 0
    exchange = lambda x: lax.all_to_all(
        x.reshape(sectors, x.shape[-2], x.shape[-1]), "sector", 0, 0, tiled=True
    )
    by_pair = lambda x: x.reshape(local_heads, samples, x.shape[1], x.shape[2])
    sector = lax.axis_index("sector")
    core = jnp.stack([mp_index % 2, sector % 2, sector // 2])
    whereabouts = core[1:]
    counts = range(width // block // 2)
    row_sums = lambda a, b: [
        pair_sum(a[n * block : (n + 1) * block], b[n * block : (n + 1) * block]) for n in counts
    ]
    lane_sums = lambda a, b: [
        pair_sum(a[:, n * block : (n + 1) * block], b[:, n * block : (n + 1) * block])
        for n in counts
    ]
    across = lambda x: swap(x, "mp", 2)
    beside = lambda x: swap(x, "sector", 1)
    barrier = lax.optimization_barrier

    fields = jnp.transpose(input_field, (0, 3, 1, 2))
    cots = jnp.transpose(pred_cotangent, (0, 3, 1, 2))
    before, after = ring_pair(
        *(jnp.stack([x[..., at] for x in (input_field, pred_cotangent)]) for at in (0, -1))
    )
    haloed = lambda x, n: jnp.concatenate([before[n][:, None], x, after[n][:, None]], axis=1)
    win = windows(haloed(fields, 0), group)

    weight_kv = jnp.concatenate(
        [
            jnp.transpose(patch_weight.reshape(groups, group, 16, width), (0, 2, 1, 3)).reshape(
                16 * chans, width
            ),
            patch_bias,
        ],
        axis=0,
    )
    key_map_t = mm(agg_query, weight_kv, 1, 1)
    value_map = jnp.dot(weight_kv, agg_value, preferred_element_type=f32).astype(bf16)
    mask = jnp.broadcast_to(
        jnp.transpose(present_mask)[:, :, None], (chans, samples, span)
    ).reshape(chans, tokens)
    probs, pooled_t = agg_forward(win, key_map_t, value_map, mask, group)
    lead_hot = (lead_index[:, None] == jnp.arange(lead_table.shape[0])[None, :]).astype(f32)
    lead_rows = jnp.dot(lead_hot, lead_table.astype(f32), precision=highest)

    head_cols = head_weight.shape[1]
    spot = lax.broadcasted_iota(jnp.int32, (head_cols, head_cols), 1)
    source = lax.broadcasted_iota(jnp.int32, (head_cols, head_cols), 0)
    place = (spot % (16 * group)) // group
    shuffle = ((spot // (16 * group) * group + spot % group) * 16 + place == source).astype(bf16)
    head_kv = jnp.dot(head_weight, shuffle, preferred_element_type=f32).astype(bf16)
    grad_head_t = windows(haloed(cots, 1), group)
    grad_end = mm(grad_head_t, head_kv, 0, 1)
    grad_mlp = grad_end.astype(bf16)
    grad_active = mm(grad_mlp, down_weight, 1, 1)

    my_chans = chans // mp_count
    my_heads = heads // mp_count
    spots = lambda var, k: (var // group * 16 + k) * group + var % group

    def ext_place(row):
        main = row < 16 * my_chans
        var = mp_index * my_chans + jnp.where(main, row // 16, row - 16 * my_chans)
        return jnp.where(main, spots(var, row % 16), 16 * chans + var)

    head_rows = -(-16 * my_chans // 128) * 128
    my_head = jnp.dot(
        one_hot(head_rows, 16 * chans, ext_place, lambda row: row < 16 * my_chans),
        grad_head_t,
        preferred_element_type=f32,
    ).astype(bf16)
    my_pooled = mp_slice(pooled_t, 0, mp_index, mp_count)

    if fast:
        qkv = jnp.transpose(qkv_weight, (1, 0, 2))
        start_x, normed1_low, packed = enter(
            pooled_t, agg_out, lead_rows, norm1_gain[None], qkv, local_heads
        )
        held = exchange(packed)
        held, grad_active, grad_mlp, my_pooled = barrier(
            (held, grad_active.astype(bf16), grad_mlp, my_pooled)
        )
        att_held, lse = attend(held, score_scale)
        att_t, mine, other = leave(core, by_pair(exchange(att_held)), attn_out_weight)
        mine = near_sum(mine, other)
        mid_x, normed2_low, active_low, grad_hidden, mine, other = feed(
            core,
            start_x,
            *far_sum(mine, across(mine)),
            norm2_gain[None],
            up_weight,
            grad_active,
        )
        mine = near_sum(mine, other)
        down_mine, down_other = strips(whereabouts, (grad_mlp, active_low, 0))
        low = jnp.dot(active_low, down_weight, preferred_element_type=f32).astype(bf16)
        first = mp_index % 2 == 0
        low, high = (low[: tokens // 2], low[tokens // 2 :])
        end_mine = near_sum(jnp.where(first, low, high), jnp.where(first, high, low))
        up_mine, up_other = strips(whereabouts, (normed2_low, grad_hidden, 0))
        down_got = beside(down_other)
        got, down_mine, up_mine, end_mine = barrier((across(mine), down_mine, up_mine, end_mine))
        grad_mid, grad_att, grad_gain_two, grad_heads = feed_back(
            core,
            mid_x,
            *far_sum(mine, got),
            norm2_gain[None],
            grad_mlp,
            attn_out_weight,
            local_heads,
            samples,
        )
        down_pair = row_sums(down_mine, down_got)
        grad_att_held, down_pair, up_other = barrier(
            (exchange(grad_heads), down_pair, up_other)
        )
        down_parts = line_parts(down_pair)
        up_got = beside(up_other)
        grad_held = attend_back(held, grad_att_held, lse, score_scale)
        end_got, down_parts, up_got, grad_att, grad_held = barrier(
            (across(end_mine), down_parts, up_got, grad_att, grad_held)
        )
        out_mine, out_other = strips(whereabouts, (grad_att, att_t, 1))
        out_got = beside(out_other)
        near, far = far_sum(end_mine, end_got)
        end_x = mid_x + jnp.concatenate(
            [jnp.where(first, near, far), jnp.where(first, far, near)], axis=0
        ).astype(f32)
        grad_packed = exchange(grad_held)
    else:
        start_x = (
            mm(pooled_t, agg_out, 0, 0).reshape(samples, span, width) + lead_rows[:, None, :]
        ).reshape(tokens, width)
        normed1, hat_one, inv_one = norm_forward(start_x, norm1_gain)
        normed1_low = normed1.astype(bf16)
        qkv_t = lax.dot_general(
            qkv_weight, normed1_low, (((0,), (1,)), ((), ())), preferred_element_type=f32
        ).astype(bf16)
        packed = jnp.transpose(
            qkv_t.reshape(3, local_heads, head_dim, samples, span), (1, 3, 0, 2, 4)
        ).reshape(local_heads, samples, 3 * head_dim, span)
        att, lse = attend_gathered(packed, score_scale)
        att_t = jnp.transpose(att, (0, 2, 1, 3)).reshape(local_width, tokens)
        mid_x = start_x + sum_over_mp(mm(att_t, attn_out_weight, 0, 0))
        normed2, hat_two, inv_two = norm_forward(mid_x, norm2_gain)
        normed2_low = normed2.astype(bf16)
        hidden = jnp.dot(normed2_low, up_weight, preferred_element_type=f32)
        active_low = jax.nn.gelu(hidden, approximate=False).astype(bf16)
        grad_hidden = (grad_active * gelu_slope(hidden)).astype(bf16)
        grad_normed2 = sum_over_mp(mm(grad_hidden, up_weight, 1, 1))
        grad_mid_norm, grad_gain_two = norm_backward(grad_normed2, norm2_gain, hat_two, inv_two)
        grad_mid = grad_end + grad_mid_norm
        grad_att = grad_mid.astype(bf16)
        grad_heads_t = mm(attn_out_weight, grad_att, 1, 1).astype(bf16)
        grad_heads = jnp.transpose(
            grad_heads_t.reshape(local_heads, head_dim, samples, span), (0, 2, 1, 3)
        )
        grad_packed = attend_back_gathered(packed, grad_heads, lse, score_scale)
        end_x = mid_x + sum_over_mp(jnp.dot(active_low, down_weight, preferred_element_type=f32))

    end_low = end_x.astype(bf16)
    head_out = mm(head_kv, end_low, 0, 1).astype(bf16)
    canvas, edges = fold(head_out, samples, cols, pix_rows, group)

    def close(canvas, rims):
        inner = canvas[:, 1:-1]
        inner = inner.at[:, 0].add(rims[0].astype(f32))
        return jnp.transpose(inner.at[:, -1].add(rims[1].astype(f32)), (0, 2, 3, 1))

    leads = lead_table.shape[0]

    if fast:
        joint = lambda *x: jnp.concatenate(x, axis=0)
        up_parts = line_parts(row_sums(up_mine, up_got))
        rims = ring_pair(edges[0], edges[1])
        grad_packed, rims, out_got = barrier((grad_packed, rims, out_got))
        out_pair = row_sums(out_mine, out_got)
        flat, mine, other = enter_back(core, by_pair(grad_packed), qkv)
        mine = near_sum(mine, other)
        part = 2 * local_width
        mid_mine, mid_other = strips(whereabouts, (normed1_low, flat[:part], 1))
        mid_got = beside(mid_other)
        end_mine, end_other = strips(
            whereabouts, (normed1_low, flat[part:], 1), (end_low, my_head, 1)
        )
        end_got = beside(end_other)
        got, mid_mine, end_mine, up_parts = barrier((across(mine), mid_mine, end_mine, up_parts))
        hot = jnp.zeros((leads + 8, samples), f32).at[:leads].set(jnp.transpose(lead_hot))
        grad_agg, extra, grad_pooled_t, agg_mine, agg_other = pool_back(
            core,
            start_x,
            *far_sum(mine, got),
            norm1_gain[None],
            grad_mid,
            agg_out,
            my_pooled,
            hot,
            grad_gain_two,
        )
        mid_got, out_pair, grad_pooled_t = barrier((mid_got, out_pair, grad_pooled_t))
        mid_pair = [
            jnp.concatenate(x, axis=1) for x in zip(row_sums(mid_mine, mid_got), out_pair)
        ]
        mid_parts = line_parts(mid_pair)
        grad_canvas, grad_edges, late_mine, late_other = agg_last(
            jnp.stack([mp_index, sector % 2, sector // 2]),
            win,
            probs,
            grad_pooled_t,
            value_map,
            key_map_t,
            weight_kv,
            agg_value,
            agg_query,
            extra,
            samples,
            cols,
            mp_count,
        )
        late_other, grad_edges, mid_parts, end_got = barrier(
            (late_other, grad_edges, mid_parts, end_got)
        )
        end_parts = line_parts(row_sums(end_mine, end_got))
        grad_rims = ring_pair(grad_edges[0], grad_edges[1])
        late_got, grad_rims = barrier((beside(late_other), grad_rims))
        agg_pair = lane_sums(agg_mine, beside(agg_other))
        late_pair = lane_sums(late_mine, late_got)
        late_parts = line_parts([jnp.concatenate(x, axis=0) for x in zip(agg_pair, late_pair)])
        outs = finish(
            (up_parts, down_parts, mid_parts, end_parts), local_width, 16 * my_chans
        )
        prediction = close_kernel(canvas, rims, chans)
        field_grad = close_kernel(grad_canvas, grad_rims, my_chans)
        late_parts, outs, prediction, field_grad = barrier(
            (late_parts, outs, prediction, field_grad)
        )
        up_sum, down_sum, out_sum, qkv_sum, head_sum = outs
        qkv_sum = jnp.transpose(qkv_sum, (1, 0, 2))
        head_sum = jnp.transpose(head_sum)
        prediction, field_grad = [jnp.transpose(x, (0, 1, 3, 2)) for x in (prediction, field_grad)]
        agg_out_sum, value_sum, patch_sum, bias_sum, query_sum, lead_sum, gain_sums = finish_late(
            late_parts, local_width, my_chans, my_heads, leads
        )
        one_sum, two_sum = (gain_sums[6:7], gain_sums[7:8])
    else:
        prediction = close(canvas, ring_pair(edges[0], edges[1]))
        flat = jnp.transpose(
            grad_packed.reshape(local_heads, samples, 3, head_dim, span), (2, 0, 3, 1, 4)
        ).reshape(3 * local_width, tokens)
        grad_normed1 = sum_over_mp(
            lax.dot_general(
                flat.reshape(3, local_width, tokens),
                qkv_weight,
                (((0, 1), (1, 2)), ((), ())),
                preferred_element_type=f32,
            )
        )
        grad_start_norm, grad_gain_one = norm_backward(grad_normed1, norm1_gain, hat_one, inv_one)
        grad_start = grad_mid + grad_start_norm
        grad_agg = grad_start.astype(bf16)
        sample_sums = jnp.sum(grad_start.reshape(samples, span, width), axis=1)
        grad_pooled_t = mm(agg_out, grad_agg, 1, 1).astype(bf16)
        grad_lead = jnp.einsum("sl,sd->ld", lead_hot, sample_sums, precision=highest)
        gains = [x.reshape(1, width) for x in (grad_gain_one, grad_gain_two)]
        grad_win, value_grad_t, key_grad = agg_backward(
            win, probs, grad_pooled_t, value_map, key_map_t
        )
        key_low = key_grad.astype(bf16)
        grad_agg_value = mm(mp_slice(weight_kv, 1, mp_index, mp_count), value_grad_t, 0, 1)
        select = one_hot(17 * my_chans, depth, ext_place)
        my_value = mm(select, value_grad_t, 1, 1).astype(bf16)
        my_key = mm(select, key_low, 1, 1).astype(bf16)
        grad_ext = mm(my_value, agg_value, 1, 1) + jnp.dot(
            my_key, agg_query, preferred_element_type=f32
        )
        grad_agg_query = jnp.dot(
            mp_slice(key_low, 0, mp_index, mp_count), weight_kv, preferred_element_type=f32
        )
        grad_canvas, grad_edges = fold(grad_win, samples, cols, pix_rows, group)
        grad_edges = mp_slice(grad_edges, 2, mp_index, mp_count)
        field_grad = close(
            mp_slice(grad_canvas, 2, mp_index, mp_count), ring_pair(grad_edges[0], grad_edges[1])
        )
        put = lambda x, dim: lax.psum_scatter(x, "sector", scatter_dimension=dim, tiled=True)
        up_sum = put(mm(normed2_low, grad_hidden, 0, 0), 0)
        down_sum = put(mm(active_low, grad_mlp, 0, 0), 1)
        out_sum = put(jnp.dot(att_t, grad_att, preferred_element_type=f32), 1)
        head_sum = put(mm(end_low, my_head[: 16 * my_chans], 0, 1), 0)
        qkv_sum = put(mm(normed1_low, flat, 0, 1), 0).reshape(block, 3, local_width)
        agg_out_sum = put(jnp.dot(my_pooled, grad_agg, preferred_element_type=f32), 1)
        late = [grad_agg_value, grad_ext, grad_agg_query, grad_lead] + gains
        value_sum, ext_sum, query_sum, lead_sum, one_sum, two_sum = [put(x, 1) for x in late]
        patch_sum = ext_sum[: 16 * my_chans].reshape(my_chans, 16, block)
        bias_sum = ext_sum[16 * my_chans :]
    return (
        prediction,
        field_grad,
        patch_sum,
        bias_sum,
        query_sum,
        value_sum,
        agg_out_sum,
        lead_sum,
        one_sum[0],
        qkv_sum,
        out_sum,
        two_sum[0],
        up_sum,
        down_sum,
        head_sum,
    )


def solution(mesh):
    placed = (
        P(None, None, None, "sector"),
        P(),
        P(),
        P(),
        P(),
        P(),
        P(),
        P(),
        P(),
        P(),
        P(None, None, "mp"),
        P("mp", None),
        P(),
        P(None, "mp"),
        P("mp", None),
        P(),
        P(None, None, None, "sector"),
    )
    return jax.shard_map(
        shards,
        mesh=mesh,
        in_specs=placed,
        out_specs=(
            P(None, None, None, "sector"),
            P(None, "mp", None, "sector"),
            P("mp", None, "sector"),
            P("mp", "sector"),
            P("mp", "sector"),
            P("mp", "sector"),
            P("mp", "sector"),
            P(None, "sector"),
            P("sector"),
            P("sector", None, "mp"),
            P("mp", "sector"),
            P("sector"),
            P("sector", "mp"),
            P("mp", "sector"),
            P("sector", "mp"),
        ),
        check_vma=False,
    )
```
